128 devices in a mesh: region: 16 (over y, x_hi, core), ctx: 8 (over z, x_lo).
Axes of the slice: x: 4 (x_hi: 2, x_lo: 2; x = x_hi * 2 + x_lo), y: 4, z: 4, core: 2. Of those that a mesh axis runs over, the one named last changes fastest.
Arguments:
- tokens: bfloat16 [16, 4096, 1152], P('region', 'ctx'), may hold values from -6 to 6
- element_ids: int32 [16, 4096], P('region', 'ctx'), may hold values from 0 to 16383, as said below
- element_slot: int32 [16384], replicated, may hold values from 0 to 16383, as said below
- live_count: int32 [16, 8], P('region', 'ctx'), may hold values from 128 to 512
- cond_table: bfloat16 [16384, 1152], P(('region', 'ctx')), may hold values from -6 to 6
- w_ada: bfloat16 [1152, 3456], replicated, may hold values from -0.1875 to 0.1875
- b_ada: float32 [3456], replicated, may hold values from -3 to 3
- w_qkv: bfloat16 [1152, 3456], replicated, may hold values from -8 to 8
- w_out: bfloat16 [1152, 1152], replicated, may hold values from -0.1875 to 0.1875
Outputs:
- block_out: bfloat16 [16, 4096, 1152], P('region', 'ctx')
The draws below stay inside these ranges and needn't reach their ends.
Inputs may be any that keep to these rules, and one draw needn't show every extreme that they name: element_ids: within each device's block of 512 patches (region r, positions c * 512 to (c + 1) * 512 - 1, device r * 8 + c of region+ctx), at most 6 patches name elements whose table row lies on one device (rows o * 128 to (o + 1) * 128 - 1); in every block some device is named by exactly 6 solid patches. element_slot is a permutation: element e is row element_slot[e] of cond_table.
All inputs are finite; a program needn't handle non-finite values.
Results may differ from the reference program's by a relative error of at most 0.027.
Values may be sent and summed in bfloat16 or wider, within the bound.
A program may use at most 192 MiB of HBM per device.

```python
import math
import jax
import jax.numpy as jnp
from jax import lax

D = 1152
HEADS = 16
TOK_DEV = 512
ELEM_DEV = 128
REGIONS = 16
CTX_SHARDS = 8
SEQ = 4096
OWNERS = 128
ELEMENTS = 16384
CAP = 6


def element_order(key):
    return jax.random.permutation(jax.random.fold_in(key, 17), ELEMENTS).astype(jnp.int32)


def draw_element_slot(key, part):
    return element_order(key)


def draw_element_ids(key, part):
    slot_of = element_order(key)
    element_at = jnp.argsort(slot_of, stable=True).astype(jnp.int32)
    ticket_count = CAP * OWNERS
    device_keys = jax.random.split(jax.random.fold_in(key, 23), OWNERS)

    def one_device(device_key):
        first_key, second_key = jax.random.split(device_key)
        tickets = jax.random.permutation(first_key, ticket_count).astype(jnp.int32)
        owner_of = tickets // CAP
        forced = owner_of[0]
        ranking = jnp.arange(ticket_count, dtype=jnp.int32) - ticket_count * (owner_of == forced).astype(jnp.int32)
        ordering = jnp.argsort(ranking, stable=True)
        chosen = owner_of[ordering[:TOK_DEV]]
        table_rows = jax.random.randint(second_key, (TOK_DEV,), 0, ELEM_DEV, dtype=jnp.int32)
        return element_at[chosen * ELEM_DEV + table_rows]
    return jax.vmap(one_device)(device_keys).reshape(REGIONS, SEQ)


def draw_w_qkv(key, part):
    base = jax.random.normal(key, (D, 3 * D), jnp.float32) * D ** (-0.5)
    return base.astype(jnp.bfloat16)


def place_ends(entries, own_key, smallest, top_value):
    longest = entries.shape.index(max(entries.shape))
    spots = []
    for shift in (0, 1):
        where = [jax.random.randint(jax.random.fold_in(own_key, axis), (), 0, length) for axis, length in enumerate(entries.shape)]
        where[longest] = (where[longest] + shift) % entries.shape[longest]
        spots.append(tuple(where))
    return entries.at[spots[0]].set(smallest).at[spots[1]].set(top_value)


def block_levels(rng, dims, cuts, least, top_value):
    def one(dim, parts):
        steps = jax.random.uniform(jax.random.fold_in(jax.random.fold_in(rng, 6), dim), (parts,), jnp.float32, least / len(cuts), top_value / len(cuts))
        return jnp.repeat(jnp.exp(steps), dims[dim] // parts).reshape((-1,) + (1,) * (len(dims) - dim - 1))

    gain = one(*cuts[0])
    for cut in cuts[1:]:
        gain = gain * one(*cut)
    return gain


def centred(key, shape, scale, reach, shards=(), held_as=jnp.bfloat16):
    entries = jax.random.normal(key, shape, jnp.float32) * scale
    if len(shards) > 0:
        entries = block_levels(key, shape, shards, -0.22, 0.18) * entries
    return jnp.clip(entries, min=-reach, max=reach).astype(held_as)


def setup_inputs(seed: int = 0) -> dict:
    seeds = jax.random.split(jax.random.key(seed), 10)
    tokens = centred(seeds[0], (REGIONS, SEQ, D), 1.0, 6.0, ((0, 16), (1, 8)))
    element_ids = draw_element_ids(jax.random.fold_in(seeds[9], 71), 0)
    element_slot = draw_element_slot(jax.random.fold_in(seeds[9], 71), 0)
    live_count = place_ends(jax.random.randint(seeds[3], (REGIONS, CTX_SHARDS), TOK_DEV // 4, TOK_DEV + 1), jax.random.fold_in(seeds[3], 1), TOK_DEV // 4, TOK_DEV).astype(jnp.int32)
    cond_table = centred(seeds[4], (ELEMENTS, D), 1.0, 6.0, ((0, 128),))
    w_ada = centred(seeds[5], (D, 3 * D), D ** -0.5, 0.1875)
    b_ada = centred(seeds[6], (3 * D,), 0.5, 3.0, (), jnp.float32)
    w_qkv = draw_w_qkv(jax.random.fold_in(seeds[9], 71), 0)
    w_out = centred(seeds[8], (D, D), D ** -0.5, 0.1875)
    return {"tokens": tokens, "element_ids": element_ids, "element_slot": element_slot, "live_count": live_count, "cond_table": cond_table, "w_ada": w_ada, "b_ada": b_ada, "w_qkv": w_qkv, "w_out": w_out}


def layer_modulate(region_tokens, mods, width):
    values = region_tokens.astype(jnp.float32)
    center = lax.optimization_barrier(jnp.mean(values, axis=1, keepdims=True))
    spread = lax.optimization_barrier(jnp.mean((values - center) ** 2, axis=1, keepdims=True))
    normed = (values - center) * lax.rsqrt(spread + 1e-06)
    shift = mods[:, :width]
    scale = mods[:, width:2 * width]
    return (normed * (1.0 + scale) + shift).astype(jnp.bfloat16)

def reference(tokens, element_ids, element_slot, live_count, cond_table, w_ada, b_ada, w_qkv, w_out):
    width = D
    head_dim = D // HEADS
    inverse_root = 1.0 / math.sqrt(head_dim)
    activated = jax.nn.silu(cond_table.astype(jnp.float32)).astype(jnp.bfloat16)
    table_mods = (jnp.dot(activated, w_ada, preferred_element_type=jnp.float32) + b_ada).astype(jnp.bfloat16)
    bias_row = b_ada.astype(jnp.bfloat16)
    query_block = math.gcd(SEQ, 512)

    def region_block(inputs):
        region_tokens, region_ids, region_live = inputs
        slots = element_slot[region_ids]
        position = jnp.arange(SEQ, dtype=jnp.int32)
        solid = position % TOK_DEV < jnp.repeat(region_live, TOK_DEV)
        mods = jnp.where(solid[:, None], table_mods[slots], bias_row[None, :]).astype(jnp.float32)
        modulated = layer_modulate(region_tokens, mods, width)
        qkv = jnp.dot(modulated, w_qkv, preferred_element_type=jnp.float32).astype(jnp.bfloat16)
        queries = qkv[:, :width].reshape(SEQ, HEADS, head_dim)
        keys_all = qkv[:, width:2 * width].reshape(SEQ, HEADS, head_dim).astype(jnp.float32)
        values_all = qkv[:, 2 * width:].reshape(SEQ, HEADS, head_dim).astype(jnp.float32)

        def attend_rows(query_rows):
            scores = jnp.einsum('qhe,khe->hqk', query_rows.astype(jnp.float32), keys_all) * inverse_root
            peak = lax.optimization_barrier(jnp.max(scores, axis=2, keepdims=True))
            expo = jnp.exp(scores - peak)
            denominator = lax.optimization_barrier(jnp.sum(expo, axis=2))
            weights = expo.astype(jnp.bfloat16).astype(jnp.float32)
            summed = jnp.einsum('hqk,khe->hqe', weights, values_all)
            result = summed / denominator[:, :, None]
            return jnp.transpose(result, (1, 0, 2)).reshape(query_rows.shape[0], width).astype(jnp.bfloat16)
        attended = lax.map(attend_rows, queries.reshape(SEQ // query_block, query_block, HEADS, head_dim))
        attended = attended.reshape(SEQ, width)
        projected = jnp.dot(attended, w_out, preferred_element_type=jnp.float32)
        gate = mods[:, 2 * width:]
        return (region_tokens.astype(jnp.float32) + gate * projected).astype(jnp.bfloat16)
    return lax.map(region_block, (tokens, element_ids, live_count))
```

```python
import functools
import math

import jax
import jax.numpy as jnp
from jax import lax
from jax.experimental import pallas as pl
from jax.experimental.pallas import tpu as pltpu
from jax.sharding import PartitionSpec as P

HEADS = 16


def layer_modulate(device_tokens, mods, width):
    values = device_tokens.astype(jnp.float32)
    center = jnp.mean(values, axis=1, keepdims=True)
    spread = jnp.mean((values - center) ** 2, axis=1, keepdims=True)
    normed = (values - center) * lax.rsqrt(spread + 1e-06)
    shift = mods[:, :width]
    scale = mods[:, width : 2 * width]
    return (normed * (1.0 + scale) + shift).astype(jnp.bfloat16)


def attend_kernel(qt_ref, k_ref, vt_ref, o_ref, s_scr, *, inv_root, chunks):
    qt = qt_ref[0, 0]
    q_rows = qt.shape[1]

    def score(c, m):
        s = jnp.dot(k_ref[c, 0], qt, preferred_element_type=jnp.float32) * inv_root
        s_scr[c] = s
        return jnp.maximum(m, jnp.max(s, axis=0, keepdims=True))

    m = lax.fori_loop(0, chunks, score, jnp.full((1, q_rows), -jnp.inf, jnp.float32))

    def accumulate(c, carry):
        total, acc = carry
        expo = jnp.exp(s_scr[c] - m)
        total = total + jnp.sum(expo, axis=0, keepdims=True)
        acc = acc + jnp.dot(
            vt_ref[c, 0], expo.astype(jnp.bfloat16), preferred_element_type=jnp.float32
        )
        return total, acc

    head_dim = qt.shape[0]
    total, acc = lax.fori_loop(
        0,
        chunks,
        accumulate,
        (
            jnp.zeros((1, q_rows), jnp.float32),
            jnp.zeros((head_dim, q_rows), jnp.float32),
        ),
    )
    o_ref[0, 0] = (acc / total).astype(o_ref.dtype)


def attend(q_t, k_tok, v_t, inv_root):
    blocks, pair, head_dim, rows = q_t.shape
    kernel = functools.partial(attend_kernel, inv_root=inv_root, chunks=blocks)
    return pl.pallas_call(
        kernel,
        out_shape=jax.ShapeDtypeStruct(q_t.shape, jnp.bfloat16),
        grid=(pair, blocks),
        in_specs=[
            pl.BlockSpec((1, 1, head_dim, rows), lambda h, b: (b, h, 0, 0)),
            pl.BlockSpec((blocks, 1, rows, head_dim), lambda h, b: (0, h, 0, 0)),
            pl.BlockSpec((blocks, 1, head_dim, rows), lambda h, b: (0, h, 0, 0)),
        ],
        out_specs=pl.BlockSpec((1, 1, head_dim, rows), lambda h, b: (b, h, 0, 0)),
        scratch_shapes=[pltpu.VMEM((blocks, rows, rows), jnp.float32)],
        compiler_params=pltpu.CompilerParams(vmem_limit_bytes=48 * 1024 * 1024),
    )(q_t, k_tok, v_t)


def per_device(
    tokens, element_ids, element_slot, live_count, cond_table, w_ada, b_ada, w_qkv, w_out
):
    device_tokens = tokens[0]
    tok_rows, width = device_tokens.shape
    owners = lax.axis_size(("region", "ctx"))
    shards = lax.axis_size("ctx")
    elem_rows = cond_table.shape[0]
    capacity = max(2, 3 * tok_rows // (2 * owners))
    slots = element_slot[element_ids[0]]
    owner_index = slots // elem_rows
    local_row = slots % elem_rows
    position = jnp.arange(tok_rows, dtype=jnp.int32)
    solid = position < live_count[0, 0]
    earlier = (
        (owner_index[:, None] == owner_index[None, :])
        & (position[None, :] < position[:, None])
        & solid[None, :]
    )
    place_rank = jnp.sum(earlier.astype(jnp.int32), axis=1)
    target = jnp.where(solid, owner_index * capacity + place_rank, owners * capacity)
    requests = jnp.zeros((owners * capacity,), jnp.int32).at[target].set(local_row, mode="drop")
    asked = lax.all_to_all(
        requests.reshape(owners, capacity),
        ("region", "ctx"),
        split_axis=0,
        concat_axis=0,
        tiled=True,
    ).reshape(-1)
    pick_at = jnp.minimum(target, owners * capacity - 1)
    served = cond_table[asked].reshape(owners, capacity, width)
    replies = lax.all_to_all(served, ("region", "ctx"), split_axis=0, concat_axis=0, tiled=True)
    picked = replies.reshape(owners * capacity, width)[pick_at]
    activated = jnp.where(solid[:, None], jax.nn.silu(picked.astype(jnp.float32)), 0.0).astype(
        jnp.bfloat16
    )
    mods = (jnp.dot(activated, w_ada, preferred_element_type=jnp.float32) + b_ada).astype(
        jnp.bfloat16
    )
    mods = mods.astype(jnp.float32)
    modulated = layer_modulate(device_tokens, mods, width)

    head_dim = width // HEADS
    pair = HEADS // shards
    inverse_root = 1.0 / math.sqrt(head_dim)
    w_parts = w_qkv.reshape(width, 3, shards, pair, head_dim)
    q_send = jnp.einsum(
        "td,dphe->phet", modulated, w_parts[:, 0], preferred_element_type=jnp.float32
    ).astype(jnp.bfloat16)
    k_send = jnp.einsum(
        "td,dphe->phte", modulated, w_parts[:, 1], preferred_element_type=jnp.float32
    ).astype(jnp.bfloat16)
    v_send = jnp.einsum(
        "td,dphe->phet", modulated, w_parts[:, 2], preferred_element_type=jnp.float32
    ).astype(jnp.bfloat16)
    q_got = lax.all_to_all(q_send, "ctx", split_axis=0, concat_axis=0, tiled=True)
    k_got = lax.all_to_all(k_send, "ctx", split_axis=0, concat_axis=0, tiled=True)
    v_got = lax.all_to_all(v_send, "ctx", split_axis=0, concat_axis=0, tiled=True)
    out_t = attend(q_got, k_got, v_got, inverse_root)
    back = lax.all_to_all(out_t, "ctx", split_axis=0, concat_axis=0, tiled=True)
    projected = jnp.einsum(
        "phet,pheD->tD",
        back,
        w_out.reshape(shards, pair, head_dim, width),
        preferred_element_type=jnp.float32,
    )
    gate = mods[:, 2 * width :]
    output = (device_tokens.astype(jnp.float32) + gate * projected).astype(jnp.bfloat16)
    return output[None]


def solution(mesh):
    placed = (
        P("region", "ctx", None),
        P("region", "ctx"),
        P(),
        P("region", "ctx"),
        P(("region", "ctx"), None),
        P(),
        P(),
        P(),
        P(),
    )
    return jax.shard_map(
        per_device, mesh=mesh, in_specs=placed, out_specs=P("region", "ctx", None), check_vma=False
    )
```

```python
import functools
import math

import jax
import jax.numpy as jnp
from jax import lax
from jax.experimental import pallas as pl
from jax.experimental.pallas import tpu as pltpu
from jax.sharding import PartitionSpec as P

HEADS = 16


def layer_modulate(device_tokens, mods, width):
    values = device_tokens.astype(jnp.float32)
    center = jnp.mean(values, axis=1, keepdims=True)
    spread = jnp.mean((values - center) ** 2, axis=1, keepdims=True)
    normed = (values - center) * lax.rsqrt(spread + 1e-06)
    shift = mods[:, :width]
    scale = mods[:, width : 2 * width]
    return (normed * (1.0 + scale) + shift).astype(jnp.bfloat16)


def attend_kernel(qt_ref, k_ref, vt_ref, o_ref, s_scr, *, inv_root, chunks):
    qt = qt_ref[0, 0]
    q_rows = qt.shape[1]

    def score(c, m):
        s = jnp.dot(k_ref[c, 0], qt, preferred_element_type=jnp.float32) * inv_root
        s_scr[c] = s
        return jnp.maximum(m, jnp.max(s, axis=0, keepdims=True))

    m = lax.fori_loop(0, chunks, score, jnp.full((1, q_rows), -jnp.inf, jnp.float32))

    def accumulate(c, carry):
        total, acc = carry
        expo = jnp.exp(s_scr[c] - m)
        total = total + jnp.sum(expo, axis=0, keepdims=True)
        acc = acc + jnp.dot(
            vt_ref[c, 0], expo.astype(jnp.bfloat16), preferred_element_type=jnp.float32
        )
        return total, acc

    head_dim = qt.shape[0]
    total, acc = lax.fori_loop(
        0,
        chunks,
        accumulate,
        (
            jnp.zeros((1, q_rows), jnp.float32),
            jnp.zeros((head_dim, q_rows), jnp.float32),
        ),
    )
    o_ref[0, 0] = (acc / total).astype(o_ref.dtype)


def attend(q_t, k_tok, v_t, inv_root):
    blocks, pair, head_dim, rows = q_t.shape
    kernel = functools.partial(attend_kernel, inv_root=inv_root, chunks=blocks)
    return pl.pallas_call(
        kernel,
        out_shape=jax.ShapeDtypeStruct(q_t.shape, jnp.bfloat16),
        grid=(pair, blocks),
        in_specs=[
            pl.BlockSpec((1, 1, head_dim, rows), lambda h, b: (b, h, 0, 0)),
            pl.BlockSpec((blocks, 1, rows, head_dim), lambda h, b: (0, h, 0, 0)),
            pl.BlockSpec((blocks, 1, head_dim, rows), lambda h, b: (0, h, 0, 0)),
        ],
        out_specs=pl.BlockSpec((1, 1, head_dim, rows), lambda h, b: (b, h, 0, 0)),
        scratch_shapes=[pltpu.VMEM((blocks, rows, rows), jnp.float32)],
        compiler_params=pltpu.CompilerParams(vmem_limit_bytes=48 * 1024 * 1024),
    )(q_t, k_tok, v_t)


def exchange_kernel(*refs, count, shards):
    sends = refs[:count]
    gots = refs[count : 2 * count]
    send_sem, recv_sem, local_sem = refs[2 * count :]
    me = lax.axis_index("ctx")
    region = lax.axis_index("region")
    mesh_id = pl.DeviceIdType.MESH
    barrier = pltpu.get_barrier_semaphore()
    for d in range(1, shards):
        peer = lax.rem(me + d, shards)
        pl.semaphore_signal(barrier, 1, device_id=(region, peer), device_id_type=mesh_id)
    pl.semaphore_wait(barrier, shards - 1)
    copies = []
    for a in range(count):
        local = pltpu.make_async_copy(sends[a].at[me], gots[a].at[me], local_sem.at[a])
        local.start()
        copies.append(local)
    for d in range(1, shards):
        peer = lax.rem(me + d, shards)
        for a in range(count):
            remote = pltpu.make_async_remote_copy(
                src_ref=sends[a].at[peer],
                dst_ref=gots[a].at[me],
                send_sem=send_sem.at[a, d - 1],
                recv_sem=recv_sem.at[a, d - 1],
                device_id=(region, peer),
                device_id_type=mesh_id,
            )
            remote.start()
            copies.append(remote)
    for copy in copies:
        copy.wait()


def exchange(arrays, shards, collective_id):
    count = len(arrays)
    kernel = functools.partial(exchange_kernel, count=count, shards=shards)
    any_spec = pl.BlockSpec(memory_space=pl.ANY)
    return pl.pallas_call(
        kernel,
        out_shape=[jax.ShapeDtypeStruct(x.shape, x.dtype) for x in arrays],
        in_specs=[any_spec] * count,
        out_specs=[any_spec] * count,
        scratch_shapes=[
            pltpu.SemaphoreType.DMA((count, shards - 1)),
            pltpu.SemaphoreType.DMA((count, shards - 1)),
            pltpu.SemaphoreType.DMA((count,)),
        ],
        compiler_params=pltpu.CompilerParams(
            collective_id=collective_id, has_side_effects=True
        ),
    )(*arrays)


def per_device(
    tokens, element_ids, element_slot, live_count, cond_table, w_ada, b_ada, w_qkv, w_out
):
    device_tokens = tokens[0]
    tok_rows, width = device_tokens.shape
    owners = lax.axis_size(("region", "ctx"))
    shards = lax.axis_size("ctx")
    elem_rows = cond_table.shape[0]
    capacity = max(2, 3 * tok_rows // (2 * owners))
    slots = element_slot[element_ids[0]]
    owner_index = slots // elem_rows
    local_row = slots % elem_rows
    position = jnp.arange(tok_rows, dtype=jnp.int32)
    solid = position < live_count[0, 0]
    earlier = (
        (owner_index[:, None] == owner_index[None, :])
        & (position[None, :] < position[:, None])
        & solid[None, :]
    )
    place_rank = jnp.sum(earlier.astype(jnp.int32), axis=1)
    target = jnp.where(solid, owner_index * capacity + place_rank, owners * capacity)
    requests = jnp.zeros((owners * capacity,), jnp.int32).at[target].set(local_row, mode="drop")
    asked = lax.all_to_all(
        requests.reshape(owners, capacity),
        ("region", "ctx"),
        split_axis=0,
        concat_axis=0,
        tiled=True,
    ).reshape(-1)
    pick_at = jnp.minimum(target, owners * capacity - 1)
    served = cond_table[asked].reshape(owners, capacity, width)
    replies = lax.all_to_all(served, ("region", "ctx"), split_axis=0, concat_axis=0, tiled=True)
    picked = replies.reshape(owners * capacity, width)[pick_at]
    activated = jnp.where(solid[:, None], jax.nn.silu(picked.astype(jnp.float32)), 0.0).astype(
        jnp.bfloat16
    )
    mods = (jnp.dot(activated, w_ada, preferred_element_type=jnp.float32) + b_ada).astype(
        jnp.bfloat16
    )
    mods = mods.astype(jnp.float32)
    modulated = layer_modulate(device_tokens, mods, width)

    head_dim = width // HEADS
    pair = HEADS // shards
    inverse_root = 1.0 / math.sqrt(head_dim)
    w_parts = w_qkv.reshape(width, 3, shards, pair, head_dim)
    q_send = jnp.einsum(
        "td,dphe->phet", modulated, w_parts[:, 0], preferred_element_type=jnp.float32
    ).astype(jnp.bfloat16)
    k_send = jnp.einsum(
        "td,dphe->phte", modulated, w_parts[:, 1], preferred_element_type=jnp.float32
    ).astype(jnp.bfloat16)
    v_send = jnp.einsum(
        "td,dphe->phet", modulated, w_parts[:, 2], preferred_element_type=jnp.float32
    ).astype(jnp.bfloat16)
    q_got, k_got, v_got = exchange([q_send, k_send, v_send], shards, 0)
    out_t = attend(q_got, k_got, v_got, inverse_root)
    (back,) = exchange([out_t], shards, 1)
    projected = jnp.einsum(
        "phet,pheD->tD",
        back,
        w_out.reshape(shards, pair, head_dim, width),
        preferred_element_type=jnp.float32,
    )
    gate = mods[:, 2 * width :]
    output = (device_tokens.astype(jnp.float32) + gate * projected).astype(jnp.bfloat16)
    return output[None]


def solution(mesh):
    placed = (
        P("region", "ctx", None),
        P("region", "ctx"),
        P(),
        P("region", "ctx"),
        P(("region", "ctx"), None),
        P(),
        P(),
        P(),
        P(),
    )
    return jax.shard_map(
        per_device, mesh=mesh, in_specs=placed, out_specs=P("region", "ctx", None), check_vma=False
    )
```

```python
import functools
import math

import jax
import jax.numpy as jnp
from jax import lax
from jax.experimental import pallas as pl
from jax.experimental.pallas import tpu as pltpu
from jax.sharding import PartitionSpec as P

HEADS = 16


def layer_modulate(device_tokens, mods, width):
    values = device_tokens.astype(jnp.float32)
    center = jnp.mean(values, axis=1, keepdims=True)
    spread = jnp.mean((values - center) ** 2, axis=1, keepdims=True)
    normed = (values - center) * lax.rsqrt(spread + 1e-06)
    shift = mods[:, :width]
    scale = mods[:, width : 2 * width]
    return (normed * (1.0 + scale) + shift).astype(jnp.bfloat16)


def start_sends(sends, gots, send_sem, recv_sem, local_sem, shards):
    me = lax.axis_index("ctx")
    region = lax.axis_index("region")
    mesh_id = pl.DeviceIdType.MESH
    barrier = pltpu.get_barrier_semaphore()
    for d in range(1, shards):
        peer = lax.rem(me + d, shards)
        pl.semaphore_signal(barrier, 1, device_id=(region, peer), device_id_type=mesh_id)
    pl.semaphore_wait(barrier, shards - 1)
    copies = []
    for a in range(len(sends)):
        local = pltpu.make_async_copy(sends[a].at[me], gots[a].at[me], local_sem.at[a])
        local.start()
        copies.append(local)
    for d in range(1, shards):
        peer = lax.rem(me + d, shards)
        for a in range(len(sends)):
            remote = pltpu.make_async_remote_copy(
                src_ref=sends[a].at[peer],
                dst_ref=gots[a].at[me],
                send_sem=send_sem.at[a, d - 1],
                recv_sem=recv_sem.at[a, d - 1],
                device_id=(region, peer),
                device_id_type=mesh_id,
            )
            remote.start()
            copies.append(remote)
    return copies


def exchange_kernel(*refs, count, shards):
    sends = refs[:count]
    gots = refs[count : 2 * count]
    copies = start_sends(sends, gots, *refs[2 * count :], shards)
    for copy in copies:
        copy.wait()


def send_scratch(count, shards):
    return [
        pltpu.SemaphoreType.DMA((count, shards - 1)),
        pltpu.SemaphoreType.DMA((count, shards - 1)),
        pltpu.SemaphoreType.DMA((count,)),
    ]


def exchange(arrays, shards, collective_id):
    count = len(arrays)
    kernel = functools.partial(exchange_kernel, count=count, shards=shards)
    any_spec = pl.BlockSpec(memory_space=pl.ANY)
    return pl.pallas_call(
        kernel,
        out_shape=[jax.ShapeDtypeStruct(x.shape, x.dtype) for x in arrays],
        in_specs=[any_spec] * count,
        out_specs=[any_spec] * count,
        scratch_shapes=send_scratch(count, shards),
        compiler_params=pltpu.CompilerParams(
            collective_id=collective_id, has_side_effects=True
        ),
    )(*arrays)


def attend_body(qt_ref, k_ref, vt_ref, o_ref, s_scr, inv_root):
    blocks, head_dim, q_rows = qt_ref.shape

    def one_block(b, carry):
        qt = qt_ref[b]

        def score(c, m):
            s = jnp.dot(k_ref[c], qt, preferred_element_type=jnp.float32) * inv_root
            s_scr[c] = s
            return jnp.maximum(m, jnp.max(s, axis=0, keepdims=True))

        m = lax.fori_loop(0, blocks, score, jnp.full((1, q_rows), -jnp.inf, jnp.float32))

        def accumulate(c, inner):
            total, acc = inner
            expo = jnp.exp(s_scr[c] - m)
            total = total + jnp.sum(expo, axis=0, keepdims=True)
            acc = acc + jnp.dot(
                vt_ref[c], expo.astype(jnp.bfloat16), preferred_element_type=jnp.float32
            )
            return total, acc

        total, acc = lax.fori_loop(
            0,
            blocks,
            accumulate,
            (
                jnp.zeros((1, q_rows), jnp.float32),
                jnp.zeros((head_dim, q_rows), jnp.float32),
            ),
        )
        o_ref[b] = (acc / total).astype(o_ref.dtype)
        return carry

    lax.fori_loop(0, blocks, one_block, 0)


def attend_send_kernel(*refs, count, shards, inv_root):
    qt_ref, k_ref, vt_ref = refs[:3]
    sends = refs[3 : 3 + count]
    o_ref = refs[3 + count]
    gots = refs[4 + count : 4 + 2 * count]
    s_scr = refs[4 + 2 * count]
    copies = start_sends(sends, gots, *refs[5 + 2 * count :], shards)
    attend_body(qt_ref, k_ref, vt_ref, o_ref, s_scr, inv_root)
    for copy in copies:
        copy.wait()


def attend_send(q_t, k_tok, v_t, sends, shards, inv_root, collective_id):
    blocks, head_dim, rows = q_t.shape
    count = len(sends)
    kernel = functools.partial(
        attend_send_kernel, count=count, shards=shards, inv_root=inv_root
    )
    any_spec = pl.BlockSpec(memory_space=pl.ANY)
    vmem_spec = pl.BlockSpec(memory_space=pltpu.VMEM)
    outs = pl.pallas_call(
        kernel,
        out_shape=[jax.ShapeDtypeStruct(q_t.shape, jnp.bfloat16)]
        + [jax.ShapeDtypeStruct(x.shape, x.dtype) for x in sends],
        in_specs=[vmem_spec] * 3 + [any_spec] * count,
        out_specs=[vmem_spec] + [any_spec] * count,
        scratch_shapes=[pltpu.VMEM((blocks, rows, rows), jnp.float32)]
        + send_scratch(count, shards),
        compiler_params=pltpu.CompilerParams(
            collective_id=collective_id,
            has_side_effects=True,
            vmem_limit_bytes=48 * 1024 * 1024,
        ),
    )(q_t, k_tok, v_t, *sends)
    return outs[0], outs[1:]


def head_pipeline(q_all, k_all, v_all, shards, inverse_root):
    pair = q_all.shape[0]
    got = exchange([q_all[0], k_all[0], v_all[0]], shards, 0)
    backs = []
    for h in range(pair):
        if h + 1 < pair:
            sends = [q_all[h + 1], k_all[h + 1], v_all[h + 1]]
        else:
            sends = []
        if h > 0:
            sends = sends + [out_prev]
        out_prev, sent = attend_send(*got, sends, shards, inverse_root, 1 + h)
        if h + 1 < pair:
            got = sent[:3]
            sent = sent[3:]
        backs.extend(sent)
    (last_back,) = exchange([out_prev], shards, 1 + pair)
    backs.append(last_back)
    return jnp.stack(backs, axis=1)


def per_device(
    tokens, element_ids, element_slot, live_count, cond_table, w_ada, b_ada, w_qkv, w_out
):
    device_tokens = tokens[0]
    tok_rows, width = device_tokens.shape
    owners = lax.axis_size(("region", "ctx"))
    shards = lax.axis_size("ctx")
    elem_rows = cond_table.shape[0]
    capacity = max(2, 3 * tok_rows // (2 * owners))
    slots = element_slot[element_ids[0]]
    owner_index = slots // elem_rows
    local_row = slots % elem_rows
    position = jnp.arange(tok_rows, dtype=jnp.int32)
    solid = position < live_count[0, 0]
    earlier = (
        (owner_index[:, None] == owner_index[None, :])
        & (position[None, :] < position[:, None])
        & solid[None, :]
    )
    place_rank = jnp.sum(earlier.astype(jnp.int32), axis=1)
    target = jnp.where(solid, owner_index * capacity + place_rank, owners * capacity)
    requests = jnp.zeros((owners * capacity,), jnp.int32).at[target].set(local_row, mode="drop")
    asked = lax.all_to_all(
        requests.reshape(owners, capacity),
        ("region", "ctx"),
        split_axis=0,
        concat_axis=0,
        tiled=True,
    ).reshape(-1)
    pick_at = jnp.minimum(target, owners * capacity - 1)
    served = cond_table[asked].reshape(owners, capacity, width)
    replies = lax.all_to_all(served, ("region", "ctx"), split_axis=0, concat_axis=0, tiled=True)
    picked = replies.reshape(owners * capacity, width)[pick_at]
    activated = jnp.where(solid[:, None], jax.nn.silu(picked.astype(jnp.float32)), 0.0).astype(
        jnp.bfloat16
    )
    mods = (jnp.dot(activated, w_ada, preferred_element_type=jnp.float32) + b_ada).astype(
        jnp.bfloat16
    )
    mods = mods.astype(jnp.float32)
    modulated = layer_modulate(device_tokens, mods, width)

    head_dim = width // HEADS
    pair = HEADS // shards
    inverse_root = 1.0 / math.sqrt(head_dim)
    w_parts = w_qkv.reshape(width, 3, shards, pair, head_dim)
    q_all = jnp.einsum(
        "td,dphe->hpet", modulated, w_parts[:, 0], preferred_element_type=jnp.float32
    ).astype(jnp.bfloat16)
    k_all = jnp.einsum(
        "td,dphe->hpte", modulated, w_parts[:, 1], preferred_element_type=jnp.float32
    ).astype(jnp.bfloat16)
    v_all = jnp.einsum(
        "td,dphe->hpet", modulated, w_parts[:, 2], preferred_element_type=jnp.float32
    ).astype(jnp.bfloat16)
    backs = head_pipeline(q_all, k_all, v_all, shards, inverse_root)
    w_out_parts = w_out.reshape(shards, pair, head_dim, width)
    projected = jnp.einsum(
        "phet,pheD->tD",
        backs,
        w_out_parts,
        preferred_element_type=jnp.float32,
    )
    gate = mods[:, 2 * width :]
    output = (device_tokens.astype(jnp.float32) + gate * projected).astype(jnp.bfloat16)
    return output[None]


def solution(mesh):
    placed = (
        P("region", "ctx", None),
        P("region", "ctx"),
        P(),
        P("region", "ctx"),
        P(("region", "ctx"), None),
        P(),
        P(),
        P(),
        P(),
    )
    return jax.shard_map(
        per_device, mesh=mesh, in_specs=placed, out_specs=P("region", "ctx", None), check_vma=False
    )
```

```python
import functools
import math

import jax
import jax.numpy as jnp
from jax import lax
from jax.experimental import pallas as pl
from jax.experimental.pallas import tpu as pltpu
from jax.sharding import PartitionSpec as P

HEADS = 16


def layer_modulate(device_tokens, mods, width):
    values = device_tokens.astype(jnp.float32)
    center = jnp.mean(values, axis=1, keepdims=True)
    spread = jnp.mean((values - center) ** 2, axis=1, keepdims=True)
    normed = (values - center) * lax.rsqrt(spread + 1e-06)
    shift = mods[:, :width]
    scale = mods[:, width : 2 * width]
    return (normed * (1.0 + scale) + shift).astype(jnp.bfloat16)


def start_sends(sends, gots, send_sem, recv_sem, local_sem, shards):
    me = lax.axis_index("ctx")
    region = lax.axis_index("region")
    mesh_id = pl.DeviceIdType.MESH
    barrier = pltpu.get_barrier_semaphore()
    for d in range(1, shards):
        peer = lax.rem(me + d, shards)
        pl.semaphore_signal(barrier, 1, device_id=(region, peer), device_id_type=mesh_id)
    pl.semaphore_wait(barrier, shards - 1)
    copies = []
    for a in range(len(sends)):
        local = pltpu.make_async_copy(sends[a].at[me], gots[a].at[me], local_sem.at[a])
        local.start()
        copies.append(local)
    for d in range(1, shards):
        peer = lax.rem(me + d, shards)
        for a in range(len(sends)):
            remote = pltpu.make_async_remote_copy(
                src_ref=sends[a].at[peer],
                dst_ref=gots[a].at[me],
                send_sem=send_sem.at[a, d - 1],
                recv_sem=recv_sem.at[a, d - 1],
                device_id=(region, peer),
                device_id_type=mesh_id,
            )
            remote.start()
            copies.append(remote)
    return copies


def exchange_kernel(*refs, count, shards):
    sends = refs[:count]
    gots = refs[count : 2 * count]
    copies = start_sends(sends, gots, *refs[2 * count :], shards)
    for copy in copies:
        copy.wait()


def send_scratch(count, shards):
    return [
        pltpu.SemaphoreType.DMA((count, shards - 1)),
        pltpu.SemaphoreType.DMA((count, shards - 1)),
        pltpu.SemaphoreType.DMA((count,)),
    ]


def exchange(arrays, shards, collective_id):
    count = len(arrays)
    kernel = functools.partial(exchange_kernel, count=count, shards=shards)
    any_spec = pl.BlockSpec(memory_space=pl.ANY)
    return pl.pallas_call(
        kernel,
        out_shape=[jax.ShapeDtypeStruct(x.shape, x.dtype) for x in arrays],
        in_specs=[any_spec] * count,
        out_specs=[any_spec] * count,
        scratch_shapes=send_scratch(count, shards),
        compiler_params=pltpu.CompilerParams(
            collective_id=collective_id, has_side_effects=True
        ),
    )(*arrays)


def attend_body(qt_ref, k_ref, vt_ref, o_ref, s_scr, inv_root):
    blocks, head_dim, q_rows = qt_ref.shape

    def one_block(b, carry):
        qt = qt_ref[b]

        def score(c, m):
            s = jnp.dot(k_ref[c], qt, preferred_element_type=jnp.float32) * inv_root
            s_scr[c] = s
            return jnp.maximum(m, jnp.max(s, axis=0, keepdims=True))

        m = lax.fori_loop(
            0, blocks, score, jnp.full((1, q_rows), -jnp.inf, jnp.float32), unroll=2
        )

        def accumulate(c, inner):
            total, acc = inner
            expo = jnp.exp(s_scr[c] - m)
            total = total + jnp.sum(expo, axis=0, keepdims=True)
            acc = acc + jnp.dot(
                vt_ref[c], expo.astype(jnp.bfloat16), preferred_element_type=jnp.float32
            )
            return total, acc

        total, acc = lax.fori_loop(
            0,
            blocks,
            accumulate,
            (
                jnp.zeros((1, q_rows), jnp.float32),
                jnp.zeros((head_dim, q_rows), jnp.float32),
            ),
            unroll=2,
        )
        o_ref[b] = (acc / total).astype(o_ref.dtype)
        return carry

    lax.fori_loop(0, blocks, one_block, 0)


def attend_send_kernel(*refs, count, shards, inv_root):
    qt_ref, k_ref, vt_ref = refs[:3]
    sends = refs[3 : 3 + count]
    o_ref = refs[3 + count]
    gots = refs[4 + count : 4 + 2 * count]
    s_scr = refs[4 + 2 * count]
    copies = start_sends(sends, gots, *refs[5 + 2 * count :], shards)
    attend_body(qt_ref, k_ref, vt_ref, o_ref, s_scr, inv_root)
    for copy in copies:
        copy.wait()


def attend_send(q_t, k_tok, v_t, sends, shards, inv_root, collective_id):
    blocks, head_dim, rows = q_t.shape
    count = len(sends)
    kernel = functools.partial(
        attend_send_kernel, count=count, shards=shards, inv_root=inv_root
    )
    any_spec = pl.BlockSpec(memory_space=pl.ANY)
    vmem_spec = pl.BlockSpec(memory_space=pltpu.VMEM)
    outs = pl.pallas_call(
        kernel,
        out_shape=[jax.ShapeDtypeStruct(q_t.shape, jnp.bfloat16)]
        + [jax.ShapeDtypeStruct(x.shape, x.dtype) for x in sends],
        in_specs=[vmem_spec] * 3 + [any_spec] * count,
        out_specs=[vmem_spec] + [any_spec] * count,
        scratch_shapes=[pltpu.VMEM((blocks, rows, rows), jnp.float32)]
        + send_scratch(count, shards),
        compiler_params=pltpu.CompilerParams(
            collective_id=collective_id,
            has_side_effects=True,
            vmem_limit_bytes=48 * 1024 * 1024,
        ),
    )(q_t, k_tok, v_t, *sends)
    return outs[0], outs[1:]


def head_pipeline(q_all, k_all, v_all, shards, inverse_root):
    pair = q_all.shape[0]
    got = exchange([q_all[0], k_all[0], v_all[0]], shards, 0)
    backs = []
    for h in range(pair):
        if h + 1 < pair:
            sends = [q_all[h + 1], k_all[h + 1], v_all[h + 1]]
        else:
            sends = []
        if h > 0:
            sends = sends + [out_prev]
        out_prev, sent = attend_send(*got, sends, shards, inverse_root, 1 + h)
        if h + 1 < pair:
            got = sent[:3]
            sent = sent[3:]
        backs.extend(sent)
    (last_back,) = exchange([out_prev], shards, 1 + pair)
    backs.append(last_back)
    return jnp.stack(backs, axis=1)


def per_device(
    tokens, element_ids, element_slot, live_count, cond_table, w_ada, b_ada, w_qkv, w_out
):
    device_tokens = tokens[0]
    tok_rows, width = device_tokens.shape
    owners = lax.axis_size(("region", "ctx"))
    shards = lax.axis_size("ctx")
    elem_rows = cond_table.shape[0]
    capacity = max(2, 3 * tok_rows // (2 * owners))
    slots = element_slot[element_ids[0]]
    owner_index = slots // elem_rows
    local_row = slots % elem_rows
    position = jnp.arange(tok_rows, dtype=jnp.int32)
    solid = position < live_count[0, 0]
    earlier = (
        (owner_index[:, None] == owner_index[None, :])
        & (position[None, :] < position[:, None])
        & solid[None, :]
    )
    place_rank = jnp.sum(earlier.astype(jnp.int32), axis=1)
    target = jnp.where(solid, owner_index * capacity + place_rank, owners * capacity)
    requests = jnp.zeros((owners * capacity,), jnp.int32).at[target].set(local_row, mode="drop")
    asked = lax.all_to_all(
        requests.reshape(owners, capacity),
        ("region", "ctx"),
        split_axis=0,
        concat_axis=0,
        tiled=True,
    ).reshape(-1)
    pick_at = jnp.minimum(target, owners * capacity - 1)
    served = cond_table[asked].reshape(owners, capacity, width)
    replies = lax.all_to_all(served, ("region", "ctx"), split_axis=0, concat_axis=0, tiled=True)
    picked = replies.reshape(owners * capacity, width)[pick_at]
    activated = jnp.where(solid[:, None], jax.nn.silu(picked.astype(jnp.float32)), 0.0).astype(
        jnp.bfloat16
    )
    mods = (jnp.dot(activated, w_ada, preferred_element_type=jnp.float32) + b_ada).astype(
        jnp.bfloat16
    )
    mods = mods.astype(jnp.float32)
    modulated = layer_modulate(device_tokens, mods, width)

    head_dim = width // HEADS
    pair = HEADS // shards
    inverse_root = 1.0 / math.sqrt(head_dim)
    w_parts = w_qkv.reshape(width, 3, shards, pair, head_dim)
    q_all = jnp.einsum(
        "td,dphe->hpet", modulated, w_parts[:, 0], preferred_element_type=jnp.float32
    ).astype(jnp.bfloat16)
    k_all = jnp.einsum(
        "td,dphe->hpte", modulated, w_parts[:, 1], preferred_element_type=jnp.float32
    ).astype(jnp.bfloat16)
    v_all = jnp.einsum(
        "td,dphe->hpet", modulated, w_parts[:, 2], preferred_element_type=jnp.float32
    ).astype(jnp.bfloat16)
    backs = head_pipeline(q_all, k_all, v_all, shards, inverse_root)
    w_out_parts = w_out.reshape(shards, pair, head_dim, width)
    projected = jnp.einsum(
        "phet,pheD->tD",
        backs,
        w_out_parts,
        preferred_element_type=jnp.float32,
    )
    gate = mods[:, 2 * width :]
    output = (device_tokens.astype(jnp.float32) + gate * projected).astype(jnp.bfloat16)
    return output[None]


def solution(mesh):
    placed = (
        P("region", "ctx", None),
        P("region", "ctx"),
        P(),
        P("region", "ctx"),
        P(("region", "ctx"), None),
        P(),
        P(),
        P(),
        P(),
    )
    return jax.shard_map(
        per_device, mesh=mesh, in_specs=placed, out_specs=P("region", "ctx", None), check_vma=False
    )
```

```python
import functools
import math

import jax
import jax.numpy as jnp
from jax import lax
from jax.experimental import pallas as pl
from jax.experimental.pallas import tpu as pltpu
from jax.sharding import PartitionSpec as P

HEADS = 16


def layer_modulate(device_tokens, mods, width):
    values = device_tokens.astype(jnp.float32)
    center = jnp.mean(values, axis=1, keepdims=True)
    spread = jnp.mean((values - center) ** 2, axis=1, keepdims=True)
    normed = (values - center) * lax.rsqrt(spread + 1e-06)
    shift = mods[:, :width]
    scale = mods[:, width : 2 * width]
    return (normed * (1.0 + scale) + shift).astype(jnp.bfloat16)


def start_sends(sends, gots, send_sem, recv_sem, local_sem, shards):
    me = lax.axis_index("ctx")
    region = lax.axis_index("region")
    mesh_id = pl.DeviceIdType.MESH
    barrier = pltpu.get_barrier_semaphore()
    for d in range(1, shards):
        peer = lax.rem(me + d, shards)
        pl.semaphore_signal(barrier, 1, device_id=(region, peer), device_id_type=mesh_id)
    pl.semaphore_wait(barrier, shards - 1)
    copies = []
    for a in range(len(sends)):
        local = pltpu.make_async_copy(sends[a].at[me], gots[a].at[me], local_sem.at[a])
        local.start()
        copies.append(local)
    for d in range(1, shards):
        peer = lax.rem(me + d, shards)
        for a in range(len(sends)):
            remote = pltpu.make_async_remote_copy(
                src_ref=sends[a].at[peer],
                dst_ref=gots[a].at[me],
                send_sem=send_sem.at[a, d - 1],
                recv_sem=recv_sem.at[a, d - 1],
                device_id=(region, peer),
                device_id_type=mesh_id,
            )
            remote.start()
            copies.append(remote)
    return copies


def exchange_kernel(*refs, count, shards):
    sends = refs[:count]
    gots = refs[count : 2 * count]
    copies = start_sends(sends, gots, *refs[2 * count :], shards)
    for copy in copies:
        copy.wait()


def send_scratch(count, shards):
    return [
        pltpu.SemaphoreType.DMA((count, shards - 1)),
        pltpu.SemaphoreType.DMA((count, shards - 1)),
        pltpu.SemaphoreType.DMA((count,)),
    ]


def exchange(arrays, shards, collective_id):
    count = len(arrays)
    kernel = functools.partial(exchange_kernel, count=count, shards=shards)
    any_spec = pl.BlockSpec(memory_space=pl.ANY)
    return pl.pallas_call(
        kernel,
        out_shape=[jax.ShapeDtypeStruct(x.shape, x.dtype) for x in arrays],
        in_specs=[any_spec] * count,
        out_specs=[any_spec] * count,
        scratch_shapes=send_scratch(count, shards),
        compiler_params=pltpu.CompilerParams(
            collective_id=collective_id, has_side_effects=True
        ),
    )(*arrays)


def attend_body(qt_ref, k_ref, vt_ref, o_ref, s_scr, inv_root):
    blocks, head_dim, q_rows = qt_ref.shape

    def one_block(b, carry):
        qt = qt_ref[b]

        def score(c, m):
            s = jnp.dot(k_ref[c], qt, preferred_element_type=jnp.float32) * inv_root
            s_scr[c] = s
            return jnp.maximum(m, jnp.max(s, axis=0, keepdims=True))

        m = lax.fori_loop(
            0, blocks, score, jnp.full((1, q_rows), -jnp.inf, jnp.float32), unroll=2
        )

        def accumulate(c, inner):
            total, acc = inner
            expo = jnp.exp(s_scr[c] - m)
            total = total + jnp.sum(expo, axis=0, keepdims=True)
            acc = acc + jnp.dot(
                vt_ref[c], expo.astype(jnp.bfloat16), preferred_element_type=jnp.float32
            )
            return total, acc

        total, acc = lax.fori_loop(
            0,
            blocks,
            accumulate,
            (
                jnp.zeros((1, q_rows), jnp.float32),
                jnp.zeros((head_dim, q_rows), jnp.float32),
            ),
            unroll=2,
        )
        o_ref[b] = (acc / total).astype(o_ref.dtype)
        return carry

    lax.fori_loop(0, blocks, one_block, 0)


def attend_send_kernel(*refs, count, shards, inv_root):
    qt_ref, k_ref, vt_ref = refs[:3]
    sends = refs[3 : 3 + count]
    o_ref = refs[3 + count]
    gots = refs[4 + count : 4 + 2 * count]
    s_scr = refs[4 + 2 * count]
    copies = start_sends(sends, gots, *refs[5 + 2 * count :], shards)
    attend_body(qt_ref, k_ref, vt_ref, o_ref, s_scr, inv_root)
    for copy in copies:
        copy.wait()


def attend_send(q_t, k_tok, v_t, sends, shards, inv_root, collective_id):
    blocks, head_dim, rows = q_t.shape
    count = len(sends)
    kernel = functools.partial(
        attend_send_kernel, count=count, shards=shards, inv_root=inv_root
    )
    any_spec = pl.BlockSpec(memory_space=pl.ANY)
    vmem_spec = pl.BlockSpec(memory_space=pltpu.VMEM)
    outs = pl.pallas_call(
        kernel,
        out_shape=[jax.ShapeDtypeStruct(q_t.shape, jnp.bfloat16)]
        + [jax.ShapeDtypeStruct(x.shape, x.dtype) for x in sends],
        in_specs=[vmem_spec] * 3 + [any_spec] * count,
        out_specs=[vmem_spec] + [any_spec] * count,
        scratch_shapes=[pltpu.VMEM((blocks, rows, rows), jnp.float32)]
        + send_scratch(count, shards),
        compiler_params=pltpu.CompilerParams(
            collective_id=collective_id,
            has_side_effects=True,
            vmem_limit_bytes=48 * 1024 * 1024,
        ),
    )(q_t, k_tok, v_t, *sends)
    return outs[0], outs[1:]


def head_pipeline(q_all, k_all, v_all, shards, inverse_root):
    pair = len(q_all)
    got = exchange([q_all[0], k_all[0], v_all[0]], shards, 0)
    backs = []
    for h in range(pair):
        if h + 1 < pair:
            sends = [q_all[h + 1], k_all[h + 1], v_all[h + 1]]
        else:
            sends = []
        if h > 0:
            sends = sends + [out_prev]
        out_prev, sent = attend_send(*got, sends, shards, inverse_root, 1 + h)
        if h + 1 < pair:
            got = sent[:3]
            sent = sent[3:]
        backs.extend(sent)
    (last_back,) = exchange([out_prev], shards, 1 + pair)
    backs.append(last_back)
    return jnp.stack(backs, axis=1)


def per_device(
    tokens, element_ids, element_slot, live_count, cond_table, w_ada, b_ada, w_qkv, w_out
):
    device_tokens = tokens[0]
    tok_rows, width = device_tokens.shape
    owners = lax.axis_size(("region", "ctx"))
    shards = lax.axis_size("ctx")
    elem_rows = cond_table.shape[0]
    capacity = -(-max(2, 3 * tok_rows // (2 * owners)) // 8) * 8
    slots = element_slot[element_ids[0]]
    owner_index = slots // elem_rows
    local_row = slots % elem_rows
    position = jnp.arange(tok_rows, dtype=jnp.int32)
    solid = position < live_count[0, 0]
    earlier = (
        (owner_index[:, None] == owner_index[None, :])
        & (position[None, :] < position[:, None])
        & solid[None, :]
    )
    place_rank = jnp.sum(earlier.astype(jnp.int32), axis=1)
    target = jnp.where(solid, owner_index * capacity + place_rank, owners * capacity)
    requests = jnp.zeros((owners * capacity,), jnp.int32).at[target].set(local_row, mode="drop")
    asked = lax.all_to_all(
        requests.reshape(owners, capacity),
        ("region", "ctx"),
        split_axis=0,
        concat_axis=0,
        tiled=True,
    ).reshape(-1)
    pick_at = jnp.minimum(target, owners * capacity - 1)
    served = cond_table[asked].reshape(owners, capacity, width)
    replies = lax.all_to_all(served, ("region", "ctx"), split_axis=0, concat_axis=0, tiled=True)
    picked = replies.reshape(owners * capacity, width)[pick_at]
    activated = jnp.where(solid[:, None], jax.nn.silu(picked.astype(jnp.float32)), 0.0).astype(
        jnp.bfloat16
    )
    mods = (jnp.dot(activated, w_ada, preferred_element_type=jnp.float32) + b_ada).astype(
        jnp.bfloat16
    )
    mods = mods.astype(jnp.float32)
    modulated = layer_modulate(device_tokens, mods, width)

    head_dim = width // HEADS
    pair = HEADS // shards
    inverse_root = 1.0 / math.sqrt(head_dim)
    w_parts = w_qkv.reshape(width, 3, shards, pair, head_dim)
    def project(i, h, pattern):
        return jnp.einsum(
            pattern, modulated, w_parts[:, i, :, h], preferred_element_type=jnp.float32
        ).astype(jnp.bfloat16)

    q_all = [project(0, h, "td,dpe->pet") for h in range(pair)]
    k_all = [project(1, h, "td,dpe->pte") for h in range(pair)]
    v_all = [project(2, h, "td,dpe->pet") for h in range(pair)]
    backs = head_pipeline(q_all, k_all, v_all, shards, inverse_root)
    w_out_parts = w_out.reshape(shards, pair, head_dim, width)
    projected = jnp.einsum(
        "phet,pheD->tD",
        backs,
        w_out_parts,
        preferred_element_type=jnp.float32,
    )
    gate = mods[:, 2 * width :]
    output = (device_tokens.astype(jnp.float32) + gate * projected).astype(jnp.bfloat16)
    return output[None]


def solution(mesh):
    placed = (
        P("region", "ctx", None),
        P("region", "ctx"),
        P(),
        P("region", "ctx"),
        P(("region", "ctx"), None),
        P(),
        P(),
        P(),
        P(),
    )
    return jax.shard_map(
        per_device, mesh=mesh, in_specs=placed, out_specs=P("region", "ctx", None), check_vma=False
    )
```

```python
import functools
import math

import jax
import jax.numpy as jnp
from jax import lax
from jax.experimental import pallas as pl
from jax.experimental.pallas import tpu as pltpu
from jax.sharding import PartitionSpec as P

HEADS = 16


def layer_modulate(device_tokens, mods, width):
    values = device_tokens.astype(jnp.float32)
    center = jnp.mean(values, axis=1, keepdims=True)
    spread = jnp.mean((values - center) ** 2, axis=1, keepdims=True)
    normed = (values - center) * lax.rsqrt(spread + 1e-06)
    shift = mods[:, :width]
    scale = mods[:, width : 2 * width]
    return (normed * (1.0 + scale) + shift).astype(jnp.bfloat16)


def start_sends(sends, gots, send_sem, recv_sem, local_sem, shards):
    me = lax.axis_index("ctx")
    region = lax.axis_index("region")
    mesh_id = pl.DeviceIdType.MESH
    barrier = pltpu.get_barrier_semaphore()
    for d in range(1, shards):
        peer = lax.rem(me + d, shards)
        pl.semaphore_signal(barrier, 1, device_id=(region, peer), device_id_type=mesh_id)
    pl.semaphore_wait(barrier, shards - 1)
    copies = []
    for a in range(len(sends)):
        local = pltpu.make_async_copy(sends[a].at[me], gots[a].at[me], local_sem.at[a])
        local.start()
        copies.append(local)
    for d in range(1, shards):
        peer = lax.rem(me + d, shards)
        for a in range(len(sends)):
            remote = pltpu.make_async_remote_copy(
                src_ref=sends[a].at[peer],
                dst_ref=gots[a].at[me],
                send_sem=send_sem.at[a, d - 1],
                recv_sem=recv_sem.at[a, d - 1],
                device_id=(region, peer),
                device_id_type=mesh_id,
            )
            remote.start()
            copies.append(remote)
    return copies


def exchange_kernel(*refs, count, shards):
    sends = refs[:count]
    gots = refs[count : 2 * count]
    copies = start_sends(sends, gots, *refs[2 * count :], shards)
    for copy in copies:
        copy.wait()


def send_scratch(count, shards):
    return [
        pltpu.SemaphoreType.DMA((count, shards - 1)),
        pltpu.SemaphoreType.DMA((count, shards - 1)),
        pltpu.SemaphoreType.DMA((count,)),
    ]


def exchange(arrays, shards, collective_id):
    count = len(arrays)
    kernel = functools.partial(exchange_kernel, count=count, shards=shards)
    any_spec = pl.BlockSpec(memory_space=pl.ANY)
    return pl.pallas_call(
        kernel,
        out_shape=[jax.ShapeDtypeStruct(x.shape, x.dtype) for x in arrays],
        in_specs=[any_spec] * count,
        out_specs=[any_spec] * count,
        scratch_shapes=send_scratch(count, shards),
        compiler_params=pltpu.CompilerParams(
            collective_id=collective_id, has_side_effects=True
        ),
    )(*arrays)


def attend_body(qt_ref, k_ref, vt_ref, o_ref, s_scr, inv_root, after_block=None):
    blocks, head_dim, q_rows = qt_ref.shape

    def one_block(b, carry):
        qt = qt_ref[b]

        def score(c, m):
            s = jnp.dot(k_ref[c], qt, preferred_element_type=jnp.float32) * inv_root
            s_scr[c] = s
            return jnp.maximum(m, jnp.max(s, axis=0, keepdims=True))

        m = lax.fori_loop(
            0, blocks, score, jnp.full((1, q_rows), -jnp.inf, jnp.float32), unroll=2
        )

        def accumulate(c, inner):
            total, acc = inner
            expo = jnp.exp(s_scr[c] - m)
            total = total + jnp.sum(expo, axis=0, keepdims=True)
            acc = acc + jnp.dot(
                vt_ref[c], expo.astype(jnp.bfloat16), preferred_element_type=jnp.float32
            )
            return total, acc

        total, acc = lax.fori_loop(
            0,
            blocks,
            accumulate,
            (
                jnp.zeros((1, q_rows), jnp.float32),
                jnp.zeros((head_dim, q_rows), jnp.float32),
            ),
            unroll=2,
        )
        o_ref[b] = (acc / total).astype(o_ref.dtype)
        if after_block is not None:
            after_block(b)
        return carry

    lax.fori_loop(0, blocks, one_block, 0)


def attend_send_kernel(*refs, count, shards, inv_root, stream):
    qt_ref, k_ref, vt_ref = refs[:3]
    sends = refs[3 : 3 + count]
    o_ref = refs[3 + count]
    gots = refs[4 + count : 4 + 2 * count]
    rest = refs[4 + 2 * count :]
    if stream:
        back_ref = rest[0]
        rest = rest[1:]
    s_scr = rest[0]
    copies = start_sends(sends, gots, *rest[1:4], shards)
    after_block = None
    if stream:
        block_send, block_recv, block_local = rest[4:7]
        me = lax.axis_index("ctx")
        region = lax.axis_index("region")

        def remote_block(b):
            return pltpu.make_async_remote_copy(
                src_ref=o_ref.at[b],
                dst_ref=back_ref.at[me],
                send_sem=block_send.at[b],
                recv_sem=block_recv.at[me],
                device_id=(region, b),
                device_id_type=pl.DeviceIdType.MESH,
            )

        def local_block(b):
            return pltpu.make_async_copy(o_ref.at[b], back_ref.at[b], block_local.at[0])

        def after_block(b):
            @pl.when(b == me)
            def _():
                local_block(b).start()

            @pl.when(b != me)
            def _():
                remote_block(b).start()

    attend_body(qt_ref, k_ref, vt_ref, o_ref, s_scr, inv_root, after_block)
    for copy in copies:
        copy.wait()
    if stream:
        for b in range(shards):
            @pl.when(b == me)
            def _():
                local_block(b).wait()

            @pl.when(b != me)
            def _():
                remote_block(b).wait_send()
                pltpu.make_async_remote_copy(
                    src_ref=o_ref.at[b],
                    dst_ref=back_ref.at[b],
                    send_sem=block_send.at[b],
                    recv_sem=block_recv.at[b],
                    device_id=(region, b),
                    device_id_type=pl.DeviceIdType.MESH,
                ).wait_recv()


def attend_send(q_t, k_tok, v_t, sends, shards, inv_root, collective_id, stream=False):
    blocks, head_dim, rows = q_t.shape
    count = len(sends)
    kernel = functools.partial(
        attend_send_kernel, count=count, shards=shards, inv_root=inv_root, stream=stream
    )
    any_spec = pl.BlockSpec(memory_space=pl.ANY)
    vmem_spec = pl.BlockSpec(memory_space=pltpu.VMEM)
    out_shape = [jax.ShapeDtypeStruct(q_t.shape, jnp.bfloat16)]
    out_shape += [jax.ShapeDtypeStruct(x.shape, x.dtype) for x in sends]
    out_specs = [vmem_spec] + [any_spec] * count
    scratch = [pltpu.VMEM((blocks, rows, rows), jnp.float32)] + send_scratch(count, shards)
    if stream:
        out_shape.append(jax.ShapeDtypeStruct(q_t.shape, jnp.bfloat16))
        out_specs.append(any_spec)
        scratch += [
            pltpu.SemaphoreType.DMA((shards,)),
            pltpu.SemaphoreType.DMA((shards,)),
            pltpu.SemaphoreType.DMA((1,)),
        ]
    outs = pl.pallas_call(
        kernel,
        out_shape=out_shape,
        in_specs=[vmem_spec] * 3 + [any_spec] * count,
        out_specs=out_specs,
        scratch_shapes=scratch,
        compiler_params=pltpu.CompilerParams(
            collective_id=collective_id,
            has_side_effects=True,
            vmem_limit_bytes=48 * 1024 * 1024,
        ),
    )(q_t, k_tok, v_t, *sends)
    return outs[0], outs[1:]


def head_pipeline(q_all, k_all, v_all, shards, inverse_root):
    pair = len(q_all)
    got = exchange([q_all[0], k_all[0], v_all[0]], shards, 0)
    backs = []
    for h in range(pair):
        last = h + 1 == pair
        sends = [] if last else [q_all[h + 1], k_all[h + 1], v_all[h + 1]]
        if h > 0:
            sends = sends + [out_prev]
        out_prev, sent = attend_send(
            *got, sends, shards, inverse_root, 1 + h, stream=last
        )
        if not last:
            got = sent[:3]
            sent = sent[3:]
        backs.extend(sent)
    return jnp.stack(backs, axis=1)


def per_device(
    tokens, element_ids, element_slot, live_count, cond_table, w_ada, b_ada, w_qkv, w_out
):
    device_tokens = tokens[0]
    tok_rows, width = device_tokens.shape
    owners = lax.axis_size(("region", "ctx"))
    shards = lax.axis_size("ctx")
    elem_rows = cond_table.shape[0]
    capacity = -(-max(2, 3 * tok_rows // (2 * owners)) // 8) * 8
    slots = element_slot[element_ids[0]]
    owner_index = slots // elem_rows
    local_row = slots % elem_rows
    position = jnp.arange(tok_rows, dtype=jnp.int32)
    solid = position < live_count[0, 0]
    earlier = (
        (owner_index[:, None] == owner_index[None, :])
        & (position[None, :] < position[:, None])
        & solid[None, :]
    )
    place_rank = jnp.sum(earlier.astype(jnp.int32), axis=1)
    target = jnp.where(solid, owner_index * capacity + place_rank, owners * capacity)
    requests = jnp.zeros((owners * capacity,), jnp.int32).at[target].set(local_row, mode="drop")
    asked = lax.all_to_all(
        requests.reshape(owners, capacity),
        ("region", "ctx"),
        split_axis=0,
        concat_axis=0,
        tiled=True,
    ).reshape(-1)
    pick_at = jnp.minimum(target, owners * capacity - 1)
    served = cond_table[asked].reshape(owners, capacity, width)
    replies = lax.all_to_all(served, ("region", "ctx"), split_axis=0, concat_axis=0, tiled=True)
    picked = replies.reshape(owners * capacity, width)[pick_at]
    activated = jnp.where(solid[:, None], jax.nn.silu(picked.astype(jnp.float32)), 0.0).astype(
        jnp.bfloat16
    )
    mods = (jnp.dot(activated, w_ada, preferred_element_type=jnp.float32) + b_ada).astype(
        jnp.bfloat16
    )
    mods = mods.astype(jnp.float32)
    modulated = layer_modulate(device_tokens, mods, width)

    head_dim = width // HEADS
    pair = HEADS // shards
    inverse_root = 1.0 / math.sqrt(head_dim)
    w_parts = w_qkv.reshape(width, 3, shards, pair, head_dim)
    def project(i, h, pattern):
        return jnp.einsum(
            pattern, modulated, w_parts[:, i, :, h], preferred_element_type=jnp.float32
        ).astype(jnp.bfloat16)

    q_all = [project(0, h, "td,dpe->pet") for h in range(pair)]
    k_all = [project(1, h, "td,dpe->pte") for h in range(pair)]
    v_all = [project(2, h, "td,dpe->pet") for h in range(pair)]
    backs = head_pipeline(q_all, k_all, v_all, shards, inverse_root)
    w_out_parts = w_out.reshape(shards, pair, head_dim, width)
    projected = jnp.einsum(
        "phet,pheD->tD",
        backs,
        w_out_parts,
        preferred_element_type=jnp.float32,
    )
    gate = mods[:, 2 * width :]
    output = (device_tokens.astype(jnp.float32) + gate * projected).astype(jnp.bfloat16)
    return output[None]


def solution(mesh):
    placed = (
        P("region", "ctx", None),
        P("region", "ctx"),
        P(),
        P("region", "ctx"),
        P(("region", "ctx"), None),
        P(),
        P(),
        P(),
        P(),
    )
    return jax.shard_map(
        per_device, mesh=mesh, in_specs=placed, out_specs=P("region", "ctx", None), check_vma=False
    )
```

```python
import functools
import math

import jax
import jax.numpy as jnp
from jax import lax
from jax.experimental import pallas as pl
from jax.experimental.pallas import tpu as pltpu
from jax.sharding import PartitionSpec as P

HEADS = 16


def layer_modulate(device_tokens, mods, width):
    values = device_tokens.astype(jnp.float32)
    center = jnp.mean(values, axis=1, keepdims=True)
    spread = jnp.mean((values - center) ** 2, axis=1, keepdims=True)
    normed = (values - center) * lax.rsqrt(spread + 1e-06)
    shift = mods[:, :width]
    scale = mods[:, width : 2 * width]
    return (normed * (1.0 + scale) + shift).astype(jnp.bfloat16)


def start_sends(sends, gots, send_sem, recv_sem, local_sem, shards):
    me = lax.axis_index("ctx")
    region = lax.axis_index("region")
    mesh_id = pl.DeviceIdType.MESH
    barrier = pltpu.get_barrier_semaphore()
    for d in range(1, shards):
        peer = lax.rem(me + d, shards)
        pl.semaphore_signal(barrier, 1, device_id=(region, peer), device_id_type=mesh_id)
    pl.semaphore_wait(barrier, shards - 1)
    copies = []
    for a in range(len(sends)):
        local = pltpu.make_async_copy(sends[a].at[me], gots[a].at[me], local_sem.at[a])
        local.start()
        copies.append(local)
    for d in range(1, shards):
        peer = lax.rem(me + d, shards)
        for a in range(len(sends)):
            remote = pltpu.make_async_remote_copy(
                src_ref=sends[a].at[peer],
                dst_ref=gots[a].at[me],
                send_sem=send_sem.at[a, d - 1],
                recv_sem=recv_sem.at[a, d - 1],
                device_id=(region, peer),
                device_id_type=mesh_id,
            )
            remote.start()
            copies.append(remote)
    return copies


def exchange_kernel(*refs, count, shards):
    sends = refs[:count]
    gots = refs[count : 2 * count]
    copies = start_sends(sends, gots, *refs[2 * count :], shards)
    for copy in copies:
        copy.wait()


def send_scratch(count, shards):
    return [
        pltpu.SemaphoreType.DMA((count, shards - 1)),
        pltpu.SemaphoreType.DMA((count, shards - 1)),
        pltpu.SemaphoreType.DMA((count,)),
    ]


def exchange(arrays, shards, collective_id):
    count = len(arrays)
    kernel = functools.partial(exchange_kernel, count=count, shards=shards)
    any_spec = pl.BlockSpec(memory_space=pl.ANY)
    return pl.pallas_call(
        kernel,
        out_shape=[jax.ShapeDtypeStruct(x.shape, x.dtype) for x in arrays],
        in_specs=[any_spec] * count,
        out_specs=[any_spec] * count,
        scratch_shapes=send_scratch(count, shards),
        compiler_params=pltpu.CompilerParams(
            collective_id=collective_id, has_side_effects=True
        ),
    )(*arrays)


def attend_body(qt_ref, k_ref, vt_ref, o_ref, s_scr, inv_root, after_block=None):
    blocks, head_dim, q_rows = qt_ref.shape

    def one_block(b, carry):
        qt = qt_ref[b]

        def score(c, m):
            s = jnp.dot(k_ref[c], qt, preferred_element_type=jnp.float32) * inv_root
            s_scr[c] = s
            return jnp.maximum(m, jnp.max(s, axis=0, keepdims=True))

        m = lax.fori_loop(
            0, blocks, score, jnp.full((1, q_rows), -jnp.inf, jnp.float32), unroll=2
        )

        def accumulate(c, inner):
            total, acc = inner
            expo = jnp.exp(s_scr[c] - m)
            total = total + jnp.sum(expo, axis=0, keepdims=True)
            acc = acc + jnp.dot(
                vt_ref[c], expo.astype(jnp.bfloat16), preferred_element_type=jnp.float32
            )
            return total, acc

        total, acc = lax.fori_loop(
            0,
            blocks,
            accumulate,
            (
                jnp.zeros((1, q_rows), jnp.float32),
                jnp.zeros((head_dim, q_rows), jnp.float32),
            ),
            unroll=2,
        )
        o_ref[b] = (acc / total).astype(o_ref.dtype)
        if after_block is not None:
            after_block(b)
        return carry

    lax.fori_loop(0, blocks, one_block, 0)


def attend_send_kernel(*refs, count, shards, inv_root, stream):
    qt_ref, k_ref, vt_ref = refs[:3]
    sends = refs[3 : 3 + count]
    o_ref = refs[3 + count]
    gots = refs[4 + count : 4 + 2 * count]
    rest = refs[4 + 2 * count :]
    if stream:
        back_ref = rest[0]
        rest = rest[1:]
    s_scr = rest[0]
    copies = start_sends(sends, gots, *rest[1:4], shards)
    after_block = None
    if stream:
        block_send, block_recv, block_local = rest[4:7]
        me = lax.axis_index("ctx")
        region = lax.axis_index("region")

        def remote_block(b):
            return pltpu.make_async_remote_copy(
                src_ref=o_ref.at[b],
                dst_ref=back_ref.at[me],
                send_sem=block_send.at[b],
                recv_sem=block_recv.at[me],
                device_id=(region, b),
                device_id_type=pl.DeviceIdType.MESH,
            )

        def local_block(b):
            return pltpu.make_async_copy(o_ref.at[b], back_ref.at[b], block_local.at[0])

        def after_block(b):
            @pl.when(b == me)
            def _():
                local_block(b).start()

            @pl.when(b != me)
            def _():
                remote_block(b).start()

    attend_body(qt_ref, k_ref, vt_ref, o_ref, s_scr, inv_root, after_block)
    for copy in copies:
        copy.wait()
    if stream:
        for b in range(shards):
            @pl.when(b == me)
            def _():
                local_block(b).wait()

            @pl.when(b != me)
            def _():
                remote_block(b).wait_send()
                pltpu.make_async_remote_copy(
                    src_ref=o_ref.at[b],
                    dst_ref=back_ref.at[b],
                    send_sem=block_send.at[b],
                    recv_sem=block_recv.at[b],
                    device_id=(region, b),
                    device_id_type=pl.DeviceIdType.MESH,
                ).wait_recv()


def attend_send(q_t, k_tok, v_t, sends, shards, inv_root, collective_id, stream=False):
    blocks, head_dim, rows = q_t.shape
    count = len(sends)
    kernel = functools.partial(
        attend_send_kernel, count=count, shards=shards, inv_root=inv_root, stream=stream
    )
    any_spec = pl.BlockSpec(memory_space=pl.ANY)
    vmem_spec = pl.BlockSpec(memory_space=pltpu.VMEM)
    out_shape = [jax.ShapeDtypeStruct(q_t.shape, jnp.bfloat16)]
    out_shape += [jax.ShapeDtypeStruct(x.shape, x.dtype) for x in sends]
    out_specs = [vmem_spec] + [any_spec] * count
    scratch = [pltpu.VMEM((blocks, rows, rows), jnp.float32)] + send_scratch(count, shards)
    if stream:
        out_shape.append(jax.ShapeDtypeStruct(q_t.shape, jnp.bfloat16))
        out_specs.append(any_spec)
        scratch += [
            pltpu.SemaphoreType.DMA((shards,)),
            pltpu.SemaphoreType.DMA((shards,)),
            pltpu.SemaphoreType.DMA((1,)),
        ]
    outs = pl.pallas_call(
        kernel,
        out_shape=out_shape,
        in_specs=[vmem_spec] * 3 + [any_spec] * count,
        out_specs=out_specs,
        scratch_shapes=scratch,
        compiler_params=pltpu.CompilerParams(
            collective_id=collective_id,
            has_side_effects=True,
            vmem_limit_bytes=48 * 1024 * 1024,
        ),
    )(q_t, k_tok, v_t, *sends)
    return outs[0], outs[1:]


def project_kernel(mod_ref, w_ref, *refs, shards, pair, head_dim):
    got0 = refs[:3]
    later = refs[3 : 3 * pair]
    send0 = refs[3 * pair : 3 * pair + 3]
    sems = refs[3 * pair + 3 :]
    modulated = mod_ref[...]

    def fill(h, dests):
        for i in range(3):
            out_t = lax.dot_general(
                w_ref[i, h],
                modulated,
                (((1,), (1,)), ((), ())),
                preferred_element_type=jnp.float32,
            )
            for p in range(shards):
                piece = out_t[p * head_dim : (p + 1) * head_dim]
                if i == 1:
                    piece = piece.T
                dests[i][p] = piece.astype(jnp.bfloat16)

    fill(0, send0)
    copies = start_sends(send0, got0, *sems, shards)
    for h in range(1, pair):
        fill(h, later[3 * (h - 1) : 3 * h])
    for copy in copies:
        copy.wait()


def project_send(modulated, w_t, shards, pair, head_dim):
    rows, width = modulated.shape
    q_shape = jax.ShapeDtypeStruct((shards, head_dim, rows), jnp.bfloat16)
    k_shape = jax.ShapeDtypeStruct((shards, rows, head_dim), jnp.bfloat16)
    shapes = [q_shape, k_shape, q_shape]
    kernel = functools.partial(
        project_kernel, shards=shards, pair=pair, head_dim=head_dim
    )
    any_spec = pl.BlockSpec(memory_space=pl.ANY)
    vmem_spec = pl.BlockSpec(memory_space=pltpu.VMEM)
    outs = pl.pallas_call(
        kernel,
        out_shape=shapes * pair,
        in_specs=[vmem_spec, vmem_spec],
        out_specs=[any_spec] * 3 + [vmem_spec] * (3 * (pair - 1)),
        scratch_shapes=[pltpu.VMEM(x.shape, x.dtype) for x in shapes]
        + send_scratch(3, shards),
        compiler_params=pltpu.CompilerParams(
            collective_id=pair + 1,
            has_side_effects=True,
            vmem_limit_bytes=48 * 1024 * 1024,
        ),
    )(modulated, w_t)
    return outs[:3], [outs[3 * h : 3 * h + 3] for h in range(1, pair)]


def head_pipeline(modulated, w_t, shards, pair, head_dim, inverse_root):
    got, later = project_send(modulated, w_t, shards, pair, head_dim)
    backs = []
    for h in range(pair):
        last = h + 1 == pair
        sends = [] if last else list(later[h])
        if h > 0:
            sends = sends + [out_prev]
        out_prev, sent = attend_send(
            *got, sends, shards, inverse_root, 1 + h, stream=last
        )
        if not last:
            got = sent[:3]
            sent = sent[3:]
        backs.extend(sent)
    return jnp.stack(backs, axis=1)


def per_device(
    tokens, element_ids, element_slot, live_count, cond_table, w_ada, b_ada, w_qkv, w_out
):
    device_tokens = tokens[0]
    tok_rows, width = device_tokens.shape
    owners = lax.axis_size(("region", "ctx"))
    shards = lax.axis_size("ctx")
    elem_rows = cond_table.shape[0]
    capacity = -(-max(2, 3 * tok_rows // (2 * owners)) // 8) * 8
    slots = element_slot[element_ids[0]]
    owner_index = slots // elem_rows
    local_row = slots % elem_rows
    position = jnp.arange(tok_rows, dtype=jnp.int32)
    solid = position < live_count[0, 0]
    earlier = (
        (owner_index[:, None] == owner_index[None, :])
        & (position[None, :] < position[:, None])
        & solid[None, :]
    )
    place_rank = jnp.sum(earlier.astype(jnp.int32), axis=1)
    target = jnp.where(solid, owner_index * capacity + place_rank, owners * capacity)
    requests = jnp.zeros((owners * capacity,), jnp.int32).at[target].set(local_row, mode="drop")
    asked = lax.all_to_all(
        requests.reshape(owners, capacity),
        ("region", "ctx"),
        split_axis=0,
        concat_axis=0,
        tiled=True,
    ).reshape(-1)
    pick_at = jnp.minimum(target, owners * capacity - 1)
    served = cond_table[asked].reshape(owners, capacity, width)
    replies = lax.all_to_all(served, ("region", "ctx"), split_axis=0, concat_axis=0, tiled=True)
    picked = replies.reshape(owners * capacity, width)[pick_at]
    activated = jnp.where(solid[:, None], jax.nn.silu(picked.astype(jnp.float32)), 0.0).astype(
        jnp.bfloat16
    )
    mods = (jnp.dot(activated, w_ada, preferred_element_type=jnp.float32) + b_ada).astype(
        jnp.bfloat16
    )
    mods = mods.astype(jnp.float32)
    modulated = layer_modulate(device_tokens, mods, width)

    head_dim = width // HEADS
    pair = HEADS // shards
    inverse_root = 1.0 / math.sqrt(head_dim)
    w_t = (
        w_qkv.reshape(width, 3, shards, pair, head_dim)
        .transpose(1, 3, 2, 4, 0)
        .reshape(3, pair, shards * head_dim, width)
    )
    backs = head_pipeline(modulated, w_t, shards, pair, head_dim, inverse_root)
    w_out_parts = w_out.reshape(shards, pair, head_dim, width)
    projected = jnp.einsum(
        "phet,pheD->tD",
        backs,
        w_out_parts,
        preferred_element_type=jnp.float32,
    )
    gate = mods[:, 2 * width :]
    output = (device_tokens.astype(jnp.float32) + gate * projected).astype(jnp.bfloat16)
    return output[None]


def solution(mesh):
    placed = (
        P("region", "ctx", None),
        P("region", "ctx"),
        P(),
        P("region", "ctx"),
        P(("region", "ctx"), None),
        P(),
        P(),
        P(),
        P(),
    )
    return jax.shard_map(
        per_device, mesh=mesh, in_specs=placed, out_specs=P("region", "ctx", None), check_vma=False
    )
```

```python
import functools
import math

import jax
import jax.numpy as jnp
from jax import lax
from jax.experimental import pallas as pl
from jax.experimental.pallas import tpu as pltpu
from jax.sharding import PartitionSpec as P

HEADS = 16


def layer_modulate(device_tokens, mods, width):
    values = device_tokens.astype(jnp.float32)
    center = jnp.mean(values, axis=1, keepdims=True)
    spread = jnp.mean((values - center) ** 2, axis=1, keepdims=True)
    normed = (values - center) * lax.rsqrt(spread + 1e-06)
    shift = mods[:, :width]
    scale = mods[:, width : 2 * width]
    return (normed * (1.0 + scale) + shift).astype(jnp.bfloat16)


def start_sends(sends, gots, send_sem, recv_sem, local_sem, shards):
    me = lax.axis_index("ctx")
    region = lax.axis_index("region")
    mesh_id = pl.DeviceIdType.MESH
    barrier = pltpu.get_barrier_semaphore()
    for d in range(1, shards):
        peer = lax.rem(me + d, shards)
        pl.semaphore_signal(barrier, 1, device_id=(region, peer), device_id_type=mesh_id)
    pl.semaphore_wait(barrier, shards - 1)
    copies = []
    for a in range(len(sends)):
        local = pltpu.make_async_copy(sends[a].at[me], gots[a].at[me], local_sem.at[a])
        local.start()
        copies.append(local)
    for d in range(1, shards):
        peer = lax.rem(me + d, shards)
        for a in range(len(sends)):
            remote = pltpu.make_async_remote_copy(
                src_ref=sends[a].at[peer],
                dst_ref=gots[a].at[me],
                send_sem=send_sem.at[a, d - 1],
                recv_sem=recv_sem.at[a, d - 1],
                device_id=(region, peer),
                device_id_type=mesh_id,
            )
            remote.start()
            copies.append(remote)
    return copies


def exchange_kernel(*refs, count, shards):
    sends = refs[:count]
    gots = refs[count : 2 * count]
    copies = start_sends(sends, gots, *refs[2 * count :], shards)
    for copy in copies:
        copy.wait()


def send_scratch(count, shards):
    return [
        pltpu.SemaphoreType.DMA((count, shards - 1)),
        pltpu.SemaphoreType.DMA((count, shards - 1)),
        pltpu.SemaphoreType.DMA((count,)),
    ]


def exchange(arrays, shards, collective_id):
    count = len(arrays)
    kernel = functools.partial(exchange_kernel, count=count, shards=shards)
    any_spec = pl.BlockSpec(memory_space=pl.ANY)
    return pl.pallas_call(
        kernel,
        out_shape=[jax.ShapeDtypeStruct(x.shape, x.dtype) for x in arrays],
        in_specs=[any_spec] * count,
        out_specs=[any_spec] * count,
        scratch_shapes=send_scratch(count, shards),
        compiler_params=pltpu.CompilerParams(
            collective_id=collective_id, has_side_effects=True
        ),
    )(*arrays)


def attend_body(qt_ref, k_ref, vt_ref, o_ref, s_scr, inv_root, after_block=None):
    blocks, head_dim, q_rows = qt_ref.shape

    def one_block(b, carry):
        qt = qt_ref[b]

        def score(c, m):
            s = jnp.dot(k_ref[c], qt, preferred_element_type=jnp.float32) * inv_root
            s_scr[c] = s
            return jnp.maximum(m, jnp.max(s, axis=0, keepdims=True))

        m = lax.fori_loop(
            0, blocks, score, jnp.full((1, q_rows), -jnp.inf, jnp.float32), unroll=2
        )

        def accumulate(c, inner):
            total, acc = inner
            expo = jnp.exp(s_scr[c] - m)
            total = total + jnp.sum(expo, axis=0, keepdims=True)
            acc = acc + jnp.dot(
                vt_ref[c], expo.astype(jnp.bfloat16), preferred_element_type=jnp.float32
            )
            return total, acc

        total, acc = lax.fori_loop(
            0,
            blocks,
            accumulate,
            (
                jnp.zeros((1, q_rows), jnp.float32),
                jnp.zeros((head_dim, q_rows), jnp.float32),
            ),
            unroll=2,
        )
        o_ref[b] = (acc / total).astype(o_ref.dtype)
        if after_block is not None:
            after_block(b)
        return carry

    lax.fori_loop(0, blocks, one_block, 0)


def attend_send_kernel(*refs, count, shards, inv_root, stream):
    qt_ref, k_ref, vt_ref = refs[:3]
    sends = refs[3 : 3 + count]
    o_ref = refs[3 + count]
    gots = refs[4 + count : 4 + 2 * count]
    rest = refs[4 + 2 * count :]
    if stream:
        back_ref = rest[0]
        rest = rest[1:]
    s_scr = rest[0]
    copies = start_sends(sends, gots, *rest[1:4], shards)
    after_block = None
    if stream:
        block_send, block_recv, block_local = rest[4:7]
        me = lax.axis_index("ctx")
        region = lax.axis_index("region")

        def remote_block(b):
            return pltpu.make_async_remote_copy(
                src_ref=o_ref.at[b],
                dst_ref=back_ref.at[me],
                send_sem=block_send.at[b],
                recv_sem=block_recv.at[me],
                device_id=(region, b),
                device_id_type=pl.DeviceIdType.MESH,
            )

        def local_block(b):
            return pltpu.make_async_copy(o_ref.at[b], back_ref.at[b], block_local.at[0])

        def after_block(b):
            @pl.when(b == me)
            def _():
                local_block(b).start()

            @pl.when(b != me)
            def _():
                remote_block(b).start()

    attend_body(qt_ref, k_ref, vt_ref, o_ref, s_scr, inv_root, after_block)
    for copy in copies:
        copy.wait()
    if stream:
        for b in range(shards):
            @pl.when(b == me)
            def _():
                local_block(b).wait()

            @pl.when(b != me)
            def _():
                remote_block(b).wait_send()
                pltpu.make_async_remote_copy(
                    src_ref=o_ref.at[b],
                    dst_ref=back_ref.at[b],
                    send_sem=block_send.at[b],
                    recv_sem=block_recv.at[b],
                    device_id=(region, b),
                    device_id_type=pl.DeviceIdType.MESH,
                ).wait_recv()


def attend_send(q_t, k_tok, v_t, sends, shards, inv_root, collective_id, stream=False):
    blocks, head_dim, rows = q_t.shape
    count = len(sends)
    kernel = functools.partial(
        attend_send_kernel, count=count, shards=shards, inv_root=inv_root, stream=stream
    )
    any_spec = pl.BlockSpec(memory_space=pl.ANY)
    vmem_spec = pl.BlockSpec(memory_space=pltpu.VMEM)
    out_shape = [jax.ShapeDtypeStruct(q_t.shape, jnp.bfloat16)]
    out_shape += [jax.ShapeDtypeStruct(x.shape, x.dtype) for x in sends]
    out_specs = [vmem_spec] + [any_spec] * count
    scratch = [pltpu.VMEM((blocks, rows, rows), jnp.float32)] + send_scratch(count, shards)
    if stream:
        out_shape.append(jax.ShapeDtypeStruct(q_t.shape, jnp.bfloat16))
        out_specs.append(any_spec)
        scratch += [
            pltpu.SemaphoreType.DMA((shards,)),
            pltpu.SemaphoreType.DMA((shards,)),
            pltpu.SemaphoreType.DMA((1,)),
        ]
    outs = pl.pallas_call(
        kernel,
        out_shape=out_shape,
        in_specs=[vmem_spec] * 3 + [any_spec] * count,
        out_specs=out_specs,
        scratch_shapes=scratch,
        compiler_params=pltpu.CompilerParams(
            collective_id=collective_id,
            has_side_effects=True,
            vmem_limit_bytes=48 * 1024 * 1024,
        ),
    )(q_t, k_tok, v_t, *sends)
    return outs[0], outs[1:]


def project_kernel(mod_ref, w_ref, *refs, shards, pair, head_dim):
    got0 = refs[:3]
    later = refs[3 : 3 * pair]
    send0 = refs[3 * pair : 3 * pair + 3]
    sems = refs[3 * pair + 3 :]
    modulated = mod_ref[...]

    def fill(h, dests):
        for i in range(3):
            out_t = lax.dot_general(
                w_ref[i, h],
                modulated,
                (((1,), (1,)), ((), ())),
                preferred_element_type=jnp.float32,
            )
            for p in range(shards):
                piece = out_t[p * head_dim : (p + 1) * head_dim]
                if i == 1:
                    piece = piece.T
                dests[i][p] = piece.astype(jnp.bfloat16)

    fill(0, send0)
    copies = start_sends(send0, got0, *sems, shards)
    for h in range(1, pair):
        fill(h, later[3 * (h - 1) : 3 * h])
    for copy in copies:
        copy.wait()


def project_send(modulated, w_t, shards, pair, head_dim):
    rows, width = modulated.shape
    q_shape = jax.ShapeDtypeStruct((shards, head_dim, rows), jnp.bfloat16)
    k_shape = jax.ShapeDtypeStruct((shards, rows, head_dim), jnp.bfloat16)
    shapes = [q_shape, k_shape, q_shape]
    kernel = functools.partial(
        project_kernel, shards=shards, pair=pair, head_dim=head_dim
    )
    any_spec = pl.BlockSpec(memory_space=pl.ANY)
    vmem_spec = pl.BlockSpec(memory_space=pltpu.VMEM)
    outs = pl.pallas_call(
        kernel,
        out_shape=shapes * pair,
        in_specs=[vmem_spec, vmem_spec],
        out_specs=[any_spec] * 3 + [vmem_spec] * (3 * (pair - 1)),
        scratch_shapes=[pltpu.VMEM(x.shape, x.dtype) for x in shapes]
        + send_scratch(3, shards),
        compiler_params=pltpu.CompilerParams(
            collective_id=pair + 1,
            has_side_effects=True,
            vmem_limit_bytes=48 * 1024 * 1024,
        ),
    )(modulated, w_t)
    return outs[:3], [outs[3 * h : 3 * h + 3] for h in range(1, pair)]


def head_pipeline(modulated, w_t, shards, pair, head_dim, inverse_root):
    got, later = project_send(modulated, w_t, shards, pair, head_dim)
    backs = []
    for h in range(pair):
        last = h + 1 == pair
        sends = [] if last else list(later[h])
        if h > 0:
            sends = sends + [out_prev]
        out_prev, sent = attend_send(
            *got, sends, shards, inverse_root, 1 + h, stream=last
        )
        if not last:
            got = sent[:3]
            sent = sent[3:]
        backs.extend(sent)
    return jnp.stack(backs, axis=1)


def per_device(
    tokens, element_ids, element_slot, live_count, cond_table, w_ada, b_ada, w_qkv, w_out
):
    device_tokens = tokens[0]
    tok_rows, width = device_tokens.shape
    owners = lax.axis_size(("region", "ctx"))
    shards = lax.axis_size("ctx")
    elem_rows = cond_table.shape[0]
    capacity = -(-max(2, 3 * tok_rows // (2 * owners)) // 8) * 8
    slots = element_slot[element_ids[0]]
    owner_index = slots // elem_rows
    local_row = slots % elem_rows
    position = jnp.arange(tok_rows, dtype=jnp.int32)
    solid = position < live_count[0, 0]
    earlier = (
        (owner_index[:, None] == owner_index[None, :])
        & (position[None, :] < position[:, None])
        & solid[None, :]
    )
    place_rank = jnp.sum(earlier.astype(jnp.int32), axis=1)
    target = jnp.where(solid, owner_index * capacity + place_rank, owners * capacity)
    requests = jnp.zeros((owners * capacity,), jnp.int32).at[target].set(local_row, mode="drop")
    asked = lax.all_to_all(
        requests.reshape(owners, capacity),
        ("region", "ctx"),
        split_axis=0,
        concat_axis=0,
        tiled=True,
    ).reshape(-1)
    pick_at = jnp.minimum(target, owners * capacity - 1)
    served_hot = (asked[:, None] == jnp.arange(elem_rows, dtype=jnp.int32)[None, :]).astype(
        jnp.bfloat16
    )
    served = (
        jnp.dot(served_hot, cond_table, preferred_element_type=jnp.float32)
        .astype(jnp.bfloat16)
        .reshape(owners, capacity, width)
    )
    replies = lax.all_to_all(served, ("region", "ctx"), split_axis=0, concat_axis=0, tiled=True)
    pick_hot = (
        pick_at[:, None] == jnp.arange(owners * capacity, dtype=jnp.int32)[None, :]
    ).astype(jnp.bfloat16)
    picked = jnp.dot(
        pick_hot, replies.reshape(owners * capacity, width), preferred_element_type=jnp.float32
    )
    activated = jnp.where(solid[:, None], jax.nn.silu(picked.astype(jnp.float32)), 0.0).astype(
        jnp.bfloat16
    )
    mods = (jnp.dot(activated, w_ada, preferred_element_type=jnp.float32) + b_ada).astype(
        jnp.bfloat16
    )
    mods = mods.astype(jnp.float32)
    modulated = layer_modulate(device_tokens, mods, width)

    head_dim = width // HEADS
    pair = HEADS // shards
    inverse_root = 1.0 / math.sqrt(head_dim)
    w_t = (
        w_qkv.reshape(width, 3, shards, pair, head_dim)
        .transpose(1, 3, 2, 4, 0)
        .reshape(3, pair, shards * head_dim, width)
    )
    backs = head_pipeline(modulated, w_t, shards, pair, head_dim, inverse_root)
    w_out_parts = w_out.reshape(shards, pair, head_dim, width)
    projected = jnp.einsum(
        "phet,pheD->tD",
        backs,
        w_out_parts,
        preferred_element_type=jnp.float32,
    )
    gate = mods[:, 2 * width :]
    output = (device_tokens.astype(jnp.float32) + gate * projected).astype(jnp.bfloat16)
    return output[None]


def solution(mesh):
    placed = (
        P("region", "ctx", None),
        P("region", "ctx"),
        P(),
        P("region", "ctx"),
        P(("region", "ctx"), None),
        P(),
        P(),
        P(),
        P(),
    )
    return jax.shard_map(
        per_device, mesh=mesh, in_specs=placed, out_specs=P("region", "ctx", None), check_vma=False
    )
```

```python
import functools
import math

import jax
import jax.numpy as jnp
from jax import lax
from jax.experimental import pallas as pl
from jax.experimental.pallas import tpu as pltpu
from jax.sharding import PartitionSpec as P

HEADS = 16


def layer_modulate(device_tokens, mods, width):
    values = device_tokens.astype(jnp.float32)
    center = jnp.mean(values, axis=1, keepdims=True)
    spread = jnp.mean((values - center) ** 2, axis=1, keepdims=True)
    normed = (values - center) * lax.rsqrt(spread + 1e-06)
    shift = mods[:, :width]
    scale = mods[:, width : 2 * width]
    return (normed * (1.0 + scale) + shift).astype(jnp.bfloat16)


def start_sends(sends, gots, send_sem, recv_sem, local_sem, shards):
    me = lax.axis_index("ctx")
    region = lax.axis_index("region")
    mesh_id = pl.DeviceIdType.MESH
    barrier = pltpu.get_barrier_semaphore()
    for d in range(1, shards):
        peer = lax.rem(me + d, shards)
        pl.semaphore_signal(barrier, 1, device_id=(region, peer), device_id_type=mesh_id)
    pl.semaphore_wait(barrier, shards - 1)
    copies = []
    for a in range(len(sends)):
        local = pltpu.make_async_copy(sends[a].at[me], gots[a].at[me], local_sem.at[a])
        local.start()
        copies.append(local)
    for d in range(1, shards):
        peer = lax.rem(me + d, shards)
        for a in range(len(sends)):
            remote = pltpu.make_async_remote_copy(
                src_ref=sends[a].at[peer],
                dst_ref=gots[a].at[me],
                send_sem=send_sem.at[a, d - 1],
                recv_sem=recv_sem.at[a, d - 1],
                device_id=(region, peer),
                device_id_type=mesh_id,
            )
            remote.start()
            copies.append(remote)
    return copies


def exchange_kernel(*refs, count, shards):
    sends = refs[:count]
    gots = refs[count : 2 * count]
    copies = start_sends(sends, gots, *refs[2 * count :], shards)
    for copy in copies:
        copy.wait()


def send_scratch(count, shards):
    return [
        pltpu.SemaphoreType.DMA((count, shards - 1)),
        pltpu.SemaphoreType.DMA((count, shards - 1)),
        pltpu.SemaphoreType.DMA((count,)),
    ]


def exchange(arrays, shards, collective_id):
    count = len(arrays)
    kernel = functools.partial(exchange_kernel, count=count, shards=shards)
    any_spec = pl.BlockSpec(memory_space=pl.ANY)
    return pl.pallas_call(
        kernel,
        out_shape=[jax.ShapeDtypeStruct(x.shape, x.dtype) for x in arrays],
        in_specs=[any_spec] * count,
        out_specs=[any_spec] * count,
        scratch_shapes=send_scratch(count, shards),
        compiler_params=pltpu.CompilerParams(
            collective_id=collective_id, has_side_effects=True
        ),
    )(*arrays)


def attend_body(qt_ref, k_ref, vt_ref, o_ref, s_scr, inv_root, after_block=None):
    blocks, head_dim, q_rows = qt_ref.shape

    def one_block(b, carry):
        qt = qt_ref[b]

        def score(c, m):
            s = jnp.dot(k_ref[c], qt, preferred_element_type=jnp.float32) * inv_root
            s_scr[c] = s
            return jnp.maximum(m, jnp.max(s, axis=0, keepdims=True))

        m = lax.fori_loop(
            0, blocks, score, jnp.full((1, q_rows), -jnp.inf, jnp.float32), unroll=2
        )

        def accumulate(c, inner):
            total, acc = inner
            expo = jnp.exp(s_scr[c] - m)
            total = total + jnp.sum(expo, axis=0, keepdims=True)
            acc = acc + jnp.dot(
                vt_ref[c], expo.astype(jnp.bfloat16), preferred_element_type=jnp.float32
            )
            return total, acc

        total, acc = lax.fori_loop(
            0,
            blocks,
            accumulate,
            (
                jnp.zeros((1, q_rows), jnp.float32),
                jnp.zeros((head_dim, q_rows), jnp.float32),
            ),
            unroll=2,
        )
        o_ref[b] = (acc / total).astype(o_ref.dtype)
        if after_block is not None:
            after_block(b)
        return carry

    lax.fori_loop(0, blocks, one_block, 0)


def attend_send_kernel(*refs, count, shards, inv_root, stream):
    qt_ref, k_ref, vt_ref = refs[:3]
    sends = refs[3 : 3 + count]
    o_ref = refs[3 + count]
    gots = refs[4 + count : 4 + 2 * count]
    rest = refs[4 + 2 * count :]
    if stream:
        back_ref = rest[0]
        rest = rest[1:]
    s_scr = rest[0]
    copies = start_sends(sends, gots, *rest[1:4], shards)
    after_block = None
    if stream:
        block_send, block_recv, block_local = rest[4:7]
        me = lax.axis_index("ctx")
        region = lax.axis_index("region")

        def remote_block(b):
            return pltpu.make_async_remote_copy(
                src_ref=o_ref.at[b],
                dst_ref=back_ref.at[me],
                send_sem=block_send.at[b],
                recv_sem=block_recv.at[me],
                device_id=(region, b),
                device_id_type=pl.DeviceIdType.MESH,
            )

        def local_block(b):
            return pltpu.make_async_copy(o_ref.at[b], back_ref.at[b], block_local.at[0])

        def after_block(b):
            @pl.when(b == me)
            def _():
                local_block(b).start()

            @pl.when(b != me)
            def _():
                remote_block(b).start()

    attend_body(qt_ref, k_ref, vt_ref, o_ref, s_scr, inv_root, after_block)
    for copy in copies:
        copy.wait()
    if stream:
        for b in range(shards):
            @pl.when(b == me)
            def _():
                local_block(b).wait()

            @pl.when(b != me)
            def _():
                remote_block(b).wait_send()
                pltpu.make_async_remote_copy(
                    src_ref=o_ref.at[b],
                    dst_ref=back_ref.at[b],
                    send_sem=block_send.at[b],
                    recv_sem=block_recv.at[b],
                    device_id=(region, b),
                    device_id_type=pl.DeviceIdType.MESH,
                ).wait_recv()


def attend_send(q_t, k_tok, v_t, sends, shards, inv_root, collective_id, stream=False):
    blocks, head_dim, rows = q_t.shape
    count = len(sends)
    kernel = functools.partial(
        attend_send_kernel, count=count, shards=shards, inv_root=inv_root, stream=stream
    )
    any_spec = pl.BlockSpec(memory_space=pl.ANY)
    vmem_spec = pl.BlockSpec(memory_space=pltpu.VMEM)
    out_shape = [jax.ShapeDtypeStruct(q_t.shape, jnp.bfloat16)]
    out_shape += [jax.ShapeDtypeStruct(x.shape, x.dtype) for x in sends]
    out_specs = [vmem_spec] + [any_spec] * count
    scratch = [pltpu.VMEM((blocks, rows, rows), jnp.float32)] + send_scratch(count, shards)
    if stream:
        out_shape.append(jax.ShapeDtypeStruct(q_t.shape, jnp.bfloat16))
        out_specs.append(any_spec)
        scratch += [
            pltpu.SemaphoreType.DMA((shards,)),
            pltpu.SemaphoreType.DMA((shards,)),
            pltpu.SemaphoreType.DMA((1,)),
        ]
    outs = pl.pallas_call(
        kernel,
        out_shape=out_shape,
        in_specs=[vmem_spec] * 3 + [any_spec] * count,
        out_specs=out_specs,
        scratch_shapes=scratch,
        compiler_params=pltpu.CompilerParams(
            collective_id=collective_id,
            has_side_effects=True,
            vmem_limit_bytes=48 * 1024 * 1024,
        ),
    )(q_t, k_tok, v_t, *sends)
    return outs[0], outs[1:]


def project_kernel(mod_ref, w_ref, act_ref, wg_ref, bg_ref, *refs, shards, pair, head_dim):
    got0 = refs[:3]
    later = refs[3 : 3 * pair]
    gate_ref = refs[3 * pair]
    send0 = refs[3 * pair + 1 : 3 * pair + 4]
    sems = refs[3 * pair + 4 :]
    modulated = mod_ref[...]

    def fill(h, dests):
        for i in range(3):
            out_t = lax.dot_general(
                w_ref[i, h],
                modulated,
                (((1,), (1,)), ((), ())),
                preferred_element_type=jnp.float32,
            )
            for p in range(shards):
                piece = out_t[p * head_dim : (p + 1) * head_dim]
                if i == 1:
                    piece = piece.T
                dests[i][p] = piece.astype(jnp.bfloat16)

    fill(0, send0)
    copies = start_sends(send0, got0, *sems, shards)
    for h in range(1, pair):
        fill(h, later[3 * (h - 1) : 3 * h])
    gate = jnp.dot(act_ref[...], wg_ref[...], preferred_element_type=jnp.float32)
    gate_ref[...] = (gate + bg_ref[...]).astype(gate_ref.dtype)
    for copy in copies:
        copy.wait()


def project_send(modulated, w_t, activated, w_gate, b_gate, shards, pair, head_dim):
    rows, width = modulated.shape
    q_shape = jax.ShapeDtypeStruct((shards, head_dim, rows), jnp.bfloat16)
    k_shape = jax.ShapeDtypeStruct((shards, rows, head_dim), jnp.bfloat16)
    shapes = [q_shape, k_shape, q_shape]
    kernel = functools.partial(
        project_kernel, shards=shards, pair=pair, head_dim=head_dim
    )
    any_spec = pl.BlockSpec(memory_space=pl.ANY)
    vmem_spec = pl.BlockSpec(memory_space=pltpu.VMEM)
    outs = pl.pallas_call(
        kernel,
        out_shape=shapes * pair
        + [jax.ShapeDtypeStruct((rows, w_gate.shape[1]), jnp.bfloat16)],
        in_specs=[vmem_spec] * 5,
        out_specs=[any_spec] * 3 + [vmem_spec] * (3 * (pair - 1) + 1),
        scratch_shapes=[pltpu.VMEM(x.shape, x.dtype) for x in shapes]
        + send_scratch(3, shards),
        compiler_params=pltpu.CompilerParams(
            collective_id=pair + 1,
            has_side_effects=True,
            vmem_limit_bytes=48 * 1024 * 1024,
        ),
    )(modulated, w_t, activated, w_gate, b_gate)
    return outs[:3], [outs[3 * h : 3 * h + 3] for h in range(1, pair)], outs[3 * pair]


def head_pipeline(modulated, w_t, gate_parts, shards, pair, head_dim, inverse_root):
    got, later, gate = project_send(modulated, w_t, *gate_parts, shards, pair, head_dim)
    backs = []
    for h in range(pair):
        last = h + 1 == pair
        sends = [] if last else list(later[h])
        if h > 0:
            sends = sends + [out_prev]
        out_prev, sent = attend_send(
            *got, sends, shards, inverse_root, 1 + h, stream=last
        )
        if not last:
            got = sent[:3]
            sent = sent[3:]
        backs.extend(sent)
    return jnp.stack(backs, axis=1), gate


def per_device(
    tokens, element_ids, element_slot, live_count, cond_table, w_ada, b_ada, w_qkv, w_out
):
    device_tokens = tokens[0]
    tok_rows, width = device_tokens.shape
    owners = lax.axis_size(("region", "ctx"))
    shards = lax.axis_size("ctx")
    elem_rows = cond_table.shape[0]
    capacity = -(-max(2, 3 * tok_rows // (2 * owners)) // 8) * 8
    slots = element_slot[element_ids[0]]
    owner_index = slots // elem_rows
    local_row = slots % elem_rows
    position = jnp.arange(tok_rows, dtype=jnp.int32)
    solid = position < live_count[0, 0]
    earlier = (
        (owner_index[:, None] == owner_index[None, :])
        & (position[None, :] < position[:, None])
        & solid[None, :]
    )
    place_rank = jnp.sum(earlier.astype(jnp.int32), axis=1)
    target = jnp.where(solid, owner_index * capacity + place_rank, owners * capacity)
    requests = jnp.zeros((owners * capacity,), jnp.int32).at[target].set(local_row, mode="drop")
    asked = lax.all_to_all(
        requests.reshape(owners, capacity),
        ("region", "ctx"),
        split_axis=0,
        concat_axis=0,
        tiled=True,
    ).reshape(-1)
    pick_at = jnp.minimum(target, owners * capacity - 1)
    served_hot = (asked[:, None] == jnp.arange(elem_rows, dtype=jnp.int32)[None, :]).astype(
        jnp.bfloat16
    )
    served = (
        jnp.dot(served_hot, cond_table, preferred_element_type=jnp.float32)
        .astype(jnp.bfloat16)
        .reshape(owners, capacity, width)
    )
    replies = lax.all_to_all(served, ("region", "ctx"), split_axis=0, concat_axis=0, tiled=True)
    pick_hot = (
        pick_at[:, None] == jnp.arange(owners * capacity, dtype=jnp.int32)[None, :]
    ).astype(jnp.bfloat16)
    picked = jnp.dot(
        pick_hot, replies.reshape(owners * capacity, width), preferred_element_type=jnp.float32
    )
    activated = jnp.where(solid[:, None], jax.nn.silu(picked.astype(jnp.float32)), 0.0).astype(
        jnp.bfloat16
    )
    mods = (
        jnp.dot(activated, w_ada[:, : 2 * width], preferred_element_type=jnp.float32)
        + b_ada[: 2 * width]
    ).astype(jnp.bfloat16)
    mods = mods.astype(jnp.float32)
    gate_parts = (activated, w_ada[:, 2 * width :], b_ada[None, 2 * width :])
    modulated = layer_modulate(device_tokens, mods, width)

    head_dim = width // HEADS
    pair = HEADS // shards
    inverse_root = 1.0 / math.sqrt(head_dim)
    w_t = (
        w_qkv.reshape(width, 3, shards, pair, head_dim)
        .transpose(1, 3, 2, 4, 0)
        .reshape(3, pair, shards * head_dim, width)
    )
    backs, gate = head_pipeline(
        modulated, w_t, gate_parts, shards, pair, head_dim, inverse_root
    )
    w_out_parts = w_out.reshape(shards, pair, head_dim, width)
    projected = jnp.einsum(
        "phet,pheD->tD",
        backs,
        w_out_parts,
        preferred_element_type=jnp.float32,
    )
    gate = gate.astype(jnp.float32)
    output = (device_tokens.astype(jnp.float32) + gate * projected).astype(jnp.bfloat16)
    return output[None]


def solution(mesh):
    placed = (
        P("region", "ctx", None),
        P("region", "ctx"),
        P(),
        P("region", "ctx"),
        P(("region", "ctx"), None),
        P(),
        P(),
        P(),
        P(),
    )
    return jax.shard_map(
        per_device, mesh=mesh, in_specs=placed, out_specs=P("region", "ctx", None), check_vma=False
    )
```

```python
import functools
import math

import jax
import jax.numpy as jnp
from jax import lax
from jax.experimental import pallas as pl
from jax.experimental.pallas import tpu as pltpu
from jax.sharding import PartitionSpec as P

HEADS = 16


def layer_modulate(device_tokens, mods, width):
    values = device_tokens.astype(jnp.float32)
    center = jnp.mean(values, axis=1, keepdims=True)
    spread = jnp.mean((values - center) ** 2, axis=1, keepdims=True)
    normed = (values - center) * lax.rsqrt(spread + 1e-06)
    shift = mods[:, :width]
    scale = mods[:, width : 2 * width]
    return (normed * (1.0 + scale) + shift).astype(jnp.bfloat16)


def start_sends(sends, gots, send_sem, recv_sem, local_sem, shards):
    me = lax.axis_index("ctx")
    region = lax.axis_index("region")
    mesh_id = pl.DeviceIdType.MESH
    barrier = pltpu.get_barrier_semaphore()
    for d in range(1, shards):
        peer = lax.rem(me + d, shards)
        pl.semaphore_signal(barrier, 1, device_id=(region, peer), device_id_type=mesh_id)
    pl.semaphore_wait(barrier, shards - 1)
    copies = []
    for a in range(len(sends)):
        local = pltpu.make_async_copy(sends[a].at[me], gots[a].at[me], local_sem.at[a])
        local.start()
        copies.append(local)
    for d in range(1, shards):
        peer = lax.rem(me + d, shards)
        for a in range(len(sends)):
            remote = pltpu.make_async_remote_copy(
                src_ref=sends[a].at[peer],
                dst_ref=gots[a].at[me],
                send_sem=send_sem.at[a, d - 1],
                recv_sem=recv_sem.at[a, d - 1],
                device_id=(region, peer),
                device_id_type=mesh_id,
            )
            remote.start()
            copies.append(remote)
    return copies


def exchange_kernel(*refs, count, shards):
    sends = refs[:count]
    gots = refs[count : 2 * count]
    copies = start_sends(sends, gots, *refs[2 * count :], shards)
    for copy in copies:
        copy.wait()


def send_scratch(count, shards):
    return [
        pltpu.SemaphoreType.DMA((count, shards - 1)),
        pltpu.SemaphoreType.DMA((count, shards - 1)),
        pltpu.SemaphoreType.DMA((count,)),
    ]


def exchange(arrays, shards, collective_id):
    count = len(arrays)
    kernel = functools.partial(exchange_kernel, count=count, shards=shards)
    any_spec = pl.BlockSpec(memory_space=pl.ANY)
    return pl.pallas_call(
        kernel,
        out_shape=[jax.ShapeDtypeStruct(x.shape, x.dtype) for x in arrays],
        in_specs=[any_spec] * count,
        out_specs=[any_spec] * count,
        scratch_shapes=send_scratch(count, shards),
        compiler_params=pltpu.CompilerParams(
            collective_id=collective_id, has_side_effects=True
        ),
    )(*arrays)


def attend_body(qt_ref, kt_ref, vt_ref, o_ref, s_scr, k_ref, inv_root, after_block=None):
    blocks, head_dim, q_rows = qt_ref.shape
    for c in range(blocks):
        k_ref[c] = kt_ref[c].astype(jnp.float32).T.astype(k_ref.dtype)

    def one_block(b, carry):
        qt = qt_ref[b]

        def score(c, m):
            s = jnp.dot(k_ref[c], qt, preferred_element_type=jnp.float32) * inv_root
            s_scr[c] = s
            return jnp.maximum(m, jnp.max(s, axis=0, keepdims=True))

        m = lax.fori_loop(
            0, blocks, score, jnp.full((1, q_rows), -jnp.inf, jnp.float32), unroll=2
        )

        def accumulate(c, inner):
            total, acc = inner
            expo = jnp.exp(s_scr[c] - m)
            total = total + jnp.sum(expo, axis=0, keepdims=True)
            acc = acc + jnp.dot(
                vt_ref[c], expo.astype(jnp.bfloat16), preferred_element_type=jnp.float32
            )
            return total, acc

        total, acc = lax.fori_loop(
            0,
            blocks,
            accumulate,
            (
                jnp.zeros((1, q_rows), jnp.float32),
                jnp.zeros((head_dim, q_rows), jnp.float32),
            ),
            unroll=2,
        )
        o_ref[b] = (acc / total).astype(o_ref.dtype)
        if after_block is not None:
            after_block(b)
        return carry

    lax.fori_loop(0, blocks, one_block, 0)


def attend_send_kernel(*refs, count, shards, inv_root, stream):
    qt_ref, k_ref, vt_ref = refs[:3]
    sends = refs[3 : 3 + count]
    o_ref = refs[3 + count]
    gots = refs[4 + count : 4 + 2 * count]
    rest = refs[4 + 2 * count :]
    if stream:
        back_ref = rest[0]
        rest = rest[1:]
    s_scr, k_scr = rest[0], rest[1]
    rest = rest[1:]
    copies = start_sends(sends, gots, *rest[1:4], shards)
    after_block = None
    if stream:
        block_send, block_recv, block_local = rest[4:7]
        me = lax.axis_index("ctx")
        region = lax.axis_index("region")

        def remote_block(b):
            return pltpu.make_async_remote_copy(
                src_ref=o_ref.at[b],
                dst_ref=back_ref.at[me],
                send_sem=block_send.at[b],
                recv_sem=block_recv.at[me],
                device_id=(region, b),
                device_id_type=pl.DeviceIdType.MESH,
            )

        def local_block(b):
            return pltpu.make_async_copy(o_ref.at[b], back_ref.at[b], block_local.at[0])

        def after_block(b):
            @pl.when(b == me)
            def _():
                local_block(b).start()

            @pl.when(b != me)
            def _():
                remote_block(b).start()

    attend_body(qt_ref, k_ref, vt_ref, o_ref, s_scr, k_scr, inv_root, after_block)
    for copy in copies:
        copy.wait()
    if stream:
        for b in range(shards):
            @pl.when(b == me)
            def _():
                local_block(b).wait()

            @pl.when(b != me)
            def _():
                remote_block(b).wait_send()
                pltpu.make_async_remote_copy(
                    src_ref=o_ref.at[b],
                    dst_ref=back_ref.at[b],
                    send_sem=block_send.at[b],
                    recv_sem=block_recv.at[b],
                    device_id=(region, b),
                    device_id_type=pl.DeviceIdType.MESH,
                ).wait_recv()


def attend_send(q_t, k_tok, v_t, sends, shards, inv_root, collective_id, stream=False):
    blocks, head_dim, rows = q_t.shape
    count = len(sends)
    kernel = functools.partial(
        attend_send_kernel, count=count, shards=shards, inv_root=inv_root, stream=stream
    )
    any_spec = pl.BlockSpec(memory_space=pl.ANY)
    vmem_spec = pl.BlockSpec(memory_space=pltpu.VMEM)
    out_shape = [jax.ShapeDtypeStruct(q_t.shape, jnp.bfloat16)]
    out_shape += [jax.ShapeDtypeStruct(x.shape, x.dtype) for x in sends]
    out_specs = [vmem_spec] + [any_spec] * count
    scratch = [
        pltpu.VMEM((blocks, rows, rows), jnp.float32),
        pltpu.VMEM((blocks, rows, head_dim), jnp.bfloat16),
    ] + send_scratch(count, shards)
    if stream:
        out_shape.append(jax.ShapeDtypeStruct(q_t.shape, jnp.bfloat16))
        out_specs.append(any_spec)
        scratch += [
            pltpu.SemaphoreType.DMA((shards,)),
            pltpu.SemaphoreType.DMA((shards,)),
            pltpu.SemaphoreType.DMA((1,)),
        ]
    outs = pl.pallas_call(
        kernel,
        out_shape=out_shape,
        in_specs=[vmem_spec] * 3 + [any_spec] * count,
        out_specs=out_specs,
        scratch_shapes=scratch,
        compiler_params=pltpu.CompilerParams(
            collective_id=collective_id,
            has_side_effects=True,
            vmem_limit_bytes=48 * 1024 * 1024,
        ),
    )(q_t, k_tok, v_t, *sends)
    return outs[0], outs[1:]


def project_kernel(mod_ref, w_ref, act_ref, wg_ref, bg_ref, *refs, shards, pair, head_dim):
    got0 = refs[:3]
    later = refs[3 : 3 * pair]
    gate_ref = refs[3 * pair]
    send0 = refs[3 * pair + 1 : 3 * pair + 4]
    sems = refs[3 * pair + 4 :]
    modulated = mod_ref[...]

    def fill(h, dests):
        for i in range(3):
            out_t = lax.dot_general(
                w_ref[i, h],
                modulated,
                (((1,), (1,)), ((), ())),
                preferred_element_type=jnp.float32,
            )
            for p in range(shards):
                piece = out_t[p * head_dim : (p + 1) * head_dim]
                dests[i][p] = piece.astype(jnp.bfloat16)

    fill(0, send0)
    copies = start_sends(send0, got0, *sems, shards)
    for h in range(1, pair):
        fill(h, later[3 * (h - 1) : 3 * h])
    gate = jnp.dot(act_ref[...], wg_ref[...], preferred_element_type=jnp.float32)
    gate_ref[...] = (gate + bg_ref[...]).astype(gate_ref.dtype)
    for copy in copies:
        copy.wait()


def project_send(modulated, w_t, activated, w_gate, b_gate, shards, pair, head_dim):
    rows, width = modulated.shape
    q_shape = jax.ShapeDtypeStruct((shards, head_dim, rows), jnp.bfloat16)
    shapes = [q_shape, q_shape, q_shape]
    kernel = functools.partial(
        project_kernel, shards=shards, pair=pair, head_dim=head_dim
    )
    any_spec = pl.BlockSpec(memory_space=pl.ANY)
    vmem_spec = pl.BlockSpec(memory_space=pltpu.VMEM)
    outs = pl.pallas_call(
        kernel,
        out_shape=shapes * pair
        + [jax.ShapeDtypeStruct((rows, w_gate.shape[1]), jnp.bfloat16)],
        in_specs=[vmem_spec] * 5,
        out_specs=[any_spec] * 3 + [vmem_spec] * (3 * (pair - 1) + 1),
        scratch_shapes=[pltpu.VMEM(x.shape, x.dtype) for x in shapes]
        + send_scratch(3, shards),
        compiler_params=pltpu.CompilerParams(
            collective_id=pair + 1,
            has_side_effects=True,
            vmem_limit_bytes=48 * 1024 * 1024,
        ),
    )(modulated, w_t, activated, w_gate, b_gate)
    return outs[:3], [outs[3 * h : 3 * h + 3] for h in range(1, pair)], outs[3 * pair]


def head_pipeline(modulated, w_t, gate_parts, shards, pair, head_dim, inverse_root):
    got, later, gate = project_send(modulated, w_t, *gate_parts, shards, pair, head_dim)
    backs = []
    for h in range(pair):
        last = h + 1 == pair
        sends = [] if last else list(later[h])
        if h > 0:
            sends = sends + [out_prev]
        out_prev, sent = attend_send(
            *got, sends, shards, inverse_root, 1 + h, stream=last
        )
        if not last:
            got = sent[:3]
            sent = sent[3:]
        backs.extend(sent)
    return jnp.stack(backs, axis=1), gate


def per_device(
    tokens, element_ids, element_slot, live_count, cond_table, w_ada, b_ada, w_qkv, w_out
):
    device_tokens = tokens[0]
    tok_rows, width = device_tokens.shape
    owners = lax.axis_size(("region", "ctx"))
    shards = lax.axis_size("ctx")
    elem_rows = cond_table.shape[0]
    capacity = -(-max(2, 3 * tok_rows // (2 * owners)) // 8) * 8
    slots = element_slot[element_ids[0]]
    owner_index = slots // elem_rows
    local_row = slots % elem_rows
    position = jnp.arange(tok_rows, dtype=jnp.int32)
    solid = position < live_count[0, 0]
    earlier = (
        (owner_index[:, None] == owner_index[None, :])
        & (position[None, :] < position[:, None])
        & solid[None, :]
    )
    place_rank = jnp.sum(earlier.astype(jnp.int32), axis=1)
    target = jnp.where(solid, owner_index * capacity + place_rank, owners * capacity)
    requests = jnp.zeros((owners * capacity,), jnp.int32).at[target].set(local_row, mode="drop")
    asked = lax.all_to_all(
        requests.reshape(owners, capacity),
        ("region", "ctx"),
        split_axis=0,
        concat_axis=0,
        tiled=True,
    ).reshape(-1)
    pick_at = jnp.minimum(target, owners * capacity - 1)
    served_hot = (asked[:, None] == jnp.arange(elem_rows, dtype=jnp.int32)[None, :]).astype(
        jnp.bfloat16
    )
    served = (
        jnp.dot(served_hot, cond_table, preferred_element_type=jnp.float32)
        .astype(jnp.bfloat16)
        .reshape(owners, capacity, width)
    )
    replies = lax.all_to_all(served, ("region", "ctx"), split_axis=0, concat_axis=0, tiled=True)
    pick_hot = (
        pick_at[:, None] == jnp.arange(owners * capacity, dtype=jnp.int32)[None, :]
    ).astype(jnp.bfloat16)
    picked = jnp.dot(
        pick_hot, replies.reshape(owners * capacity, width), preferred_element_type=jnp.float32
    )
    activated = jnp.where(solid[:, None], jax.nn.silu(picked.astype(jnp.float32)), 0.0).astype(
        jnp.bfloat16
    )
    mods = (
        jnp.dot(activated, w_ada[:, : 2 * width], preferred_element_type=jnp.float32)
        + b_ada[: 2 * width]
    ).astype(jnp.bfloat16)
    mods = mods.astype(jnp.float32)
    gate_parts = (activated, w_ada[:, 2 * width :], b_ada[None, 2 * width :])
    modulated = layer_modulate(device_tokens, mods, width)

    head_dim = width // HEADS
    pair = HEADS // shards
    inverse_root = 1.0 / math.sqrt(head_dim)
    w_t = (
        w_qkv.reshape(width, 3, shards, pair, head_dim)
        .transpose(1, 3, 2, 4, 0)
        .reshape(3, pair, shards * head_dim, width)
    )
    backs, gate = head_pipeline(
        modulated, w_t, gate_parts, shards, pair, head_dim, inverse_root
    )
    w_out_parts = w_out.reshape(shards, pair, head_dim, width)
    projected = jnp.einsum(
        "phet,pheD->tD",
        backs,
        w_out_parts,
        preferred_element_type=jnp.float32,
    )
    gate = gate.astype(jnp.float32)
    output = (device_tokens.astype(jnp.float32) + gate * projected).astype(jnp.bfloat16)
    return output[None]


def solution(mesh):
    placed = (
        P("region", "ctx", None),
        P("region", "ctx"),
        P(),
        P("region", "ctx"),
        P(("region", "ctx"), None),
        P(),
        P(),
        P(),
        P(),
    )
    return jax.shard_map(
        per_device, mesh=mesh, in_specs=placed, out_specs=P("region", "ctx", None), check_vma=False
    )
```

```python
import functools
import math

import jax
import jax.numpy as jnp
from jax import lax
from jax.experimental import pallas as pl
from jax.experimental.pallas import tpu as pltpu
from jax.sharding import PartitionSpec as P

HEADS = 16


def layer_modulate(device_tokens, mods, width):
    values = device_tokens.astype(jnp.float32)
    center = jnp.mean(values, axis=1, keepdims=True)
    spread = jnp.mean((values - center) ** 2, axis=1, keepdims=True)
    normed = (values - center) * lax.rsqrt(spread + 1e-06)
    shift = mods[:, :width]
    scale = mods[:, width : 2 * width]
    return (normed * (1.0 + scale) + shift).astype(jnp.bfloat16)


def enter(shards):
    me = lax.axis_index("ctx")
    region = lax.axis_index("region")
    barrier = pltpu.get_barrier_semaphore()
    for d in range(1, shards):
        peer = lax.rem(me + d, shards)
        pl.semaphore_signal(
            barrier, 1, device_id=(region, peer), device_id_type=pl.DeviceIdType.MESH
        )
    pl.semaphore_wait(barrier, shards - 1)


def start_array(a, send, got, send_sem, recv_sem, local_sem, shards):
    me = lax.axis_index("ctx")
    region = lax.axis_index("region")
    local = pltpu.make_async_copy(send.at[me], got.at[me], local_sem.at[a])
    local.start()
    copies = [local]
    for d in range(1, shards):
        peer = lax.rem(me + d, shards)
        remote = pltpu.make_async_remote_copy(
            src_ref=send.at[peer],
            dst_ref=got.at[me],
            send_sem=send_sem.at[a, d - 1],
            recv_sem=recv_sem.at[a, d - 1],
            device_id=(region, peer),
            device_id_type=pl.DeviceIdType.MESH,
        )
        remote.start()
        copies.append(remote)
    return copies


def start_sends(sends, gots, send_sem, recv_sem, local_sem, shards):
    enter(shards)
    copies = []
    for a in range(len(sends)):
        copies += start_array(a, sends[a], gots[a], send_sem, recv_sem, local_sem, shards)
    return copies


def exchange_kernel(*refs, count, shards):
    sends = refs[:count]
    gots = refs[count : 2 * count]
    copies = start_sends(sends, gots, *refs[2 * count :], shards)
    for copy in copies:
        copy.wait()


def send_scratch(count, shards):
    return [
        pltpu.SemaphoreType.DMA((count, shards - 1)),
        pltpu.SemaphoreType.DMA((count, shards - 1)),
        pltpu.SemaphoreType.DMA((count,)),
    ]


def exchange(arrays, shards, collective_id):
    count = len(arrays)
    kernel = functools.partial(exchange_kernel, count=count, shards=shards)
    any_spec = pl.BlockSpec(memory_space=pl.ANY)
    return pl.pallas_call(
        kernel,
        out_shape=[jax.ShapeDtypeStruct(x.shape, x.dtype) for x in arrays],
        in_specs=[any_spec] * count,
        out_specs=[any_spec] * count,
        scratch_shapes=send_scratch(count, shards),
        compiler_params=pltpu.CompilerParams(
            collective_id=collective_id, has_side_effects=True
        ),
    )(*arrays)


def attend_body(qt_ref, kt_ref, vt_ref, o_ref, s_scr, k_ref, inv_root, after_block=None):
    blocks, head_dim, q_rows = qt_ref.shape
    for c in range(blocks):
        k_ref[c] = kt_ref[c].astype(jnp.float32).T.astype(k_ref.dtype)

    def one_block(b, carry):
        qt = qt_ref[b]

        def score(c, m):
            s = jnp.dot(k_ref[c], qt, preferred_element_type=jnp.float32) * inv_root
            s_scr[c] = s
            return jnp.maximum(m, jnp.max(s, axis=0, keepdims=True))

        m = lax.fori_loop(
            0, blocks, score, jnp.full((1, q_rows), -jnp.inf, jnp.float32), unroll=2
        )

        def accumulate(c, inner):
            total, acc = inner
            expo = jnp.exp(s_scr[c] - m)
            total = total + jnp.sum(expo, axis=0, keepdims=True)
            acc = acc + jnp.dot(
                vt_ref[c], expo.astype(jnp.bfloat16), preferred_element_type=jnp.float32
            )
            return total, acc

        total, acc = lax.fori_loop(
            0,
            blocks,
            accumulate,
            (
                jnp.zeros((1, q_rows), jnp.float32),
                jnp.zeros((head_dim, q_rows), jnp.float32),
            ),
            unroll=2,
        )
        o_ref[b] = (acc / total).astype(o_ref.dtype)
        if after_block is not None:
            after_block(b)
        return carry

    lax.fori_loop(0, blocks, one_block, 0)


def attend_send_kernel(*refs, count, shards, inv_root, stream):
    qt_ref, k_ref, vt_ref = refs[:3]
    sends = refs[3 : 3 + count]
    o_ref = refs[3 + count]
    gots = refs[4 + count : 4 + 2 * count]
    rest = refs[4 + 2 * count :]
    if stream:
        back_ref = rest[0]
        rest = rest[1:]
    s_scr, k_scr = rest[0], rest[1]
    rest = rest[1:]
    copies = start_sends(sends, gots, *rest[1:4], shards)
    after_block = None
    if stream:
        block_send, block_recv, block_local = rest[4:7]
        me = lax.axis_index("ctx")
        region = lax.axis_index("region")

        def remote_block(b):
            return pltpu.make_async_remote_copy(
                src_ref=o_ref.at[b],
                dst_ref=back_ref.at[me],
                send_sem=block_send.at[b],
                recv_sem=block_recv.at[me],
                device_id=(region, b),
                device_id_type=pl.DeviceIdType.MESH,
            )

        def local_block(b):
            return pltpu.make_async_copy(o_ref.at[b], back_ref.at[b], block_local.at[0])

        def after_block(b):
            @pl.when(b == me)
            def _():
                local_block(b).start()

            @pl.when(b != me)
            def _():
                remote_block(b).start()

    attend_body(qt_ref, k_ref, vt_ref, o_ref, s_scr, k_scr, inv_root, after_block)
    for copy in copies:
        copy.wait()
    if stream:
        for b in range(shards):
            @pl.when(b == me)
            def _():
                local_block(b).wait()

            @pl.when(b != me)
            def _():
                remote_block(b).wait_send()
                pltpu.make_async_remote_copy(
                    src_ref=o_ref.at[b],
                    dst_ref=back_ref.at[b],
                    send_sem=block_send.at[b],
                    recv_sem=block_recv.at[b],
                    device_id=(region, b),
                    device_id_type=pl.DeviceIdType.MESH,
                ).wait_recv()


def attend_send(q_t, k_tok, v_t, sends, shards, inv_root, collective_id, stream=False):
    blocks, head_dim, rows = q_t.shape
    count = len(sends)
    kernel = functools.partial(
        attend_send_kernel, count=count, shards=shards, inv_root=inv_root, stream=stream
    )
    any_spec = pl.BlockSpec(memory_space=pl.ANY)
    vmem_spec = pl.BlockSpec(memory_space=pltpu.VMEM)
    out_shape = [jax.ShapeDtypeStruct(q_t.shape, jnp.bfloat16)]
    out_shape += [jax.ShapeDtypeStruct(x.shape, x.dtype) for x in sends]
    out_specs = [vmem_spec] + [any_spec] * count
    scratch = [
        pltpu.VMEM((blocks, rows, rows), jnp.float32),
        pltpu.VMEM((blocks, rows, head_dim), jnp.bfloat16),
    ] + send_scratch(count, shards)
    if stream:
        out_shape.append(jax.ShapeDtypeStruct(q_t.shape, jnp.bfloat16))
        out_specs.append(any_spec)
        scratch += [
            pltpu.SemaphoreType.DMA((shards,)),
            pltpu.SemaphoreType.DMA((shards,)),
            pltpu.SemaphoreType.DMA((1,)),
        ]
    outs = pl.pallas_call(
        kernel,
        out_shape=out_shape,
        in_specs=[vmem_spec] * 3 + [any_spec] * count,
        out_specs=out_specs,
        scratch_shapes=scratch,
        compiler_params=pltpu.CompilerParams(
            collective_id=collective_id,
            has_side_effects=True,
            vmem_limit_bytes=48 * 1024 * 1024,
        ),
    )(q_t, k_tok, v_t, *sends)
    return outs[0], outs[1:]


def project_kernel(mod_ref, w_ref, act_ref, wg_ref, bg_ref, *refs, shards, pair, head_dim):
    got0 = refs[:3]
    later = refs[3 : 3 * pair]
    gate_ref = refs[3 * pair]
    send0 = refs[3 * pair + 1 : 3 * pair + 4]
    sems = refs[3 * pair + 4 :]
    modulated = mod_ref[...]

    def fill(h, dests, i):
        out_t = lax.dot_general(
            w_ref[i, h],
            modulated,
            (((1,), (1,)), ((), ())),
            preferred_element_type=jnp.float32,
        )
        for p in range(shards):
            piece = out_t[p * head_dim : (p + 1) * head_dim]
            dests[i][p] = piece.astype(jnp.bfloat16)

    enter(shards)
    copies = []
    for i in range(3):
        fill(0, send0, i)
        copies += start_array(i, send0[i], got0[i], *sems, shards)
    for h in range(1, pair):
        for i in range(3):
            fill(h, later[3 * (h - 1) : 3 * h], i)
    gate = jnp.dot(act_ref[...], wg_ref[...], preferred_element_type=jnp.float32)
    gate_ref[...] = (gate + bg_ref[...]).astype(gate_ref.dtype)
    for copy in copies:
        copy.wait()


def project_send(modulated, w_t, activated, w_gate, b_gate, shards, pair, head_dim):
    rows, width = modulated.shape
    q_shape = jax.ShapeDtypeStruct((shards, head_dim, rows), jnp.bfloat16)
    shapes = [q_shape, q_shape, q_shape]
    kernel = functools.partial(
        project_kernel, shards=shards, pair=pair, head_dim=head_dim
    )
    any_spec = pl.BlockSpec(memory_space=pl.ANY)
    vmem_spec = pl.BlockSpec(memory_space=pltpu.VMEM)
    outs = pl.pallas_call(
        kernel,
        out_shape=shapes * pair
        + [jax.ShapeDtypeStruct((rows, w_gate.shape[1]), jnp.bfloat16)],
        in_specs=[vmem_spec] * 5,
        out_specs=[any_spec] * 3 + [vmem_spec] * (3 * (pair - 1) + 1),
        scratch_shapes=[pltpu.VMEM(x.shape, x.dtype) for x in shapes]
        + send_scratch(3, shards),
        compiler_params=pltpu.CompilerParams(
            collective_id=pair + 1,
            has_side_effects=True,
            vmem_limit_bytes=48 * 1024 * 1024,
        ),
    )(modulated, w_t, activated, w_gate, b_gate)
    return outs[:3], [outs[3 * h : 3 * h + 3] for h in range(1, pair)], outs[3 * pair]


def head_pipeline(modulated, w_t, gate_parts, shards, pair, head_dim, inverse_root):
    got, later, gate = project_send(modulated, w_t, *gate_parts, shards, pair, head_dim)
    backs = []
    for h in range(pair):
        last = h + 1 == pair
        sends = [] if last else list(later[h])
        if h > 0:
            sends = sends + [out_prev]
        out_prev, sent = attend_send(
            *got, sends, shards, inverse_root, 1 + h, stream=last
        )
        if not last:
            got = sent[:3]
            sent = sent[3:]
        backs.extend(sent)
    return jnp.stack(backs, axis=1), gate


def per_device(
    tokens, element_ids, element_slot, live_count, cond_table, w_ada, b_ada, w_qkv, w_out
):
    device_tokens = tokens[0]
    tok_rows, width = device_tokens.shape
    owners = lax.axis_size(("region", "ctx"))
    shards = lax.axis_size("ctx")
    elem_rows = cond_table.shape[0]
    capacity = -(-max(2, 3 * tok_rows // (2 * owners)) // 8) * 8
    slots = element_slot[element_ids[0]]
    owner_index = slots // elem_rows
    local_row = slots % elem_rows
    position = jnp.arange(tok_rows, dtype=jnp.int32)
    solid = position < live_count[0, 0]
    earlier = (
        (owner_index[:, None] == owner_index[None, :])
        & (position[None, :] < position[:, None])
        & solid[None, :]
    )
    place_rank = jnp.sum(earlier.astype(jnp.int32), axis=1)
    target = jnp.where(solid, owner_index * capacity + place_rank, owners * capacity)
    requests = jnp.zeros((owners * capacity,), jnp.int32).at[target].set(local_row, mode="drop")
    asked = lax.all_to_all(
        requests.reshape(owners, capacity),
        ("region", "ctx"),
        split_axis=0,
        concat_axis=0,
        tiled=True,
    ).reshape(-1)
    pick_at = jnp.minimum(target, owners * capacity - 1)
    served_hot = (asked[:, None] == jnp.arange(elem_rows, dtype=jnp.int32)[None, :]).astype(
        jnp.bfloat16
    )
    served = (
        jnp.dot(served_hot, cond_table, preferred_element_type=jnp.float32)
        .astype(jnp.bfloat16)
        .reshape(owners, capacity, width)
    )
    replies = lax.all_to_all(served, ("region", "ctx"), split_axis=0, concat_axis=0, tiled=True)
    pick_hot = (
        pick_at[:, None] == jnp.arange(owners * capacity, dtype=jnp.int32)[None, :]
    ).astype(jnp.bfloat16)
    picked = jnp.dot(
        pick_hot, replies.reshape(owners * capacity, width), preferred_element_type=jnp.float32
    )
    activated = jnp.where(solid[:, None], jax.nn.silu(picked.astype(jnp.float32)), 0.0).astype(
        jnp.bfloat16
    )
    mods = (
        jnp.dot(activated, w_ada[:, : 2 * width], preferred_element_type=jnp.float32)
        + b_ada[: 2 * width]
    ).astype(jnp.bfloat16)
    mods = mods.astype(jnp.float32)
    gate_parts = (activated, w_ada[:, 2 * width :], b_ada[None, 2 * width :])
    modulated = layer_modulate(device_tokens, mods, width)

    head_dim = width // HEADS
    pair = HEADS // shards
    inverse_root = 1.0 / math.sqrt(head_dim)
    w_t = (
        w_qkv.reshape(width, 3, shards, pair, head_dim)
        .transpose(1, 3, 2, 4, 0)
        .reshape(3, pair, shards * head_dim, width)
    )
    backs, gate = head_pipeline(
        modulated, w_t, gate_parts, shards, pair, head_dim, inverse_root
    )
    w_out_parts = w_out.reshape(shards, pair, head_dim, width)
    projected = jnp.einsum(
        "phet,pheD->tD",
        backs,
        w_out_parts,
        preferred_element_type=jnp.float32,
    )
    gate = gate.astype(jnp.float32)
    output = (device_tokens.astype(jnp.float32) + gate * projected).astype(jnp.bfloat16)
    return output[None]


def solution(mesh):
    placed = (
        P("region", "ctx", None),
        P("region", "ctx"),
        P(),
        P("region", "ctx"),
        P(("region", "ctx"), None),
        P(),
        P(),
        P(),
        P(),
    )
    return jax.shard_map(
        per_device, mesh=mesh, in_specs=placed, out_specs=P("region", "ctx", None), check_vma=False
    )
```

```python
import functools
import math

import jax
import jax.numpy as jnp
from jax import lax
from jax.experimental import pallas as pl
from jax.experimental.pallas import tpu as pltpu
from jax.sharding import PartitionSpec as P

HEADS = 16


def layer_modulate(device_tokens, mods, width):
    values = device_tokens.astype(jnp.float32)
    center = jnp.mean(values, axis=1, keepdims=True)
    spread = jnp.mean((values - center) ** 2, axis=1, keepdims=True)
    normed = (values - center) * lax.rsqrt(spread + 1e-06)
    shift = mods[:, :width]
    scale = mods[:, width : 2 * width]
    return (normed * (1.0 + scale) + shift).astype(jnp.bfloat16)


def enter(shards):
    me = lax.axis_index("ctx")
    region = lax.axis_index("region")
    barrier = pltpu.get_barrier_semaphore()
    for d in range(1, shards):
        peer = lax.rem(me + d, shards)
        pl.semaphore_signal(
            barrier, 1, device_id=(region, peer), device_id_type=pl.DeviceIdType.MESH
        )
    pl.semaphore_wait(barrier, shards - 1)


def start_array(a, send, got, send_sem, recv_sem, local_sem, shards):
    me = lax.axis_index("ctx")
    region = lax.axis_index("region")
    local = pltpu.make_async_copy(send.at[me], got.at[me], local_sem.at[a])
    local.start()
    copies = [local]
    for d in range(1, shards):
        peer = lax.rem(me + d, shards)
        remote = pltpu.make_async_remote_copy(
            src_ref=send.at[peer],
            dst_ref=got.at[me],
            send_sem=send_sem.at[a, d - 1],
            recv_sem=recv_sem.at[a, d - 1],
            device_id=(region, peer),
            device_id_type=pl.DeviceIdType.MESH,
        )
        remote.start()
        copies.append(remote)
    return copies


def start_sends(sends, gots, send_sem, recv_sem, local_sem, shards):
    enter(shards)
    copies = []
    for a in range(len(sends)):
        copies += start_array(a, sends[a], gots[a], send_sem, recv_sem, local_sem, shards)
    return copies


def exchange_kernel(*refs, count, shards):
    sends = refs[:count]
    gots = refs[count : 2 * count]
    copies = start_sends(sends, gots, *refs[2 * count :], shards)
    for copy in copies:
        copy.wait()


def send_scratch(count, shards):
    return [
        pltpu.SemaphoreType.DMA((count, shards - 1)),
        pltpu.SemaphoreType.DMA((count, shards - 1)),
        pltpu.SemaphoreType.DMA((count,)),
    ]


def exchange(arrays, shards, collective_id):
    count = len(arrays)
    kernel = functools.partial(exchange_kernel, count=count, shards=shards)
    any_spec = pl.BlockSpec(memory_space=pl.ANY)
    return pl.pallas_call(
        kernel,
        out_shape=[jax.ShapeDtypeStruct(x.shape, x.dtype) for x in arrays],
        in_specs=[any_spec] * count,
        out_specs=[any_spec] * count,
        scratch_shapes=send_scratch(count, shards),
        compiler_params=pltpu.CompilerParams(
            collective_id=collective_id, has_side_effects=True
        ),
    )(*arrays)


def attend_body(qt_ref, kt_ref, vt_ref, o_ref, s_scr, k_ref, inv_root, after_block=None):
    blocks, head_dim, q_rows = qt_ref.shape
    for c in range(blocks):
        k_ref[c] = kt_ref[c].astype(jnp.float32).T.astype(k_ref.dtype)

    me = lax.axis_index("ctx")

    def one_block(j, carry):
        b = lax.rem(j + me + 1, blocks)
        qt = qt_ref[b]

        def score(c, m):
            s = jnp.dot(k_ref[c], qt, preferred_element_type=jnp.float32) * inv_root
            s_scr[c] = s
            return jnp.maximum(m, jnp.max(s, axis=0, keepdims=True))

        m = lax.fori_loop(
            0, blocks, score, jnp.full((1, q_rows), -jnp.inf, jnp.float32), unroll=2
        )

        def accumulate(c, inner):
            total, acc = inner
            expo = jnp.exp(s_scr[c] - m)
            total = total + jnp.sum(expo, axis=0, keepdims=True)
            acc = acc + jnp.dot(
                vt_ref[c], expo.astype(jnp.bfloat16), preferred_element_type=jnp.float32
            )
            return total, acc

        total, acc = lax.fori_loop(
            0,
            blocks,
            accumulate,
            (
                jnp.zeros((1, q_rows), jnp.float32),
                jnp.zeros((head_dim, q_rows), jnp.float32),
            ),
            unroll=2,
        )
        o_ref[b] = (acc / total).astype(o_ref.dtype)
        if after_block is not None:
            after_block(b)
        return carry

    lax.fori_loop(0, blocks, one_block, 0)


def attend_send_kernel(*refs, count, shards, inv_root, stream):
    qt_ref, k_ref, vt_ref = refs[:3]
    sends = refs[3 : 3 + count]
    o_ref = refs[3 + count]
    gots = refs[4 + count : 4 + 2 * count]
    rest = refs[4 + 2 * count :]
    if stream:
        back_ref = rest[0]
        rest = rest[1:]
    s_scr, k_scr = rest[0], rest[1]
    rest = rest[1:]
    copies = start_sends(sends, gots, *rest[1:4], shards)
    after_block = None
    if stream:
        block_send, block_recv, block_local = rest[4:7]
        me = lax.axis_index("ctx")
        region = lax.axis_index("region")

        def remote_block(b):
            return pltpu.make_async_remote_copy(
                src_ref=o_ref.at[b],
                dst_ref=back_ref.at[me],
                send_sem=block_send.at[b],
                recv_sem=block_recv.at[me],
                device_id=(region, b),
                device_id_type=pl.DeviceIdType.MESH,
            )

        def local_block(b):
            return pltpu.make_async_copy(o_ref.at[b], back_ref.at[b], block_local.at[0])

        def after_block(b):
            @pl.when(b == me)
            def _():
                local_block(b).start()

            @pl.when(b != me)
            def _():
                remote_block(b).start()

    attend_body(qt_ref, k_ref, vt_ref, o_ref, s_scr, k_scr, inv_root, after_block)
    for copy in copies:
        copy.wait()
    if stream:
        for b in range(shards):
            @pl.when(b == me)
            def _():
                local_block(b).wait()

            @pl.when(b != me)
            def _():
                remote_block(b).wait_send()
                pltpu.make_async_remote_copy(
                    src_ref=o_ref.at[b],
                    dst_ref=back_ref.at[b],
                    send_sem=block_send.at[b],
                    recv_sem=block_recv.at[b],
                    device_id=(region, b),
                    device_id_type=pl.DeviceIdType.MESH,
                ).wait_recv()


def attend_send(q_t, k_tok, v_t, sends, shards, inv_root, collective_id, stream=False):
    blocks, head_dim, rows = q_t.shape
    count = len(sends)
    kernel = functools.partial(
        attend_send_kernel, count=count, shards=shards, inv_root=inv_root, stream=stream
    )
    any_spec = pl.BlockSpec(memory_space=pl.ANY)
    vmem_spec = pl.BlockSpec(memory_space=pltpu.VMEM)
    out_shape = [jax.ShapeDtypeStruct(q_t.shape, jnp.bfloat16)]
    out_shape += [jax.ShapeDtypeStruct(x.shape, x.dtype) for x in sends]
    out_specs = [vmem_spec] + [any_spec] * count
    scratch = [
        pltpu.VMEM((blocks, rows, rows), jnp.float32),
        pltpu.VMEM((blocks, rows, head_dim), jnp.bfloat16),
    ] + send_scratch(count, shards)
    if stream:
        out_shape.append(jax.ShapeDtypeStruct(q_t.shape, jnp.bfloat16))
        out_specs.append(any_spec)
        scratch += [
            pltpu.SemaphoreType.DMA((shards,)),
            pltpu.SemaphoreType.DMA((shards,)),
            pltpu.SemaphoreType.DMA((1,)),
        ]
    outs = pl.pallas_call(
        kernel,
        out_shape=out_shape,
        in_specs=[vmem_spec] * 3 + [any_spec] * count,
        out_specs=out_specs,
        scratch_shapes=scratch,
        compiler_params=pltpu.CompilerParams(
            collective_id=collective_id,
            has_side_effects=True,
            vmem_limit_bytes=48 * 1024 * 1024,
        ),
    )(q_t, k_tok, v_t, *sends)
    return outs[0], outs[1:]


def project_kernel(mod_ref, w_ref, act_ref, wg_ref, bg_ref, *refs, shards, pair, head_dim):
    got0 = refs[:3]
    later = refs[3 : 3 * pair]
    gate_ref = refs[3 * pair]
    send0 = refs[3 * pair + 1 : 3 * pair + 4]
    sems = refs[3 * pair + 4 :]
    modulated = mod_ref[...]

    def fill(h, dests, i):
        out_t = lax.dot_general(
            w_ref[i, h],
            modulated,
            (((1,), (1,)), ((), ())),
            preferred_element_type=jnp.float32,
        )
        for p in range(shards):
            piece = out_t[p * head_dim : (p + 1) * head_dim]
            dests[i][p] = piece.astype(jnp.bfloat16)

    enter(shards)
    copies = []
    for i in range(3):
        fill(0, send0, i)
        copies += start_array(i, send0[i], got0[i], *sems, shards)
    for h in range(1, pair):
        for i in range(3):
            fill(h, later[3 * (h - 1) : 3 * h], i)
    gate = jnp.dot(act_ref[...], wg_ref[...], preferred_element_type=jnp.float32)
    gate_ref[...] = (gate + bg_ref[...]).astype(gate_ref.dtype)
    for copy in copies:
        copy.wait()


def project_send(modulated, w_t, activated, w_gate, b_gate, shards, pair, head_dim):
    rows, width = modulated.shape
    q_shape = jax.ShapeDtypeStruct((shards, head_dim, rows), jnp.bfloat16)
    shapes = [q_shape, q_shape, q_shape]
    kernel = functools.partial(
        project_kernel, shards=shards, pair=pair, head_dim=head_dim
    )
    any_spec = pl.BlockSpec(memory_space=pl.ANY)
    vmem_spec = pl.BlockSpec(memory_space=pltpu.VMEM)
    outs = pl.pallas_call(
        kernel,
        out_shape=shapes * pair
        + [jax.ShapeDtypeStruct((rows, w_gate.shape[1]), jnp.bfloat16)],
        in_specs=[vmem_spec] * 5,
        out_specs=[any_spec] * 3 + [vmem_spec] * (3 * (pair - 1) + 1),
        scratch_shapes=[pltpu.VMEM(x.shape, x.dtype) for x in shapes]
        + send_scratch(3, shards),
        compiler_params=pltpu.CompilerParams(
            collective_id=pair + 1,
            has_side_effects=True,
            vmem_limit_bytes=48 * 1024 * 1024,
        ),
    )(modulated, w_t, activated, w_gate, b_gate)
    return outs[:3], [outs[3 * h : 3 * h + 3] for h in range(1, pair)], outs[3 * pair]


def head_pipeline(modulated, w_t, gate_parts, shards, pair, head_dim, inverse_root):
    got, later, gate = project_send(modulated, w_t, *gate_parts, shards, pair, head_dim)
    backs = []
    for h in range(pair):
        last = h + 1 == pair
        sends = [] if last else list(later[h])
        if h > 0:
            sends = sends + [out_prev]
        out_prev, sent = attend_send(
            *got, sends, shards, inverse_root, 1 + h, stream=last
        )
        if not last:
            got = sent[:3]
            sent = sent[3:]
        backs.extend(sent)
    return jnp.stack(backs, axis=1), gate


def per_device(
    tokens, element_ids, element_slot, live_count, cond_table, w_ada, b_ada, w_qkv, w_out
):
    device_tokens = tokens[0]
    tok_rows, width = device_tokens.shape
    owners = lax.axis_size(("region", "ctx"))
    shards = lax.axis_size("ctx")
    elem_rows = cond_table.shape[0]
    capacity = -(-max(2, 3 * tok_rows // (2 * owners)) // 8) * 8
    slots = element_slot[element_ids[0]]
    owner_index = slots // elem_rows
    local_row = slots % elem_rows
    position = jnp.arange(tok_rows, dtype=jnp.int32)
    solid = position < live_count[0, 0]
    earlier = (
        (owner_index[:, None] == owner_index[None, :])
        & (position[None, :] < position[:, None])
        & solid[None, :]
    )
    place_rank = jnp.sum(earlier.astype(jnp.int32), axis=1)
    target = jnp.where(solid, owner_index * capacity + place_rank, owners * capacity)
    requests = jnp.zeros((owners * capacity,), jnp.int32).at[target].set(local_row, mode="drop")
    asked = lax.all_to_all(
        requests.reshape(owners, capacity),
        ("region", "ctx"),
        split_axis=0,
        concat_axis=0,
        tiled=True,
    ).reshape(-1)
    pick_at = jnp.minimum(target, owners * capacity - 1)
    served_hot = (asked[:, None] == jnp.arange(elem_rows, dtype=jnp.int32)[None, :]).astype(
        jnp.bfloat16
    )
    served = (
        jnp.dot(served_hot, cond_table, preferred_element_type=jnp.float32)
        .astype(jnp.bfloat16)
        .reshape(owners, capacity, width)
    )
    replies = lax.all_to_all(served, ("region", "ctx"), split_axis=0, concat_axis=0, tiled=True)
    pick_hot = (
        pick_at[:, None] == jnp.arange(owners * capacity, dtype=jnp.int32)[None, :]
    ).astype(jnp.bfloat16)
    picked = jnp.dot(
        pick_hot, replies.reshape(owners * capacity, width), preferred_element_type=jnp.float32
    )
    activated = jnp.where(solid[:, None], jax.nn.silu(picked.astype(jnp.float32)), 0.0).astype(
        jnp.bfloat16
    )
    mods = (
        jnp.dot(activated, w_ada[:, : 2 * width], preferred_element_type=jnp.float32)
        + b_ada[: 2 * width]
    ).astype(jnp.bfloat16)
    mods = mods.astype(jnp.float32)
    gate_parts = (activated, w_ada[:, 2 * width :], b_ada[None, 2 * width :])
    modulated = layer_modulate(device_tokens, mods, width)

    head_dim = width // HEADS
    pair = HEADS // shards
    inverse_root = 1.0 / math.sqrt(head_dim)
    w_t = (
        w_qkv.reshape(width, 3, shards, pair, head_dim)
        .transpose(1, 3, 2, 4, 0)
        .reshape(3, pair, shards * head_dim, width)
    )
    backs, gate = head_pipeline(
        modulated, w_t, gate_parts, shards, pair, head_dim, inverse_root
    )
    w_out_parts = w_out.reshape(shards, pair, head_dim, width)
    projected = jnp.einsum(
        "phet,pheD->tD",
        backs,
        w_out_parts,
        preferred_element_type=jnp.float32,
    )
    gate = gate.astype(jnp.float32)
    output = (device_tokens.astype(jnp.float32) + gate * projected).astype(jnp.bfloat16)
    return output[None]


def solution(mesh):
    placed = (
        P("region", "ctx", None),
        P("region", "ctx"),
        P(),
        P("region", "ctx"),
        P(("region", "ctx"), None),
        P(),
        P(),
        P(),
        P(),
    )
    return jax.shard_map(
        per_device, mesh=mesh, in_specs=placed, out_specs=P("region", "ctx", None), check_vma=False
    )
```

```python
import functools
import math

import jax
import jax.numpy as jnp
from jax import lax
from jax.experimental import pallas as pl
from jax.experimental.pallas import tpu as pltpu
from jax.sharding import PartitionSpec as P

HEADS = 16


def layer_modulate(device_tokens, mods, width):
    values = device_tokens.astype(jnp.float32)
    center = jnp.mean(values, axis=1, keepdims=True)
    spread = jnp.mean((values - center) ** 2, axis=1, keepdims=True)
    normed = (values - center) * lax.rsqrt(spread + 1e-06)
    shift = mods[:, :width]
    scale = mods[:, width : 2 * width]
    return (normed * (1.0 + scale) + shift).astype(jnp.bfloat16)


def enter(shards):
    me = lax.axis_index("ctx")
    region = lax.axis_index("region")
    barrier = pltpu.get_barrier_semaphore()
    for d in range(1, shards):
        peer = lax.rem(me + d, shards)
        pl.semaphore_signal(
            barrier, 1, device_id=(region, peer), device_id_type=pl.DeviceIdType.MESH
        )
    pl.semaphore_wait(barrier, shards - 1)


def start_array(a, send, got, send_sem, recv_sem, local_sem, shards):
    me = lax.axis_index("ctx")
    region = lax.axis_index("region")
    local = pltpu.make_async_copy(send.at[me], got.at[me], local_sem.at[a])
    local.start()
    copies = [local]
    for d in range(1, shards):
        peer = lax.rem(me + d, shards)
        remote = pltpu.make_async_remote_copy(
            src_ref=send.at[peer],
            dst_ref=got.at[me],
            send_sem=send_sem.at[a, d - 1],
            recv_sem=recv_sem.at[a, d - 1],
            device_id=(region, peer),
            device_id_type=pl.DeviceIdType.MESH,
        )
        remote.start()
        copies.append(remote)
    return copies


def start_sends(sends, gots, send_sem, recv_sem, local_sem, shards):
    enter(shards)
    copies = []
    for a in range(len(sends)):
        copies += start_array(a, sends[a], gots[a], send_sem, recv_sem, local_sem, shards)
    return copies


def exchange_kernel(*refs, count, shards):
    sends = refs[:count]
    gots = refs[count : 2 * count]
    copies = start_sends(sends, gots, *refs[2 * count :], shards)
    for copy in copies:
        copy.wait()


def send_scratch(count, shards):
    return [
        pltpu.SemaphoreType.DMA((count, shards - 1)),
        pltpu.SemaphoreType.DMA((count, shards - 1)),
        pltpu.SemaphoreType.DMA((count,)),
    ]


def exchange(arrays, shards, collective_id):
    count = len(arrays)
    kernel = functools.partial(exchange_kernel, count=count, shards=shards)
    any_spec = pl.BlockSpec(memory_space=pl.ANY)
    return pl.pallas_call(
        kernel,
        out_shape=[jax.ShapeDtypeStruct(x.shape, x.dtype) for x in arrays],
        in_specs=[any_spec] * count,
        out_specs=[any_spec] * count,
        scratch_shapes=send_scratch(count, shards),
        compiler_params=pltpu.CompilerParams(
            collective_id=collective_id, has_side_effects=True
        ),
    )(*arrays)


def attend_body(qt_ref, kt_ref, vt_ref, o_ref, s_scr, k_ref, inv_root, after_block=None):
    blocks, head_dim, q_rows = qt_ref.shape
    for c in range(blocks):
        k_ref[c] = kt_ref[c].astype(jnp.float32).T.astype(k_ref.dtype)

    me = lax.axis_index("ctx")

    def one_block(j, carry):
        b = lax.rem(j + me + 1, blocks)
        qt = qt_ref[b]

        def score(c, m):
            s = jnp.dot(k_ref[c], qt, preferred_element_type=jnp.float32) * inv_root
            s_scr[c] = s
            return jnp.maximum(m, jnp.max(s, axis=0, keepdims=True))

        m = lax.fori_loop(
            0, blocks, score, jnp.full((1, q_rows), -jnp.inf, jnp.float32), unroll=2
        )

        def accumulate(c, inner):
            total, acc = inner
            expo = jnp.exp(s_scr[c] - m)
            total = total + jnp.sum(expo, axis=0, keepdims=True)
            acc = acc + jnp.dot(
                vt_ref[c], expo.astype(jnp.bfloat16), preferred_element_type=jnp.float32
            )
            return total, acc

        total, acc = lax.fori_loop(
            0,
            blocks,
            accumulate,
            (
                jnp.zeros((1, q_rows), jnp.float32),
                jnp.zeros((head_dim, q_rows), jnp.float32),
            ),
            unroll=2,
        )
        o_ref[b] = (acc / total).astype(o_ref.dtype)
        if after_block is not None:
            after_block(b)
        return carry

    lax.fori_loop(0, blocks, one_block, 0)


def attend_send_kernel(*refs, count, shards, inv_root, stream):
    qt_ref, k_ref, vt_ref = refs[:3]
    sends = refs[3 : 3 + count]
    o_ref = refs[3 + count]
    gots = refs[4 + count : 4 + 2 * count]
    rest = refs[4 + 2 * count :]
    if stream:
        back_ref = rest[0]
        rest = rest[1:]
    s_scr, k_scr = rest[0], rest[1]
    rest = rest[1:]
    copies = start_sends(sends, gots, *rest[1:4], shards)
    after_block = None
    if stream:
        block_send, block_recv, block_local = rest[4:7]
        me = lax.axis_index("ctx")
        region = lax.axis_index("region")

        def remote_block(b):
            return pltpu.make_async_remote_copy(
                src_ref=o_ref.at[b],
                dst_ref=back_ref.at[me],
                send_sem=block_send.at[b],
                recv_sem=block_recv.at[me],
                device_id=(region, b),
                device_id_type=pl.DeviceIdType.MESH,
            )

        def local_block(b):
            return pltpu.make_async_copy(o_ref.at[b], back_ref.at[b], block_local.at[0])

        def after_block(b):
            @pl.when(b == me)
            def _():
                local_block(b).start()

            @pl.when(b != me)
            def _():
                remote_block(b).start()

    attend_body(qt_ref, k_ref, vt_ref, o_ref, s_scr, k_scr, inv_root, after_block)
    for copy in copies:
        copy.wait()
    if stream:
        for b in range(shards):
            @pl.when(b == me)
            def _():
                local_block(b).wait()

            @pl.when(b != me)
            def _():
                remote_block(b).wait_send()
                pltpu.make_async_remote_copy(
                    src_ref=o_ref.at[b],
                    dst_ref=back_ref.at[b],
                    send_sem=block_send.at[b],
                    recv_sem=block_recv.at[b],
                    device_id=(region, b),
                    device_id_type=pl.DeviceIdType.MESH,
                ).wait_recv()


def attend_send(q_t, k_tok, v_t, sends, shards, inv_root, collective_id, stream=False):
    blocks, head_dim, rows = q_t.shape
    count = len(sends)
    kernel = functools.partial(
        attend_send_kernel, count=count, shards=shards, inv_root=inv_root, stream=stream
    )
    any_spec = pl.BlockSpec(memory_space=pl.ANY)
    vmem_spec = pl.BlockSpec(memory_space=pltpu.VMEM)
    out_shape = [jax.ShapeDtypeStruct(q_t.shape, jnp.bfloat16)]
    out_shape += [jax.ShapeDtypeStruct(x.shape, x.dtype) for x in sends]
    out_specs = [vmem_spec] + [any_spec] * count
    scratch = [
        pltpu.VMEM((blocks, rows, rows), jnp.float32),
        pltpu.VMEM((blocks, rows, head_dim), jnp.bfloat16),
    ] + send_scratch(count, shards)
    if stream:
        out_shape.append(jax.ShapeDtypeStruct(q_t.shape, jnp.bfloat16))
        out_specs.append(any_spec)
        scratch += [
            pltpu.SemaphoreType.DMA((shards,)),
            pltpu.SemaphoreType.DMA((shards,)),
            pltpu.SemaphoreType.DMA((1,)),
        ]
    outs = pl.pallas_call(
        kernel,
        out_shape=out_shape,
        in_specs=[vmem_spec] * 3 + [any_spec] * count,
        out_specs=out_specs,
        scratch_shapes=scratch,
        compiler_params=pltpu.CompilerParams(
            collective_id=collective_id,
            has_side_effects=True,
            vmem_limit_bytes=48 * 1024 * 1024,
        ),
    )(q_t, k_tok, v_t, *sends)
    return outs[0], outs[1:]


def project_kernel(mod_ref, w_ref, act_ref, wg_ref, bg_ref, *refs, shards, pair, head_dim):
    got0 = refs[:3]
    later = refs[3 : 3 * pair]
    gate_ref = refs[3 * pair]
    send0 = refs[3 * pair + 1 : 3 * pair + 4]
    sems = refs[3 * pair + 4 :]
    modulated = mod_ref[...]

    def fill(h, dests, i):
        out_t = lax.dot_general(
            w_ref[i, h],
            modulated,
            (((1,), (1,)), ((), ())),
            preferred_element_type=jnp.float32,
        )
        for p in range(shards):
            piece = out_t[p * head_dim : (p + 1) * head_dim]
            dests[i][p] = piece.astype(jnp.bfloat16)

    enter(shards)
    copies = []
    for i in range(3):
        fill(0, send0, i)
        copies += start_array(i, send0[i], got0[i], *sems, shards)
    for h in range(1, pair):
        for i in range(3):
            fill(h, later[3 * (h - 1) : 3 * h], i)
    gate = jnp.dot(act_ref[...], wg_ref[...], preferred_element_type=jnp.float32)
    gate_ref[...] = (gate + bg_ref[...]).astype(gate_ref.dtype)
    for copy in copies:
        copy.wait()


def project_send(modulated, w_t, activated, w_gate, b_gate, shards, pair, head_dim):
    rows, width = modulated.shape
    q_shape = jax.ShapeDtypeStruct((shards, head_dim, rows), jnp.bfloat16)
    shapes = [q_shape, q_shape, q_shape]
    kernel = functools.partial(
        project_kernel, shards=shards, pair=pair, head_dim=head_dim
    )
    any_spec = pl.BlockSpec(memory_space=pl.ANY)
    vmem_spec = pl.BlockSpec(memory_space=pltpu.VMEM)
    outs = pl.pallas_call(
        kernel,
        out_shape=shapes * pair
        + [jax.ShapeDtypeStruct((rows, w_gate.shape[1]), jnp.bfloat16)],
        in_specs=[vmem_spec] * 5,
        out_specs=[any_spec] * 3 + [vmem_spec] * (3 * (pair - 1) + 1),
        scratch_shapes=[pltpu.VMEM(x.shape, x.dtype) for x in shapes]
        + send_scratch(3, shards),
        compiler_params=pltpu.CompilerParams(
            collective_id=pair + 1,
            has_side_effects=True,
            vmem_limit_bytes=48 * 1024 * 1024,
        ),
    )(modulated, w_t, activated, w_gate, b_gate)
    return outs[:3], [outs[3 * h : 3 * h + 3] for h in range(1, pair)], outs[3 * pair]


def head_pipeline(modulated, w_t, gate_parts, shards, pair, head_dim, inverse_root):
    got, later, gate = project_send(modulated, w_t, *gate_parts, shards, pair, head_dim)
    backs = []
    for h in range(pair):
        last = h + 1 == pair
        sends = [] if last else list(later[h])
        if h > 0:
            sends = sends + [out_prev]
        out_prev, sent = attend_send(
            *got, sends, shards, inverse_root, 1 + h, stream=last
        )
        if not last:
            got = sent[:3]
            sent = sent[3:]
        backs.extend(sent)
    return jnp.stack(backs, axis=1), gate


def per_device(
    tokens, element_ids, element_slot, live_count, cond_table, w_ada, b_ada, w_qkv, w_out
):
    device_tokens = tokens[0]
    tok_rows, width = device_tokens.shape
    owners = lax.axis_size(("region", "ctx"))
    shards = lax.axis_size("ctx")
    elem_rows = cond_table.shape[0]
    capacity = -(-max(2, 3 * tok_rows // (2 * owners)) // 8) * 8
    slots = element_slot[element_ids[0]]
    owner_index = slots // elem_rows
    local_row = slots % elem_rows
    position = jnp.arange(tok_rows, dtype=jnp.int32)
    solid = position < live_count[0, 0]
    earlier = (
        (owner_index[:, None] == owner_index[None, :])
        & (position[None, :] < position[:, None])
        & solid[None, :]
    )
    place_rank = jnp.sum(earlier.astype(jnp.int32), axis=1)
    target = jnp.where(solid, owner_index * capacity + place_rank, owners * capacity)
    requests = jnp.zeros((owners * capacity,), jnp.int32).at[target].set(local_row, mode="drop")
    by_owner = requests.reshape(owners // shards, shards, capacity)
    by_owner = lax.all_to_all(by_owner, "ctx", split_axis=1, concat_axis=1, tiled=True)
    asked = lax.all_to_all(by_owner, "region", split_axis=0, concat_axis=0, tiled=True).reshape(-1)
    pick_at = jnp.minimum(target, owners * capacity - 1)
    served_hot = (asked[:, None] == jnp.arange(elem_rows, dtype=jnp.int32)[None, :]).astype(
        jnp.bfloat16
    )
    served = (
        jnp.dot(served_hot, cond_table, preferred_element_type=jnp.float32)
        .astype(jnp.bfloat16)
        .reshape(owners, capacity, width)
    )
    replies = lax.all_to_all(served, ("region", "ctx"), split_axis=0, concat_axis=0, tiled=True)
    pick_hot = (
        pick_at[:, None] == jnp.arange(owners * capacity, dtype=jnp.int32)[None, :]
    ).astype(jnp.bfloat16)
    picked = jnp.dot(
        pick_hot, replies.reshape(owners * capacity, width), preferred_element_type=jnp.float32
    )
    activated = jnp.where(solid[:, None], jax.nn.silu(picked.astype(jnp.float32)), 0.0).astype(
        jnp.bfloat16
    )
    mods = (
        jnp.dot(activated, w_ada[:, : 2 * width], preferred_element_type=jnp.float32)
        + b_ada[: 2 * width]
    ).astype(jnp.bfloat16)
    mods = mods.astype(jnp.float32)
    gate_parts = (activated, w_ada[:, 2 * width :], b_ada[None, 2 * width :])
    modulated = layer_modulate(device_tokens, mods, width)

    head_dim = width // HEADS
    pair = HEADS // shards
    inverse_root = 1.0 / math.sqrt(head_dim)
    w_t = (
        w_qkv.reshape(width, 3, shards, pair, head_dim)
        .transpose(1, 3, 2, 4, 0)
        .reshape(3, pair, shards * head_dim, width)
    )
    backs, gate = head_pipeline(
        modulated, w_t, gate_parts, shards, pair, head_dim, inverse_root
    )
    w_out_parts = w_out.reshape(shards, pair, head_dim, width)
    projected = jnp.einsum(
        "phet,pheD->tD",
        backs,
        w_out_parts,
        preferred_element_type=jnp.float32,
    )
    gate = gate.astype(jnp.float32)
    output = (device_tokens.astype(jnp.float32) + gate * projected).astype(jnp.bfloat16)
    return output[None]


def solution(mesh):
    placed = (
        P("region", "ctx", None),
        P("region", "ctx"),
        P(),
        P("region", "ctx"),
        P(("region", "ctx"), None),
        P(),
        P(),
        P(),
        P(),
    )
    return jax.shard_map(
        per_device, mesh=mesh, in_specs=placed, out_specs=P("region", "ctx", None), check_vma=False
    )
```

```python
import functools
import math

import jax
import jax.numpy as jnp
from jax import lax
from jax.experimental import pallas as pl
from jax.experimental.pallas import tpu as pltpu
from jax.sharding import PartitionSpec as P

HEADS = 16


def layer_modulate(device_tokens, mods, width):
    values = device_tokens.astype(jnp.float32)
    center = jnp.mean(values, axis=1, keepdims=True)
    spread = jnp.mean((values - center) ** 2, axis=1, keepdims=True)
    normed = (values - center) * lax.rsqrt(spread + 1e-06)
    shift = mods[:, :width]
    scale = mods[:, width : 2 * width]
    return (normed * (1.0 + scale) + shift).astype(jnp.bfloat16)


def enter(shards):
    me = lax.axis_index("ctx")
    region = lax.axis_index("region")
    barrier = pltpu.get_barrier_semaphore()
    for d in range(1, shards):
        peer = lax.rem(me + d, shards)
        pl.semaphore_signal(
            barrier, 1, device_id=(region, peer), device_id_type=pl.DeviceIdType.MESH
        )
    pl.semaphore_wait(barrier, shards - 1)


def start_array(a, send, got, send_sem, recv_sem, local_sem, shards):
    me = lax.axis_index("ctx")
    region = lax.axis_index("region")
    local = pltpu.make_async_copy(send.at[me], got.at[me], local_sem.at[a])
    local.start()
    copies = [local]
    for d in range(1, shards):
        peer = lax.rem(me + d, shards)
        remote = pltpu.make_async_remote_copy(
            src_ref=send.at[peer],
            dst_ref=got.at[me],
            send_sem=send_sem.at[a, d - 1],
            recv_sem=recv_sem.at[a, d - 1],
            device_id=(region, peer),
            device_id_type=pl.DeviceIdType.MESH,
        )
        remote.start()
        copies.append(remote)
    return copies


def start_sends(sends, gots, send_sem, recv_sem, local_sem, shards):
    enter(shards)
    copies = []
    for a in range(len(sends)):
        copies += start_array(a, sends[a], gots[a], send_sem, recv_sem, local_sem, shards)
    return copies


def exchange_kernel(*refs, count, shards):
    sends = refs[:count]
    gots = refs[count : 2 * count]
    copies = start_sends(sends, gots, *refs[2 * count :], shards)
    for copy in copies:
        copy.wait()


def send_scratch(count, shards):
    return [
        pltpu.SemaphoreType.DMA((count, shards - 1)),
        pltpu.SemaphoreType.DMA((count, shards - 1)),
        pltpu.SemaphoreType.DMA((count,)),
    ]


def exchange(arrays, shards, collective_id):
    count = len(arrays)
    kernel = functools.partial(exchange_kernel, count=count, shards=shards)
    any_spec = pl.BlockSpec(memory_space=pl.ANY)
    return pl.pallas_call(
        kernel,
        out_shape=[jax.ShapeDtypeStruct(x.shape, x.dtype) for x in arrays],
        in_specs=[any_spec] * count,
        out_specs=[any_spec] * count,
        scratch_shapes=send_scratch(count, shards),
        compiler_params=pltpu.CompilerParams(
            collective_id=collective_id, has_side_effects=True
        ),
    )(*arrays)


def attend_body(qt_ref, kt_ref, vt_ref, o_ref, s_scr, k_ref, inv_root, after_block=None):
    blocks, head_dim, q_rows = qt_ref.shape
    for c in range(blocks):
        k_ref[c] = kt_ref[c].astype(jnp.float32).T.astype(k_ref.dtype)

    me = lax.axis_index("ctx")

    def one_block(j, carry):
        b = lax.rem(j + me + 1, blocks)
        qt = qt_ref[b]

        def score(c, m):
            s = jnp.dot(k_ref[c], qt, preferred_element_type=jnp.float32) * inv_root
            s_scr[c] = s
            return jnp.maximum(m, jnp.max(s, axis=0, keepdims=True))

        m = lax.fori_loop(
            0, blocks, score, jnp.full((1, q_rows), -jnp.inf, jnp.float32), unroll=2
        )

        def accumulate(c, inner):
            total, acc = inner
            expo = jnp.exp(s_scr[c] - m)
            total = total + jnp.sum(expo, axis=0, keepdims=True)
            acc = acc + jnp.dot(
                vt_ref[c], expo.astype(jnp.bfloat16), preferred_element_type=jnp.float32
            )
            return total, acc

        total, acc = lax.fori_loop(
            0,
            blocks,
            accumulate,
            (
                jnp.zeros((1, q_rows), jnp.float32),
                jnp.zeros((head_dim, q_rows), jnp.float32),
            ),
            unroll=2,
        )
        o_ref[b] = (acc / total).astype(o_ref.dtype)
        if after_block is not None:
            after_block(b)
        return carry

    lax.fori_loop(0, blocks, one_block, 0)


def attend_send_kernel(*refs, count, shards, inv_root, stream):
    qt_ref, k_ref, vt_ref = refs[:3]
    sends = refs[3 : 3 + count]
    o_ref = refs[3 + count]
    gots = refs[4 + count : 4 + 2 * count]
    rest = refs[4 + 2 * count :]
    if stream:
        back_ref = rest[0]
        rest = rest[1:]
    s_scr, k_scr = rest[0], rest[1]
    rest = rest[1:]
    copies = start_sends(sends, gots, *rest[1:4], shards)
    after_block = None
    if stream:
        block_send, block_recv, block_local = rest[4:7]
        me = lax.axis_index("ctx")
        region = lax.axis_index("region")

        def remote_block(b):
            return pltpu.make_async_remote_copy(
                src_ref=o_ref.at[b],
                dst_ref=back_ref.at[me],
                send_sem=block_send.at[b],
                recv_sem=block_recv.at[me],
                device_id=(region, b),
                device_id_type=pl.DeviceIdType.MESH,
            )

        def local_block(b):
            return pltpu.make_async_copy(o_ref.at[b], back_ref.at[b], block_local.at[0])

        def after_block(b):
            @pl.when(b == me)
            def _():
                local_block(b).start()

            @pl.when(b != me)
            def _():
                remote_block(b).start()

    attend_body(qt_ref, k_ref, vt_ref, o_ref, s_scr, k_scr, inv_root, after_block)
    for copy in copies:
        copy.wait()
    if stream:
        for b in range(shards):
            @pl.when(b == me)
            def _():
                local_block(b).wait()

            @pl.when(b != me)
            def _():
                remote_block(b).wait_send()
                pltpu.make_async_remote_copy(
                    src_ref=o_ref.at[b],
                    dst_ref=back_ref.at[b],
                    send_sem=block_send.at[b],
                    recv_sem=block_recv.at[b],
                    device_id=(region, b),
                    device_id_type=pl.DeviceIdType.MESH,
                ).wait_recv()


def attend_send(q_t, k_tok, v_t, sends, shards, inv_root, collective_id, stream=False):
    blocks, head_dim, rows = q_t.shape
    count = len(sends)
    kernel = functools.partial(
        attend_send_kernel, count=count, shards=shards, inv_root=inv_root, stream=stream
    )
    any_spec = pl.BlockSpec(memory_space=pl.ANY)
    vmem_spec = pl.BlockSpec(memory_space=pltpu.VMEM)
    out_shape = [jax.ShapeDtypeStruct(q_t.shape, jnp.bfloat16)]
    out_shape += [jax.ShapeDtypeStruct(x.shape, x.dtype) for x in sends]
    out_specs = [vmem_spec] + [any_spec] * count
    scratch = [
        pltpu.VMEM((blocks, rows, rows), jnp.float32),
        pltpu.VMEM((blocks, rows, head_dim), jnp.bfloat16),
    ] + send_scratch(count, shards)
    if stream:
        out_shape.append(jax.ShapeDtypeStruct(q_t.shape, jnp.bfloat16))
        out_specs.append(any_spec)
        scratch += [
            pltpu.SemaphoreType.DMA((shards,)),
            pltpu.SemaphoreType.DMA((shards,)),
            pltpu.SemaphoreType.DMA((1,)),
        ]
    outs = pl.pallas_call(
        kernel,
        out_shape=out_shape,
        in_specs=[vmem_spec] * 3 + [any_spec] * count,
        out_specs=out_specs,
        scratch_shapes=scratch,
        compiler_params=pltpu.CompilerParams(
            collective_id=collective_id,
            has_side_effects=True,
            vmem_limit_bytes=48 * 1024 * 1024,
        ),
    )(q_t, k_tok, v_t, *sends)
    return outs[0], outs[1:]


def project_kernel(mod_ref, w_ref, act_ref, wg_ref, bg_ref, *refs, shards, pair, head_dim):
    got0 = refs[:3]
    later = refs[3 : 3 * pair]
    gate_ref = refs[3 * pair]
    send0 = refs[3 * pair + 1 : 3 * pair + 4]
    sems = refs[3 * pair + 4 :]
    modulated = mod_ref[...]

    def fill(h, dests, i):
        out_t = lax.dot_general(
            w_ref[i, h],
            modulated,
            (((1,), (1,)), ((), ())),
            preferred_element_type=jnp.float32,
        )
        for p in range(shards):
            piece = out_t[p * head_dim : (p + 1) * head_dim]
            dests[i][p] = piece.astype(jnp.bfloat16)

    enter(shards)
    copies = []
    for i in range(3):
        fill(0, send0, i)
        copies += start_array(i, send0[i], got0[i], *sems, shards)
    for h in range(1, pair):
        for i in range(3):
            fill(h, later[3 * (h - 1) : 3 * h], i)
    gate = jnp.dot(act_ref[...], wg_ref[...], preferred_element_type=jnp.float32)
    gate_ref[...] = (gate + bg_ref[...]).astype(gate_ref.dtype)
    for copy in copies:
        copy.wait()


def project_send(modulated, w_t, activated, w_gate, b_gate, shards, pair, head_dim):
    rows, width = modulated.shape
    q_shape = jax.ShapeDtypeStruct((shards, head_dim, rows), jnp.bfloat16)
    shapes = [q_shape, q_shape, q_shape]
    kernel = functools.partial(
        project_kernel, shards=shards, pair=pair, head_dim=head_dim
    )
    any_spec = pl.BlockSpec(memory_space=pl.ANY)
    vmem_spec = pl.BlockSpec(memory_space=pltpu.VMEM)
    outs = pl.pallas_call(
        kernel,
        out_shape=shapes * pair
        + [jax.ShapeDtypeStruct((rows, w_gate.shape[1]), jnp.bfloat16)],
        in_specs=[vmem_spec] * 5,
        out_specs=[any_spec] * 3 + [vmem_spec] * (3 * (pair - 1) + 1),
        scratch_shapes=[pltpu.VMEM(x.shape, x.dtype) for x in shapes]
        + send_scratch(3, shards),
        compiler_params=pltpu.CompilerParams(
            collective_id=pair + 1,
            has_side_effects=True,
            vmem_limit_bytes=48 * 1024 * 1024,
        ),
    )(modulated, w_t, activated, w_gate, b_gate)
    return outs[:3], [outs[3 * h : 3 * h + 3] for h in range(1, pair)], outs[3 * pair]


def head_pipeline(modulated, w_t, gate_parts, shards, pair, head_dim, inverse_root):
    got, later, gate = project_send(modulated, w_t, *gate_parts, shards, pair, head_dim)
    backs = []
    for h in range(pair):
        last = h + 1 == pair
        sends = [] if last else list(later[h])
        if h > 0:
            sends = sends + [out_prev]
        out_prev, sent = attend_send(
            *got, sends, shards, inverse_root, 1 + h, stream=last
        )
        if not last:
            got = sent[:3]
            sent = sent[3:]
        backs.extend(sent)
    return jnp.stack(backs, axis=1), gate


def request_kernel(req_ref, asked_ref, send_sem, recv_sem, local_sem, *, groups, shards):
    total = groups * shards
    me = lax.axis_index("region") * shards + lax.axis_index("ctx")
    mesh_id = pl.DeviceIdType.MESH
    barrier = pltpu.get_barrier_semaphore()

    def greet(d, carry):
        peer = lax.rem(me + d, total)
        pl.semaphore_signal(
            barrier, 1, device_id=(peer // shards, peer % shards), device_id_type=mesh_id
        )
        return carry

    lax.fori_loop(1, total, greet, 0)
    pl.semaphore_wait(barrier, total - 1)
    local = pltpu.make_async_copy(req_ref.at[me], asked_ref.at[me], local_sem.at[0])
    local.start()

    def remote(d):
        peer = lax.rem(me + d, total)
        return pltpu.make_async_remote_copy(
            src_ref=req_ref.at[peer],
            dst_ref=asked_ref.at[me],
            send_sem=send_sem.at[d - 1],
            recv_sem=recv_sem.at[d - 1],
            device_id=(peer // shards, peer % shards),
            device_id_type=mesh_id,
        )

    def launch(d, carry):
        remote(d).start()
        return carry

    def finish(d, carry):
        remote(d).wait()
        return carry

    lax.fori_loop(1, total, launch, 0)
    local.wait()
    lax.fori_loop(1, total, finish, 0)


def exchange_requests(requests, groups, shards):
    total = groups * shards
    any_spec = pl.BlockSpec(memory_space=pl.ANY)
    return pl.pallas_call(
        functools.partial(request_kernel, groups=groups, shards=shards),
        out_shape=jax.ShapeDtypeStruct(requests.shape, requests.dtype),
        in_specs=[any_spec],
        out_specs=any_spec,
        scratch_shapes=[
            pltpu.SemaphoreType.DMA((total - 1,)),
            pltpu.SemaphoreType.DMA((total - 1,)),
            pltpu.SemaphoreType.DMA((1,)),
        ],
        compiler_params=pltpu.CompilerParams(collective_id=7, has_side_effects=True),
    )(requests)


def per_device(
    tokens, element_ids, element_slot, live_count, cond_table, w_ada, b_ada, w_qkv, w_out
):
    device_tokens = tokens[0]
    tok_rows, width = device_tokens.shape
    owners = lax.axis_size(("region", "ctx"))
    shards = lax.axis_size("ctx")
    elem_rows = cond_table.shape[0]
    capacity = -(-max(2, 3 * tok_rows // (2 * owners)) // 8) * 8
    slots = element_slot[element_ids[0]]
    owner_index = slots // elem_rows
    local_row = slots % elem_rows
    position = jnp.arange(tok_rows, dtype=jnp.int32)
    solid = position < live_count[0, 0]
    earlier = (
        (owner_index[:, None] == owner_index[None, :])
        & (position[None, :] < position[:, None])
        & solid[None, :]
    )
    place_rank = jnp.sum(earlier.astype(jnp.int32), axis=1)
    target = jnp.where(solid, owner_index * capacity + place_rank, owners * capacity)
    requests = jnp.zeros((owners * capacity,), jnp.int32).at[target].set(local_row, mode="drop")
    asked = exchange_requests(
        requests.reshape(owners, capacity), owners // shards, shards
    ).reshape(-1)
    pick_at = jnp.minimum(target, owners * capacity - 1)
    served_hot = (asked[:, None] == jnp.arange(elem_rows, dtype=jnp.int32)[None, :]).astype(
        jnp.bfloat16
    )
    served = (
        jnp.dot(served_hot, cond_table, preferred_element_type=jnp.float32)
        .astype(jnp.bfloat16)
        .reshape(owners, capacity, width)
    )
    replies = lax.all_to_all(served, ("region", "ctx"), split_axis=0, concat_axis=0, tiled=True)
    pick_hot = (
        pick_at[:, None] == jnp.arange(owners * capacity, dtype=jnp.int32)[None, :]
    ).astype(jnp.bfloat16)
    picked = jnp.dot(
        pick_hot, replies.reshape(owners * capacity, width), preferred_element_type=jnp.float32
    )
    activated = jnp.where(solid[:, None], jax.nn.silu(picked.astype(jnp.float32)), 0.0).astype(
        jnp.bfloat16
    )
    mods = (
        jnp.dot(activated, w_ada[:, : 2 * width], preferred_element_type=jnp.float32)
        + b_ada[: 2 * width]
    ).astype(jnp.bfloat16)
    mods = mods.astype(jnp.float32)
    gate_parts = (activated, w_ada[:, 2 * width :], b_ada[None, 2 * width :])
    modulated = layer_modulate(device_tokens, mods, width)

    head_dim = width // HEADS
    pair = HEADS // shards
    inverse_root = 1.0 / math.sqrt(head_dim)
    w_t = (
        w_qkv.reshape(width, 3, shards, pair, head_dim)
        .transpose(1, 3, 2, 4, 0)
        .reshape(3, pair, shards * head_dim, width)
    )
    backs, gate = head_pipeline(
        modulated, w_t, gate_parts, shards, pair, head_dim, inverse_root
    )
    w_out_parts = w_out.reshape(shards, pair, head_dim, width)
    projected = jnp.einsum(
        "phet,pheD->tD",
        backs,
        w_out_parts,
        preferred_element_type=jnp.float32,
    )
    gate = gate.astype(jnp.float32)
    output = (device_tokens.astype(jnp.float32) + gate * projected).astype(jnp.bfloat16)
    return output[None]


def solution(mesh):
    placed = (
        P("region", "ctx", None),
        P("region", "ctx"),
        P(),
        P("region", "ctx"),
        P(("region", "ctx"), None),
        P(),
        P(),
        P(),
        P(),
    )
    return jax.shard_map(
        per_device, mesh=mesh, in_specs=placed, out_specs=P("region", "ctx", None), check_vma=False
    )
```

```python
import functools
import math

import jax
import jax.numpy as jnp
from jax import lax
from jax.experimental import pallas as pl
from jax.experimental.pallas import tpu as pltpu
from jax.sharding import PartitionSpec as P

HEADS = 16


def layer_modulate(device_tokens, mods, width):
    values = device_tokens.astype(jnp.float32)
    center = jnp.mean(values, axis=1, keepdims=True)
    spread = jnp.mean((values - center) ** 2, axis=1, keepdims=True)
    normed = (values - center) * lax.rsqrt(spread + 1e-06)
    shift = mods[:, :width]
    scale = mods[:, width : 2 * width]
    return (normed * (1.0 + scale) + shift).astype(jnp.bfloat16)


def enter(shards):
    me = lax.axis_index("ctx")
    region = lax.axis_index("region")
    barrier = pltpu.get_barrier_semaphore()
    for d in range(1, shards):
        peer = lax.rem(me + d, shards)
        pl.semaphore_signal(
            barrier, 1, device_id=(region, peer), device_id_type=pl.DeviceIdType.MESH
        )
    pl.semaphore_wait(barrier, shards - 1)


def start_array(a, send, got, send_sem, recv_sem, local_sem, shards):
    me = lax.axis_index("ctx")
    region = lax.axis_index("region")
    local = pltpu.make_async_copy(send.at[me], got.at[me], local_sem.at[a])
    local.start()
    copies = [local]
    for d in range(1, shards):
        peer = lax.rem(me + d, shards)
        remote = pltpu.make_async_remote_copy(
            src_ref=send.at[peer],
            dst_ref=got.at[me],
            send_sem=send_sem.at[a, d - 1],
            recv_sem=recv_sem.at[a, d - 1],
            device_id=(region, peer),
            device_id_type=pl.DeviceIdType.MESH,
        )
        remote.start()
        copies.append(remote)
    return copies


def start_sends(sends, gots, send_sem, recv_sem, local_sem, shards):
    enter(shards)
    copies = []
    for a in range(len(sends)):
        copies += start_array(a, sends[a], gots[a], send_sem, recv_sem, local_sem, shards)
    return copies


def exchange_kernel(*refs, count, shards):
    sends = refs[:count]
    gots = refs[count : 2 * count]
    copies = start_sends(sends, gots, *refs[2 * count :], shards)
    for copy in copies:
        copy.wait()


def send_scratch(count, shards):
    return [
        pltpu.SemaphoreType.DMA((count, shards - 1)),
        pltpu.SemaphoreType.DMA((count, shards - 1)),
        pltpu.SemaphoreType.DMA((count,)),
    ]


def exchange(arrays, shards, collective_id):
    count = len(arrays)
    kernel = functools.partial(exchange_kernel, count=count, shards=shards)
    any_spec = pl.BlockSpec(memory_space=pl.ANY)
    return pl.pallas_call(
        kernel,
        out_shape=[jax.ShapeDtypeStruct(x.shape, x.dtype) for x in arrays],
        in_specs=[any_spec] * count,
        out_specs=[any_spec] * count,
        scratch_shapes=send_scratch(count, shards),
        compiler_params=pltpu.CompilerParams(
            collective_id=collective_id, has_side_effects=True
        ),
    )(*arrays)


def attend_body(
    qt_ref, kt_ref, vt_ref, o_ref, s_scr, k_ref, inv_root, after_block=None, before_block=None,
    first=1,
):
    blocks, head_dim, q_rows = qt_ref.shape
    for c in range(blocks):
        k_ref[c] = kt_ref[c].astype(jnp.float32).T.astype(k_ref.dtype)

    me = lax.axis_index("ctx")

    def one_block(j, carry):
        b = lax.rem(j + me + first, blocks)
        if before_block is not None:
            before_block(j, b)
        qt = qt_ref[b]

        def score(c, m):
            s = jnp.dot(k_ref[c], qt, preferred_element_type=jnp.float32) * inv_root
            s_scr[c] = s
            return jnp.maximum(m, jnp.max(s, axis=0, keepdims=True))

        m = lax.fori_loop(
            0, blocks, score, jnp.full((1, q_rows), -jnp.inf, jnp.float32), unroll=2
        )

        def accumulate(c, inner):
            total, acc = inner
            expo = jnp.exp(s_scr[c] - m)
            total = total + jnp.sum(expo, axis=0, keepdims=True)
            acc = acc + jnp.dot(
                vt_ref[c], expo.astype(jnp.bfloat16), preferred_element_type=jnp.float32
            )
            return total, acc

        total, acc = lax.fori_loop(
            0,
            blocks,
            accumulate,
            (
                jnp.zeros((1, q_rows), jnp.float32),
                jnp.zeros((head_dim, q_rows), jnp.float32),
            ),
            unroll=2,
        )
        o_ref[b] = (acc / total).astype(o_ref.dtype)
        if after_block is not None:
            after_block(b)
        return carry

    lax.fori_loop(0, blocks, one_block, 0)


def attend_send_kernel(*refs, count, shards, inv_root, stream, pull):
    qt_ref, k_ref, vt_ref = refs[:3]
    sends = refs[3 : 3 + count]
    o_ref = refs[3 + count]
    gots = refs[4 + count : 4 + 2 * count]
    rest = refs[4 + 2 * count :]
    if stream:
        back_ref = rest[0]
        rest = rest[1:]
    s_scr, k_scr = rest[0], rest[1]
    rest = rest[1:]
    copies = start_sends(sends, gots, *rest[1:4], shards)
    before_block = None
    first = 1
    if pull:
        q_vmem, q_send, q_recv, q_local = rest[7:11] if stream else rest[4:8]
        me_q = lax.axis_index("ctx")
        region_q = lax.axis_index("region")
        q_local_copy = pltpu.make_async_copy(qt_ref.at[me_q], q_vmem.at[me_q], q_local.at[0])
        q_local_copy.start()

        def q_remote(d):
            peer = lax.rem(me_q + d, shards)
            return pltpu.make_async_remote_copy(
                src_ref=qt_ref.at[peer],
                dst_ref=q_vmem.at[me_q],
                send_sem=q_send.at[d - 1],
                recv_sem=q_recv.at[d - 1],
                device_id=(region_q, peer),
                device_id_type=pl.DeviceIdType.MESH,
            )

        for d in range(1, shards):
            q_remote(d).start()

        def before_block(j, b):
            @pl.when(j == 0)
            def _():
                q_local_copy.wait()

            @pl.when(j > 0)
            def _():
                pltpu.make_async_remote_copy(
                    src_ref=qt_ref.at[b],
                    dst_ref=q_vmem.at[b],
                    send_sem=q_send.at[shards - 1 - j],
                    recv_sem=q_recv.at[shards - 1 - j],
                    device_id=(region_q, b),
                    device_id_type=pl.DeviceIdType.MESH,
                ).wait_recv()

        first = 0
        qt_ref = q_vmem
    after_block = None
    if stream:
        block_send, block_recv, block_local = rest[4:7]
        me = lax.axis_index("ctx")
        region = lax.axis_index("region")

        def remote_block(b):
            return pltpu.make_async_remote_copy(
                src_ref=o_ref.at[b],
                dst_ref=back_ref.at[me],
                send_sem=block_send.at[b],
                recv_sem=block_recv.at[me],
                device_id=(region, b),
                device_id_type=pl.DeviceIdType.MESH,
            )

        def local_block(b):
            return pltpu.make_async_copy(o_ref.at[b], back_ref.at[b], block_local.at[0])

        def after_block(b):
            @pl.when(b == me)
            def _():
                local_block(b).start()

            @pl.when(b != me)
            def _():
                remote_block(b).start()

    attend_body(
        qt_ref, k_ref, vt_ref, o_ref, s_scr, k_scr, inv_root, after_block, before_block, first
    )
    for copy in copies:
        copy.wait()
    if pull:
        for d in range(1, shards):
            q_remote(d).wait_send()
    if stream:
        for b in range(shards):
            @pl.when(b == me)
            def _():
                local_block(b).wait()

            @pl.when(b != me)
            def _():
                remote_block(b).wait_send()
                pltpu.make_async_remote_copy(
                    src_ref=o_ref.at[b],
                    dst_ref=back_ref.at[b],
                    send_sem=block_send.at[b],
                    recv_sem=block_recv.at[b],
                    device_id=(region, b),
                    device_id_type=pl.DeviceIdType.MESH,
                ).wait_recv()


def attend_send(
    q_t, k_tok, v_t, sends, shards, inv_root, collective_id, stream=False, pull=False
):
    blocks, head_dim, rows = q_t.shape
    count = len(sends)
    kernel = functools.partial(
        attend_send_kernel,
        count=count,
        shards=shards,
        inv_root=inv_root,
        stream=stream,
        pull=pull,
    )
    any_spec = pl.BlockSpec(memory_space=pl.ANY)
    vmem_spec = pl.BlockSpec(memory_space=pltpu.VMEM)
    out_shape = [jax.ShapeDtypeStruct(q_t.shape, jnp.bfloat16)]
    out_shape += [jax.ShapeDtypeStruct(x.shape, x.dtype) for x in sends]
    out_specs = [vmem_spec] + [any_spec] * count
    scratch = [
        pltpu.VMEM((blocks, rows, rows), jnp.float32),
        pltpu.VMEM((blocks, rows, head_dim), jnp.bfloat16),
    ] + send_scratch(count, shards)
    if stream:
        out_shape.append(jax.ShapeDtypeStruct(q_t.shape, jnp.bfloat16))
        out_specs.append(any_spec)
        scratch += [
            pltpu.SemaphoreType.DMA((shards,)),
            pltpu.SemaphoreType.DMA((shards,)),
            pltpu.SemaphoreType.DMA((1,)),
        ]
    if pull:
        scratch += [
            pltpu.VMEM(q_t.shape, q_t.dtype),
            pltpu.SemaphoreType.DMA((shards - 1,)),
            pltpu.SemaphoreType.DMA((shards - 1,)),
            pltpu.SemaphoreType.DMA((1,)),
        ]
    outs = pl.pallas_call(
        kernel,
        out_shape=out_shape,
        in_specs=[any_spec if pull else vmem_spec] + [vmem_spec] * 2 + [any_spec] * count,
        out_specs=out_specs,
        scratch_shapes=scratch,
        compiler_params=pltpu.CompilerParams(
            collective_id=collective_id,
            has_side_effects=True,
            vmem_limit_bytes=48 * 1024 * 1024,
        ),
    )(q_t, k_tok, v_t, *sends)
    return outs[0], outs[1:]


def project_kernel(mod_ref, w_ref, act_ref, wg_ref, bg_ref, *refs, shards, pair, head_dim):
    got0 = refs[:2]
    q0_ref = refs[2]
    later = refs[3 : 3 * pair]
    gate_ref = refs[3 * pair]
    send0 = (q0_ref,) + tuple(refs[3 * pair + 1 : 3 * pair + 3])
    sems = refs[3 * pair + 3 :]
    modulated = mod_ref[...]

    def fill(h, dests, i):
        out_t = lax.dot_general(
            w_ref[i, h],
            modulated,
            (((1,), (1,)), ((), ())),
            preferred_element_type=jnp.float32,
        )
        for p in range(shards):
            piece = out_t[p * head_dim : (p + 1) * head_dim]
            dests[i][p] = piece.astype(jnp.bfloat16)

    enter(shards)
    copies = []
    fill(0, send0, 0)
    for i in range(1, 3):
        fill(0, send0, i)
        copies += start_array(i - 1, send0[i], got0[i - 1], *sems, shards)
    for h in range(1, pair):
        for i in range(3):
            fill(h, later[3 * (h - 1) : 3 * h], i)
    gate = jnp.dot(act_ref[...], wg_ref[...], preferred_element_type=jnp.float32)
    gate_ref[...] = (gate + bg_ref[...]).astype(gate_ref.dtype)
    for copy in copies:
        copy.wait()


def project_send(modulated, w_t, activated, w_gate, b_gate, shards, pair, head_dim):
    rows, width = modulated.shape
    q_shape = jax.ShapeDtypeStruct((shards, head_dim, rows), jnp.bfloat16)
    shapes = [q_shape, q_shape, q_shape]
    kernel = functools.partial(
        project_kernel, shards=shards, pair=pair, head_dim=head_dim
    )
    any_spec = pl.BlockSpec(memory_space=pl.ANY)
    vmem_spec = pl.BlockSpec(memory_space=pltpu.VMEM)
    outs = pl.pallas_call(
        kernel,
        out_shape=shapes * pair
        + [jax.ShapeDtypeStruct((rows, w_gate.shape[1]), jnp.bfloat16)],
        in_specs=[vmem_spec] * 5,
        out_specs=[any_spec] * 2 + [vmem_spec] * (3 * (pair - 1) + 2),
        scratch_shapes=[pltpu.VMEM(x.shape, x.dtype) for x in shapes[1:]]
        + send_scratch(2, shards),
        compiler_params=pltpu.CompilerParams(
            collective_id=pair + 1,
            has_side_effects=True,
            vmem_limit_bytes=48 * 1024 * 1024,
        ),
    )(modulated, w_t, activated, w_gate, b_gate)
    got = (outs[2], outs[0], outs[1])
    return got, [outs[3 * h : 3 * h + 3] for h in range(1, pair)], outs[3 * pair]


def head_pipeline(modulated, w_t, gate_parts, shards, pair, head_dim, inverse_root):
    got, later, gate = project_send(modulated, w_t, *gate_parts, shards, pair, head_dim)
    backs = []
    for h in range(pair):
        last = h + 1 == pair
        sends = [] if last else list(later[h])
        if h > 0:
            sends = sends + [out_prev]
        out_prev, sent = attend_send(
            *got, sends, shards, inverse_root, 1 + h, stream=last, pull=h == 0
        )
        if not last:
            got = sent[:3]
            sent = sent[3:]
        backs.extend(sent)
    return jnp.stack(backs, axis=1), gate


def request_kernel(req_ref, asked_ref, send_sem, recv_sem, local_sem, *, groups, shards):
    total = groups * shards
    me = lax.axis_index("region") * shards + lax.axis_index("ctx")
    mesh_id = pl.DeviceIdType.MESH
    barrier = pltpu.get_barrier_semaphore()

    def greet(d, carry):
        peer = lax.rem(me + d, total)
        pl.semaphore_signal(
            barrier, 1, device_id=(peer // shards, peer % shards), device_id_type=mesh_id
        )
        return carry

    lax.fori_loop(1, total, greet, 0)
    pl.semaphore_wait(barrier, total - 1)
    local = pltpu.make_async_copy(req_ref.at[me], asked_ref.at[me], local_sem.at[0])
    local.start()

    def remote(d):
        peer = lax.rem(me + d, total)
        return pltpu.make_async_remote_copy(
            src_ref=req_ref.at[peer],
            dst_ref=asked_ref.at[me],
            send_sem=send_sem.at[d - 1],
            recv_sem=recv_sem.at[d - 1],
            device_id=(peer // shards, peer % shards),
            device_id_type=mesh_id,
        )

    def launch(d, carry):
        remote(d).start()
        return carry

    def finish(d, carry):
        remote(d).wait()
        return carry

    lax.fori_loop(1, total, launch, 0)
    local.wait()
    lax.fori_loop(1, total, finish, 0)


def exchange_requests(requests, groups, shards):
    total = groups * shards
    any_spec = pl.BlockSpec(memory_space=pl.ANY)
    return pl.pallas_call(
        functools.partial(request_kernel, groups=groups, shards=shards),
        out_shape=jax.ShapeDtypeStruct(requests.shape, requests.dtype),
        in_specs=[any_spec],
        out_specs=any_spec,
        scratch_shapes=[
            pltpu.SemaphoreType.DMA((total - 1,)),
            pltpu.SemaphoreType.DMA((total - 1,)),
            pltpu.SemaphoreType.DMA((1,)),
        ],
        compiler_params=pltpu.CompilerParams(collective_id=7, has_side_effects=True),
    )(requests)


def per_device(
    tokens, element_ids, element_slot, live_count, cond_table, w_ada, b_ada, w_qkv, w_out
):
    device_tokens = tokens[0]
    tok_rows, width = device_tokens.shape
    owners = lax.axis_size(("region", "ctx"))
    shards = lax.axis_size("ctx")
    elem_rows = cond_table.shape[0]
    capacity = -(-max(2, 3 * tok_rows // (2 * owners)) // 8) * 8
    slots = element_slot[element_ids[0]]
    owner_index = slots // elem_rows
    local_row = slots % elem_rows
    position = jnp.arange(tok_rows, dtype=jnp.int32)
    solid = position < live_count[0, 0]
    earlier = (
        (owner_index[:, None] == owner_index[None, :])
        & (position[None, :] < position[:, None])
        & solid[None, :]
    )
    place_rank = jnp.sum(earlier.astype(jnp.int32), axis=1)
    target = jnp.where(solid, owner_index * capacity + place_rank, owners * capacity)
    requests = jnp.zeros((owners * capacity,), jnp.int32).at[target].set(local_row, mode="drop")
    asked = exchange_requests(
        requests.reshape(owners, capacity), owners // shards, shards
    ).reshape(-1)
    pick_at = jnp.minimum(target, owners * capacity - 1)
    served_hot = (asked[:, None] == jnp.arange(elem_rows, dtype=jnp.int32)[None, :]).astype(
        jnp.bfloat16
    )
    served = (
        jnp.dot(served_hot, cond_table, preferred_element_type=jnp.float32)
        .astype(jnp.bfloat16)
        .reshape(owners, capacity, width)
    )
    replies = lax.all_to_all(served, ("region", "ctx"), split_axis=0, concat_axis=0, tiled=True)
    pick_hot = (
        pick_at[:, None] == jnp.arange(owners * capacity, dtype=jnp.int32)[None, :]
    ).astype(jnp.bfloat16)
    picked = jnp.dot(
        pick_hot, replies.reshape(owners * capacity, width), preferred_element_type=jnp.float32
    )
    activated = jnp.where(solid[:, None], jax.nn.silu(picked.astype(jnp.float32)), 0.0).astype(
        jnp.bfloat16
    )
    mods = (
        jnp.dot(activated, w_ada[:, : 2 * width], preferred_element_type=jnp.float32)
        + b_ada[: 2 * width]
    ).astype(jnp.bfloat16)
    mods = mods.astype(jnp.float32)
    gate_parts = (activated, w_ada[:, 2 * width :], b_ada[None, 2 * width :])
    modulated = layer_modulate(device_tokens, mods, width)

    head_dim = width // HEADS
    pair = HEADS // shards
    inverse_root = 1.0 / math.sqrt(head_dim)
    w_t = (
        w_qkv.reshape(width, 3, shards, pair, head_dim)
        .transpose(1, 3, 2, 4, 0)
        .reshape(3, pair, shards * head_dim, width)
    )
    backs, gate = head_pipeline(
        modulated, w_t, gate_parts, shards, pair, head_dim, inverse_root
    )
    w_out_parts = w_out.reshape(shards, pair, head_dim, width)
    projected = jnp.einsum(
        "phet,pheD->tD",
        backs,
        w_out_parts,
        preferred_element_type=jnp.float32,
    )
    gate = gate.astype(jnp.float32)
    output = (device_tokens.astype(jnp.float32) + gate * projected).astype(jnp.bfloat16)
    return output[None]


def solution(mesh):
    placed = (
        P("region", "ctx", None),
        P("region", "ctx"),
        P(),
        P("region", "ctx"),
        P(("region", "ctx"), None),
        P(),
        P(),
        P(),
        P(),
    )
    return jax.shard_map(
        per_device, mesh=mesh, in_specs=placed, out_specs=P("region", "ctx", None), check_vma=False
    )
```

```python
import functools
import math

import jax
import jax.numpy as jnp
from jax import lax
from jax.experimental import pallas as pl
from jax.experimental.pallas import tpu as pltpu
from jax.sharding import PartitionSpec as P

HEADS = 16


def layer_modulate(device_tokens, mods, width):
    values = device_tokens.astype(jnp.float32)
    center = jnp.mean(values, axis=1, keepdims=True)
    spread = jnp.mean((values - center) ** 2, axis=1, keepdims=True)
    normed = (values - center) * lax.rsqrt(spread + 1e-06)
    shift = mods[:, :width]
    scale = mods[:, width : 2 * width]
    return (normed * (1.0 + scale) + shift).astype(jnp.bfloat16)


def enter(shards):
    me = lax.axis_index("ctx")
    region = lax.axis_index("region")
    barrier = pltpu.get_barrier_semaphore()
    for d in range(1, shards):
        peer = lax.rem(me + d, shards)
        pl.semaphore_signal(
            barrier, 1, device_id=(region, peer), device_id_type=pl.DeviceIdType.MESH
        )
    pl.semaphore_wait(barrier, shards - 1)


def start_array(a, send, got, send_sem, recv_sem, local_sem, shards):
    me = lax.axis_index("ctx")
    region = lax.axis_index("region")
    local = pltpu.make_async_copy(send.at[me], got.at[me], local_sem.at[a])
    local.start()
    copies = [local]
    for d in range(1, shards):
        peer = lax.rem(me + d, shards)
        remote = pltpu.make_async_remote_copy(
            src_ref=send.at[peer],
            dst_ref=got.at[me],
            send_sem=send_sem.at[a, d - 1],
            recv_sem=recv_sem.at[a, d - 1],
            device_id=(region, peer),
            device_id_type=pl.DeviceIdType.MESH,
        )
        remote.start()
        copies.append(remote)
    return copies


def start_sends(sends, gots, send_sem, recv_sem, local_sem, shards):
    enter(shards)
    copies = []
    for a in range(len(sends)):
        copies += start_array(a, sends[a], gots[a], send_sem, recv_sem, local_sem, shards)
    return copies


def exchange_kernel(*refs, count, shards):
    sends = refs[:count]
    gots = refs[count : 2 * count]
    copies = start_sends(sends, gots, *refs[2 * count :], shards)
    for copy in copies:
        copy.wait()


def send_scratch(count, shards):
    return [
        pltpu.SemaphoreType.DMA((count, shards - 1)),
        pltpu.SemaphoreType.DMA((count, shards - 1)),
        pltpu.SemaphoreType.DMA((count,)),
    ]


def exchange(arrays, shards, collective_id):
    count = len(arrays)
    kernel = functools.partial(exchange_kernel, count=count, shards=shards)
    any_spec = pl.BlockSpec(memory_space=pl.ANY)
    return pl.pallas_call(
        kernel,
        out_shape=[jax.ShapeDtypeStruct(x.shape, x.dtype) for x in arrays],
        in_specs=[any_spec] * count,
        out_specs=[any_spec] * count,
        scratch_shapes=send_scratch(count, shards),
        compiler_params=pltpu.CompilerParams(
            collective_id=collective_id, has_side_effects=True
        ),
    )(*arrays)


def attend_body(
    qt_ref, kt_ref, vt_ref, o_ref, s_scr, k_ref, inv_root, after_block=None, before_block=None,
    first=1,
):
    blocks, head_dim, q_rows = qt_ref.shape
    for c in range(blocks):
        k_ref[c] = kt_ref[c].astype(jnp.float32).T.astype(k_ref.dtype)

    me = lax.axis_index("ctx")

    def one_block(j, carry):
        b = lax.rem(j + me + first, blocks)
        if before_block is not None:
            before_block(j, b)
        qt = qt_ref[b]

        def score(c, m):
            s = jnp.dot(k_ref[c], qt, preferred_element_type=jnp.float32) * inv_root
            s_scr[c] = s
            return jnp.maximum(m, jnp.max(s, axis=0, keepdims=True))

        m = lax.fori_loop(
            0, blocks, score, jnp.full((1, q_rows), -jnp.inf, jnp.float32), unroll=2
        )

        def accumulate(c, inner):
            total, acc = inner
            expo = jnp.exp(s_scr[c] - m)
            total = total + jnp.sum(expo, axis=0, keepdims=True)
            acc = acc + jnp.dot(
                vt_ref[c], expo.astype(jnp.bfloat16), preferred_element_type=jnp.float32
            )
            return total, acc

        total, acc = lax.fori_loop(
            0,
            blocks,
            accumulate,
            (
                jnp.zeros((1, q_rows), jnp.float32),
                jnp.zeros((head_dim, q_rows), jnp.float32),
            ),
            unroll=2,
        )
        o_ref[b] = (acc / total).astype(o_ref.dtype)
        if after_block is not None:
            after_block(b)
        return carry

    lax.fori_loop(0, blocks, one_block, 0)


def attend_send_kernel(*refs, count, shards, inv_root, stream, pull):
    qt_ref, k_ref, vt_ref = refs[:3]
    sends = refs[3 : 3 + count]
    o_ref = refs[3 + count]
    gots = refs[4 + count : 4 + 2 * count]
    rest = refs[4 + 2 * count :]
    if stream:
        back_ref = rest[0]
        rest = rest[1:]
    s_scr, k_scr = rest[0], rest[1]
    rest = rest[1:]
    enter(shards)
    before_block = None
    first = 1
    if pull:
        q_vmem, q_send, q_recv, q_local = rest[7:11] if stream else rest[4:8]
        me_q = lax.axis_index("ctx")
        region_q = lax.axis_index("region")
        q_local_copy = pltpu.make_async_copy(qt_ref.at[me_q], q_vmem.at[me_q], q_local.at[0])
        q_local_copy.start()

        def q_remote(d):
            peer = lax.rem(me_q + d, shards)
            return pltpu.make_async_remote_copy(
                src_ref=qt_ref.at[peer],
                dst_ref=q_vmem.at[me_q],
                send_sem=q_send.at[d - 1],
                recv_sem=q_recv.at[d - 1],
                device_id=(region_q, peer),
                device_id_type=pl.DeviceIdType.MESH,
            )

        for d in range(1, shards):
            q_remote(d).start()

        def before_block(j, b):
            @pl.when(j == 0)
            def _():
                q_local_copy.wait()

            @pl.when(j > 0)
            def _():
                pltpu.make_async_remote_copy(
                    src_ref=qt_ref.at[b],
                    dst_ref=q_vmem.at[b],
                    send_sem=q_send.at[shards - 1 - j],
                    recv_sem=q_recv.at[shards - 1 - j],
                    device_id=(region_q, b),
                    device_id_type=pl.DeviceIdType.MESH,
                ).wait_recv()

        first = 0
        qt_ref = q_vmem
    copies = []
    for a in range(count):
        copies += start_array(a, sends[a], gots[a], *rest[1:4], shards)
    after_block = None
    if stream:
        block_send, block_recv, block_local = rest[4:7]
        me = lax.axis_index("ctx")
        region = lax.axis_index("region")

        def remote_block(b):
            return pltpu.make_async_remote_copy(
                src_ref=o_ref.at[b],
                dst_ref=back_ref.at[me],
                send_sem=block_send.at[b],
                recv_sem=block_recv.at[me],
                device_id=(region, b),
                device_id_type=pl.DeviceIdType.MESH,
            )

        def local_block(b):
            return pltpu.make_async_copy(o_ref.at[b], back_ref.at[b], block_local.at[0])

        def after_block(b):
            @pl.when(b == me)
            def _():
                local_block(b).start()

            @pl.when(b != me)
            def _():
                remote_block(b).start()

    attend_body(
        qt_ref, k_ref, vt_ref, o_ref, s_scr, k_scr, inv_root, after_block, before_block, first
    )
    for copy in copies:
        copy.wait()
    if pull:
        for d in range(1, shards):
            q_remote(d).wait_send()
    if stream:
        for b in range(shards):
            @pl.when(b == me)
            def _():
                local_block(b).wait()

            @pl.when(b != me)
            def _():
                remote_block(b).wait_send()
                pltpu.make_async_remote_copy(
                    src_ref=o_ref.at[b],
                    dst_ref=back_ref.at[b],
                    send_sem=block_send.at[b],
                    recv_sem=block_recv.at[b],
                    device_id=(region, b),
                    device_id_type=pl.DeviceIdType.MESH,
                ).wait_recv()


def attend_send(
    q_t, k_tok, v_t, sends, shards, inv_root, collective_id, stream=False, pull=False
):
    blocks, head_dim, rows = q_t.shape
    count = len(sends)
    kernel = functools.partial(
        attend_send_kernel,
        count=count,
        shards=shards,
        inv_root=inv_root,
        stream=stream,
        pull=pull,
    )
    any_spec = pl.BlockSpec(memory_space=pl.ANY)
    vmem_spec = pl.BlockSpec(memory_space=pltpu.VMEM)
    out_shape = [jax.ShapeDtypeStruct(q_t.shape, jnp.bfloat16)]
    out_shape += [jax.ShapeDtypeStruct(x.shape, x.dtype) for x in sends]
    out_specs = [vmem_spec] + [any_spec] * count
    scratch = [
        pltpu.VMEM((blocks, rows, rows), jnp.float32),
        pltpu.VMEM((blocks, rows, head_dim), jnp.bfloat16),
    ] + send_scratch(count, shards)
    if stream:
        out_shape.append(jax.ShapeDtypeStruct(q_t.shape, jnp.bfloat16))
        out_specs.append(any_spec)
        scratch += [
            pltpu.SemaphoreType.DMA((shards,)),
            pltpu.SemaphoreType.DMA((shards,)),
            pltpu.SemaphoreType.DMA((1,)),
        ]
    if pull:
        scratch += [
            pltpu.VMEM(q_t.shape, q_t.dtype),
            pltpu.SemaphoreType.DMA((shards - 1,)),
            pltpu.SemaphoreType.DMA((shards - 1,)),
            pltpu.SemaphoreType.DMA((1,)),
        ]
    outs = pl.pallas_call(
        kernel,
        out_shape=out_shape,
        in_specs=[any_spec if pull else vmem_spec] + [vmem_spec] * 2 + [any_spec] * count,
        out_specs=out_specs,
        scratch_shapes=scratch,
        compiler_params=pltpu.CompilerParams(
            collective_id=collective_id,
            has_side_effects=True,
            vmem_limit_bytes=48 * 1024 * 1024,
        ),
    )(q_t, k_tok, v_t, *sends)
    return outs[0], outs[1:]


def project_kernel(mod_ref, w_ref, act_ref, wg_ref, bg_ref, *refs, shards, pair, head_dim):
    got0 = refs[:2]
    q0_ref = refs[2]
    later = refs[3 : 3 * pair]
    gate_ref = refs[3 * pair]
    send0 = (q0_ref,) + tuple(refs[3 * pair + 1 : 3 * pair + 3])
    sems = refs[3 * pair + 3 :]
    modulated = mod_ref[...]

    def fill(h, dests, i):
        out_t = lax.dot_general(
            w_ref[i, h],
            modulated,
            (((1,), (1,)), ((), ())),
            preferred_element_type=jnp.float32,
        )
        for p in range(shards):
            piece = out_t[p * head_dim : (p + 1) * head_dim]
            dests[i][p] = piece.astype(jnp.bfloat16)

    enter(shards)
    copies = []
    fill(0, send0, 0)
    for i in range(1, 3):
        fill(0, send0, i)
        copies += start_array(i - 1, send0[i], got0[i - 1], *sems, shards)
    for h in range(1, pair):
        for i in range(3):
            fill(h, later[3 * (h - 1) : 3 * h], i)
    gate = jnp.dot(act_ref[...], wg_ref[...], preferred_element_type=jnp.float32)
    gate_ref[...] = (gate + bg_ref[...]).astype(gate_ref.dtype)
    for copy in copies:
        copy.wait()


def project_send(modulated, w_t, activated, w_gate, b_gate, shards, pair, head_dim):
    rows, width = modulated.shape
    q_shape = jax.ShapeDtypeStruct((shards, head_dim, rows), jnp.bfloat16)
    shapes = [q_shape, q_shape, q_shape]
    kernel = functools.partial(
        project_kernel, shards=shards, pair=pair, head_dim=head_dim
    )
    any_spec = pl.BlockSpec(memory_space=pl.ANY)
    vmem_spec = pl.BlockSpec(memory_space=pltpu.VMEM)
    outs = pl.pallas_call(
        kernel,
        out_shape=shapes * pair
        + [jax.ShapeDtypeStruct((rows, w_gate.shape[1]), jnp.bfloat16)],
        in_specs=[vmem_spec] * 5,
        out_specs=[any_spec] * 2 + [vmem_spec] * (3 * (pair - 1) + 2),
        scratch_shapes=[pltpu.VMEM(x.shape, x.dtype) for x in shapes[1:]]
        + send_scratch(2, shards),
        compiler_params=pltpu.CompilerParams(
            collective_id=pair + 1,
            has_side_effects=True,
            vmem_limit_bytes=48 * 1024 * 1024,
        ),
    )(modulated, w_t, activated, w_gate, b_gate)
    got = (outs[2], outs[0], outs[1])
    return got, [outs[3 * h : 3 * h + 3] for h in range(1, pair)], outs[3 * pair]


def head_pipeline(modulated, w_t, gate_parts, shards, pair, head_dim, inverse_root):
    got, later, gate = project_send(modulated, w_t, *gate_parts, shards, pair, head_dim)
    backs = []
    for h in range(pair):
        last = h + 1 == pair
        sends = [] if last else list(later[h])
        if h > 0:
            sends = sends + [out_prev]
        out_prev, sent = attend_send(
            *got, sends, shards, inverse_root, 1 + h, stream=last, pull=h == 0
        )
        if not last:
            got = sent[:3]
            sent = sent[3:]
        backs.extend(sent)
    return jnp.stack(backs, axis=1), gate


def request_kernel(req_ref, asked_ref, send_sem, recv_sem, local_sem, *, groups, shards):
    total = groups * shards
    me = lax.axis_index("region") * shards + lax.axis_index("ctx")
    mesh_id = pl.DeviceIdType.MESH
    barrier = pltpu.get_barrier_semaphore()

    def greet(d, carry):
        peer = lax.rem(me + d, total)
        pl.semaphore_signal(
            barrier, 1, device_id=(peer // shards, peer % shards), device_id_type=mesh_id
        )
        return carry

    lax.fori_loop(1, total, greet, 0)
    pl.semaphore_wait(barrier, total - 1)
    local = pltpu.make_async_copy(req_ref.at[me], asked_ref.at[me], local_sem.at[0])
    local.start()

    def remote(d):
        peer = lax.rem(me + d, total)
        return pltpu.make_async_remote_copy(
            src_ref=req_ref.at[peer],
            dst_ref=asked_ref.at[me],
            send_sem=send_sem.at[d - 1],
            recv_sem=recv_sem.at[d - 1],
            device_id=(peer // shards, peer % shards),
            device_id_type=mesh_id,
        )

    def launch(d, carry):
        remote(d).start()
        return carry

    def finish(d, carry):
        remote(d).wait()
        return carry

    lax.fori_loop(1, total, launch, 0)
    local.wait()
    lax.fori_loop(1, total, finish, 0)


def exchange_requests(requests, groups, shards):
    total = groups * shards
    any_spec = pl.BlockSpec(memory_space=pl.ANY)
    return pl.pallas_call(
        functools.partial(request_kernel, groups=groups, shards=shards),
        out_shape=jax.ShapeDtypeStruct(requests.shape, requests.dtype),
        in_specs=[any_spec],
        out_specs=any_spec,
        scratch_shapes=[
            pltpu.SemaphoreType.DMA((total - 1,)),
            pltpu.SemaphoreType.DMA((total - 1,)),
            pltpu.SemaphoreType.DMA((1,)),
        ],
        compiler_params=pltpu.CompilerParams(collective_id=7, has_side_effects=True),
    )(requests)


def per_device(
    tokens, element_ids, element_slot, live_count, cond_table, w_ada, b_ada, w_qkv, w_out
):
    device_tokens = tokens[0]
    tok_rows, width = device_tokens.shape
    owners = lax.axis_size(("region", "ctx"))
    shards = lax.axis_size("ctx")
    elem_rows = cond_table.shape[0]
    capacity = -(-max(2, 3 * tok_rows // (2 * owners)) // 8) * 8
    slots = element_slot[element_ids[0]]
    owner_index = slots // elem_rows
    local_row = slots % elem_rows
    position = jnp.arange(tok_rows, dtype=jnp.int32)
    solid = position < live_count[0, 0]
    earlier = (
        (owner_index[:, None] == owner_index[None, :])
        & (position[None, :] < position[:, None])
        & solid[None, :]
    )
    place_rank = jnp.sum(earlier.astype(jnp.int32), axis=1)
    target = jnp.where(solid, owner_index * capacity + place_rank, owners * capacity)
    requests = jnp.zeros((owners * capacity,), jnp.int32).at[target].set(local_row, mode="drop")
    asked = exchange_requests(
        requests.reshape(owners, capacity), owners // shards, shards
    ).reshape(-1)
    pick_at = jnp.minimum(target, owners * capacity - 1)
    served_hot = (asked[:, None] == jnp.arange(elem_rows, dtype=jnp.int32)[None, :]).astype(
        jnp.bfloat16
    )
    served = (
        jnp.dot(served_hot, cond_table, preferred_element_type=jnp.float32)
        .astype(jnp.bfloat16)
        .reshape(owners, capacity, width)
    )
    replies = lax.all_to_all(served, ("region", "ctx"), split_axis=0, concat_axis=0, tiled=True)
    pick_hot = (
        pick_at[:, None] == jnp.arange(owners * capacity, dtype=jnp.int32)[None, :]
    ).astype(jnp.bfloat16)
    picked = jnp.dot(
        pick_hot, replies.reshape(owners * capacity, width), preferred_element_type=jnp.float32
    )
    activated = jnp.where(solid[:, None], jax.nn.silu(picked.astype(jnp.float32)), 0.0).astype(
        jnp.bfloat16
    )
    mods = (
        jnp.dot(activated, w_ada[:, : 2 * width], preferred_element_type=jnp.float32)
        + b_ada[: 2 * width]
    ).astype(jnp.bfloat16)
    mods = mods.astype(jnp.float32)
    gate_parts = (activated, w_ada[:, 2 * width :], b_ada[None, 2 * width :])
    modulated = layer_modulate(device_tokens, mods, width)

    head_dim = width // HEADS
    pair = HEADS // shards
    inverse_root = 1.0 / math.sqrt(head_dim)
    w_t = (
        w_qkv.reshape(width, 3, shards, pair, head_dim)
        .transpose(1, 3, 2, 4, 0)
        .reshape(3, pair, shards * head_dim, width)
    )
    backs, gate = head_pipeline(
        modulated, w_t, gate_parts, shards, pair, head_dim, inverse_root
    )
    w_out_parts = w_out.reshape(shards, pair, head_dim, width)
    projected = jnp.einsum(
        "phet,pheD->tD",
        backs,
        w_out_parts,
        preferred_element_type=jnp.float32,
    )
    gate = gate.astype(jnp.float32)
    output = (device_tokens.astype(jnp.float32) + gate * projected).astype(jnp.bfloat16)
    return output[None]


def solution(mesh):
    placed = (
        P("region", "ctx", None),
        P("region", "ctx"),
        P(),
        P("region", "ctx"),
        P(("region", "ctx"), None),
        P(),
        P(),
        P(),
        P(),
    )
    return jax.shard_map(
        per_device, mesh=mesh, in_specs=placed, out_specs=P("region", "ctx", None), check_vma=False
    )
```

```python
import functools
import math

import jax
import jax.numpy as jnp
from jax import lax
from jax.experimental import pallas as pl
from jax.experimental.pallas import tpu as pltpu
from jax.sharding import PartitionSpec as P

HEADS = 16


def layer_modulate(device_tokens, mods, width):
    values = device_tokens.astype(jnp.float32)
    center = jnp.mean(values, axis=1, keepdims=True)
    spread = jnp.mean((values - center) ** 2, axis=1, keepdims=True)
    normed = (values - center) * lax.rsqrt(spread + 1e-06)
    shift = mods[:, :width]
    scale = mods[:, width : 2 * width]
    return (normed * (1.0 + scale) + shift).astype(jnp.bfloat16)


def enter(shards):
    me = lax.axis_index("ctx")
    region = lax.axis_index("region")
    barrier = pltpu.get_barrier_semaphore()
    for d in range(1, shards):
        peer = lax.rem(me + d, shards)
        pl.semaphore_signal(
            barrier, 1, device_id=(region, peer), device_id_type=pl.DeviceIdType.MESH
        )
    pl.semaphore_wait(barrier, shards - 1)


def start_array(a, send, got, send_sem, recv_sem, local_sem, shards):
    me = lax.axis_index("ctx")
    region = lax.axis_index("region")
    local = pltpu.make_async_copy(send.at[me], got.at[me], local_sem.at[a])
    local.start()
    copies = [local]
    for d in range(1, shards):
        peer = lax.rem(me + d, shards)
        remote = pltpu.make_async_remote_copy(
            src_ref=send.at[peer],
            dst_ref=got.at[me],
            send_sem=send_sem.at[a, d - 1],
            recv_sem=recv_sem.at[a, d - 1],
            device_id=(region, peer),
            device_id_type=pl.DeviceIdType.MESH,
        )
        remote.start()
        copies.append(remote)
    return copies


def start_sends(sends, gots, send_sem, recv_sem, local_sem, shards):
    enter(shards)
    copies = []
    for a in range(len(sends)):
        copies += start_array(a, sends[a], gots[a], send_sem, recv_sem, local_sem, shards)
    return copies


def exchange_kernel(*refs, count, shards):
    sends = refs[:count]
    gots = refs[count : 2 * count]
    copies = start_sends(sends, gots, *refs[2 * count :], shards)
    for copy in copies:
        copy.wait()


def send_scratch(count, shards):
    return [
        pltpu.SemaphoreType.DMA((count, shards - 1)),
        pltpu.SemaphoreType.DMA((count, shards - 1)),
        pltpu.SemaphoreType.DMA((count,)),
    ]


def exchange(arrays, shards, collective_id):
    count = len(arrays)
    kernel = functools.partial(exchange_kernel, count=count, shards=shards)
    any_spec = pl.BlockSpec(memory_space=pl.ANY)
    return pl.pallas_call(
        kernel,
        out_shape=[jax.ShapeDtypeStruct(x.shape, x.dtype) for x in arrays],
        in_specs=[any_spec] * count,
        out_specs=[any_spec] * count,
        scratch_shapes=send_scratch(count, shards),
        compiler_params=pltpu.CompilerParams(
            collective_id=collective_id, has_side_effects=True
        ),
    )(*arrays)


def attend_body(
    qt_ref, kt_ref, vt_ref, o_ref, s_scr, k_ref, inv_root, after_block=None, before_block=None,
    first=1,
):
    blocks, head_dim, q_rows = qt_ref.shape
    for c in range(blocks):
        k_ref[c] = kt_ref[c].astype(jnp.float32).T.astype(k_ref.dtype)

    me = lax.axis_index("ctx")

    def one_block(j, carry):
        if first == 0:
            b = lax.rem(me - j + blocks, blocks)
        else:
            b = lax.rem(j + me + first, blocks)
        if before_block is not None:
            before_block(j, b)
        qt = qt_ref[b]

        def score(c, m):
            s = jnp.dot(k_ref[c], qt, preferred_element_type=jnp.float32) * inv_root
            s_scr[c] = s
            return jnp.maximum(m, jnp.max(s, axis=0, keepdims=True))

        m = lax.fori_loop(
            0, blocks, score, jnp.full((1, q_rows), -jnp.inf, jnp.float32), unroll=2
        )

        def accumulate(c, inner):
            total, acc = inner
            expo = jnp.exp(s_scr[c] - m)
            total = total + jnp.sum(expo, axis=0, keepdims=True)
            acc = acc + jnp.dot(
                vt_ref[c], expo.astype(jnp.bfloat16), preferred_element_type=jnp.float32
            )
            return total, acc

        total, acc = lax.fori_loop(
            0,
            blocks,
            accumulate,
            (
                jnp.zeros((1, q_rows), jnp.float32),
                jnp.zeros((head_dim, q_rows), jnp.float32),
            ),
            unroll=2,
        )
        o_ref[b] = (acc / total).astype(o_ref.dtype)
        if after_block is not None:
            after_block(b)
        return carry

    lax.fori_loop(0, blocks, one_block, 0)


def attend_send_kernel(*refs, count, shards, inv_root, stream, pull):
    qt_ref, k_ref, vt_ref = refs[:3]
    sends = refs[3 : 3 + count]
    o_ref = refs[3 + count]
    gots = refs[4 + count : 4 + 2 * count]
    rest = refs[4 + 2 * count :]
    if stream:
        back_ref = rest[0]
        rest = rest[1:]
    s_scr, k_scr = rest[0], rest[1]
    rest = rest[1:]
    enter(shards)
    before_block = None
    first = 1
    if pull:
        q_vmem, q_send, q_recv, q_local = rest[7:11] if stream else rest[4:8]
        me_q = lax.axis_index("ctx")
        region_q = lax.axis_index("region")
        q_local_copy = pltpu.make_async_copy(qt_ref.at[me_q], q_vmem.at[me_q], q_local.at[0])
        q_local_copy.start()

        def q_remote(d):
            peer = lax.rem(me_q + d, shards)
            return pltpu.make_async_remote_copy(
                src_ref=qt_ref.at[peer],
                dst_ref=q_vmem.at[me_q],
                send_sem=q_send.at[d - 1],
                recv_sem=q_recv.at[d - 1],
                device_id=(region_q, peer),
                device_id_type=pl.DeviceIdType.MESH,
            )

        for d in range(1, shards):
            q_remote(d).start()

        def before_block(j, b):
            @pl.when(j == 0)
            def _():
                q_local_copy.wait()

            @pl.when(j > 0)
            def _():
                pltpu.make_async_remote_copy(
                    src_ref=qt_ref.at[b],
                    dst_ref=q_vmem.at[b],
                    send_sem=q_send.at[j - 1],
                    recv_sem=q_recv.at[j - 1],
                    device_id=(region_q, b),
                    device_id_type=pl.DeviceIdType.MESH,
                ).wait_recv()

        first = 0
        qt_ref = q_vmem
    copies = []
    for a in range(count):
        copies += start_array(a, sends[a], gots[a], *rest[1:4], shards)
    after_block = None
    if stream:
        block_send, block_recv, block_local = rest[4:7]
        me = lax.axis_index("ctx")
        region = lax.axis_index("region")

        def remote_block(b):
            return pltpu.make_async_remote_copy(
                src_ref=o_ref.at[b],
                dst_ref=back_ref.at[me],
                send_sem=block_send.at[b],
                recv_sem=block_recv.at[me],
                device_id=(region, b),
                device_id_type=pl.DeviceIdType.MESH,
            )

        def local_block(b):
            return pltpu.make_async_copy(o_ref.at[b], back_ref.at[b], block_local.at[0])

        def after_block(b):
            @pl.when(b == me)
            def _():
                local_block(b).start()

            @pl.when(b != me)
            def _():
                remote_block(b).start()

    attend_body(
        qt_ref, k_ref, vt_ref, o_ref, s_scr, k_scr, inv_root, after_block, before_block, first
    )
    for copy in copies:
        copy.wait()
    if pull:
        for d in range(1, shards):
            q_remote(d).wait_send()
    if stream:
        for b in range(shards):
            @pl.when(b == me)
            def _():
                local_block(b).wait()

            @pl.when(b != me)
            def _():
                remote_block(b).wait_send()
                pltpu.make_async_remote_copy(
                    src_ref=o_ref.at[b],
                    dst_ref=back_ref.at[b],
                    send_sem=block_send.at[b],
                    recv_sem=block_recv.at[b],
                    device_id=(region, b),
                    device_id_type=pl.DeviceIdType.MESH,
                ).wait_recv()


def attend_send(
    q_t, k_tok, v_t, sends, shards, inv_root, collective_id, stream=False, pull=False
):
    blocks, head_dim, rows = q_t.shape
    count = len(sends)
    kernel = functools.partial(
        attend_send_kernel,
        count=count,
        shards=shards,
        inv_root=inv_root,
        stream=stream,
        pull=pull,
    )
    any_spec = pl.BlockSpec(memory_space=pl.ANY)
    vmem_spec = pl.BlockSpec(memory_space=pltpu.VMEM)
    out_shape = [jax.ShapeDtypeStruct(q_t.shape, jnp.bfloat16)]
    out_shape += [jax.ShapeDtypeStruct(x.shape, x.dtype) for x in sends]
    out_specs = [vmem_spec] + [any_spec] * count
    scratch = [
        pltpu.VMEM((blocks, rows, rows), jnp.float32),
        pltpu.VMEM((blocks, rows, head_dim), jnp.bfloat16),
    ] + send_scratch(count, shards)
    if stream:
        out_shape.append(jax.ShapeDtypeStruct(q_t.shape, jnp.bfloat16))
        out_specs.append(any_spec)
        scratch += [
            pltpu.SemaphoreType.DMA((shards,)),
            pltpu.SemaphoreType.DMA((shards,)),
            pltpu.SemaphoreType.DMA((1,)),
        ]
    if pull:
        scratch += [
            pltpu.VMEM(q_t.shape, q_t.dtype),
            pltpu.SemaphoreType.DMA((shards - 1,)),
            pltpu.SemaphoreType.DMA((shards - 1,)),
            pltpu.SemaphoreType.DMA((1,)),
        ]
    outs = pl.pallas_call(
        kernel,
        out_shape=out_shape,
        in_specs=[any_spec if pull else vmem_spec] + [vmem_spec] * 2 + [any_spec] * count,
        out_specs=out_specs,
        scratch_shapes=scratch,
        compiler_params=pltpu.CompilerParams(
            collective_id=collective_id,
            has_side_effects=True,
            vmem_limit_bytes=48 * 1024 * 1024,
        ),
    )(q_t, k_tok, v_t, *sends)
    return outs[0], outs[1:]


def project_kernel(mod_ref, w_ref, act_ref, wg_ref, bg_ref, *refs, shards, pair, head_dim):
    got0 = refs[:2]
    q0_ref = refs[2]
    later = refs[3 : 3 * pair]
    gate_ref = refs[3 * pair]
    send0 = (q0_ref,) + tuple(refs[3 * pair + 1 : 3 * pair + 3])
    sems = refs[3 * pair + 3 :]
    modulated = mod_ref[...]

    def fill(h, dests, i):
        out_t = lax.dot_general(
            w_ref[i, h],
            modulated,
            (((1,), (1,)), ((), ())),
            preferred_element_type=jnp.float32,
        )
        for p in range(shards):
            piece = out_t[p * head_dim : (p + 1) * head_dim]
            dests[i][p] = piece.astype(jnp.bfloat16)

    enter(shards)
    copies = []
    fill(0, send0, 0)
    for i in range(1, 3):
        fill(0, send0, i)
        copies += start_array(i - 1, send0[i], got0[i - 1], *sems, shards)
    for h in range(1, pair):
        for i in range(3):
            fill(h, later[3 * (h - 1) : 3 * h], i)
    gate = jnp.dot(act_ref[...], wg_ref[...], preferred_element_type=jnp.float32)
    gate_ref[...] = (gate + bg_ref[...]).astype(gate_ref.dtype)
    for copy in copies:
        copy.wait()


def project_send(modulated, w_t, activated, w_gate, b_gate, shards, pair, head_dim):
    rows, width = modulated.shape
    q_shape = jax.ShapeDtypeStruct((shards, head_dim, rows), jnp.bfloat16)
    shapes = [q_shape, q_shape, q_shape]
    kernel = functools.partial(
        project_kernel, shards=shards, pair=pair, head_dim=head_dim
    )
    any_spec = pl.BlockSpec(memory_space=pl.ANY)
    vmem_spec = pl.BlockSpec(memory_space=pltpu.VMEM)
    outs = pl.pallas_call(
        kernel,
        out_shape=shapes * pair
        + [jax.ShapeDtypeStruct((rows, w_gate.shape[1]), jnp.bfloat16)],
        in_specs=[vmem_spec] * 5,
        out_specs=[any_spec] * 2 + [vmem_spec] * (3 * (pair - 1) + 2),
        scratch_shapes=[pltpu.VMEM(x.shape, x.dtype) for x in shapes[1:]]
        + send_scratch(2, shards),
        compiler_params=pltpu.CompilerParams(
            collective_id=pair + 1,
            has_side_effects=True,
            vmem_limit_bytes=48 * 1024 * 1024,
        ),
    )(modulated, w_t, activated, w_gate, b_gate)
    got = (outs[2], outs[0], outs[1])
    return got, [outs[3 * h : 3 * h + 3] for h in range(1, pair)], outs[3 * pair]


def head_pipeline(modulated, w_t, gate_parts, shards, pair, head_dim, inverse_root):
    got, later, gate = project_send(modulated, w_t, *gate_parts, shards, pair, head_dim)
    backs = []
    for h in range(pair):
        last = h + 1 == pair
        sends = [] if last else list(later[h])
        if h > 0:
            sends = sends + [out_prev]
        out_prev, sent = attend_send(
            *got, sends, shards, inverse_root, 1 + h, stream=last, pull=h == 0
        )
        if not last:
            got = sent[:3]
            sent = sent[3:]
        backs.extend(sent)
    return jnp.stack(backs, axis=1), gate


def request_kernel(req_ref, asked_ref, send_sem, recv_sem, local_sem, *, groups, shards):
    total = groups * shards
    me = lax.axis_index("region") * shards + lax.axis_index("ctx")
    mesh_id = pl.DeviceIdType.MESH
    barrier = pltpu.get_barrier_semaphore()

    def greet(d, carry):
        peer = lax.rem(me + d, total)
        pl.semaphore_signal(
            barrier, 1, device_id=(peer // shards, peer % shards), device_id_type=mesh_id
        )
        return carry

    lax.fori_loop(1, total, greet, 0)
    pl.semaphore_wait(barrier, total - 1)
    local = pltpu.make_async_copy(req_ref.at[me], asked_ref.at[me], local_sem.at[0])
    local.start()

    def remote(d):
        peer = lax.rem(me + d, total)
        return pltpu.make_async_remote_copy(
            src_ref=req_ref.at[peer],
            dst_ref=asked_ref.at[me],
            send_sem=send_sem.at[d - 1],
            recv_sem=recv_sem.at[d - 1],
            device_id=(peer // shards, peer % shards),
            device_id_type=mesh_id,
        )

    def launch(d, carry):
        remote(d).start()
        return carry

    def finish(d, carry):
        remote(d).wait()
        return carry

    lax.fori_loop(1, total, launch, 0)
    local.wait()
    lax.fori_loop(1, total, finish, 0)


def exchange_requests(requests, groups, shards):
    total = groups * shards
    any_spec = pl.BlockSpec(memory_space=pl.ANY)
    return pl.pallas_call(
        functools.partial(request_kernel, groups=groups, shards=shards),
        out_shape=jax.ShapeDtypeStruct(requests.shape, requests.dtype),
        in_specs=[any_spec],
        out_specs=any_spec,
        scratch_shapes=[
            pltpu.SemaphoreType.DMA((total - 1,)),
            pltpu.SemaphoreType.DMA((total - 1,)),
            pltpu.SemaphoreType.DMA((1,)),
        ],
        compiler_params=pltpu.CompilerParams(collective_id=7, has_side_effects=True),
    )(requests)


def per_device(
    tokens, element_ids, element_slot, live_count, cond_table, w_ada, b_ada, w_qkv, w_out
):
    device_tokens = tokens[0]
    tok_rows, width = device_tokens.shape
    owners = lax.axis_size(("region", "ctx"))
    shards = lax.axis_size("ctx")
    elem_rows = cond_table.shape[0]
    capacity = -(-max(2, 3 * tok_rows // (2 * owners)) // 8) * 8
    slots = element_slot[element_ids[0]]
    owner_index = slots // elem_rows
    local_row = slots % elem_rows
    position = jnp.arange(tok_rows, dtype=jnp.int32)
    solid = position < live_count[0, 0]
    earlier = (
        (owner_index[:, None] == owner_index[None, :])
        & (position[None, :] < position[:, None])
        & solid[None, :]
    )
    place_rank = jnp.sum(earlier.astype(jnp.int32), axis=1)
    target = jnp.where(solid, owner_index * capacity + place_rank, owners * capacity)
    requests = jnp.zeros((owners * capacity,), jnp.int32).at[target].set(local_row, mode="drop")
    asked = exchange_requests(
        requests.reshape(owners, capacity), owners // shards, shards
    ).reshape(-1)
    pick_at = jnp.minimum(target, owners * capacity - 1)
    served_hot = (asked[:, None] == jnp.arange(elem_rows, dtype=jnp.int32)[None, :]).astype(
        jnp.bfloat16
    )
    served = (
        jnp.dot(served_hot, cond_table, preferred_element_type=jnp.float32)
        .astype(jnp.bfloat16)
        .reshape(owners, capacity, width)
    )
    replies = lax.all_to_all(served, ("region", "ctx"), split_axis=0, concat_axis=0, tiled=True)
    pick_hot = (
        pick_at[:, None] == jnp.arange(owners * capacity, dtype=jnp.int32)[None, :]
    ).astype(jnp.bfloat16)
    picked = jnp.dot(
        pick_hot, replies.reshape(owners * capacity, width), preferred_element_type=jnp.float32
    )
    activated = jnp.where(solid[:, None], jax.nn.silu(picked.astype(jnp.float32)), 0.0).astype(
        jnp.bfloat16
    )
    mods = (
        jnp.dot(activated, w_ada[:, : 2 * width], preferred_element_type=jnp.float32)
        + b_ada[: 2 * width]
    ).astype(jnp.bfloat16)
    mods = mods.astype(jnp.float32)
    gate_parts = (activated, w_ada[:, 2 * width :], b_ada[None, 2 * width :])
    modulated = layer_modulate(device_tokens, mods, width)

    head_dim = width // HEADS
    pair = HEADS // shards
    inverse_root = 1.0 / math.sqrt(head_dim)
    w_t = (
        w_qkv.reshape(width, 3, shards, pair, head_dim)
        .transpose(1, 3, 2, 4, 0)
        .reshape(3, pair, shards * head_dim, width)
    )
    backs, gate = head_pipeline(
        modulated, w_t, gate_parts, shards, pair, head_dim, inverse_root
    )
    w_out_parts = w_out.reshape(shards, pair, head_dim, width)
    projected = jnp.einsum(
        "phet,pheD->tD",
        backs,
        w_out_parts,
        preferred_element_type=jnp.float32,
    )
    gate = gate.astype(jnp.float32)
    output = (device_tokens.astype(jnp.float32) + gate * projected).astype(jnp.bfloat16)
    return output[None]


def solution(mesh):
    placed = (
        P("region", "ctx", None),
        P("region", "ctx"),
        P(),
        P("region", "ctx"),
        P(("region", "ctx"), None),
        P(),
        P(),
        P(),
        P(),
    )
    return jax.shard_map(
        per_device, mesh=mesh, in_specs=placed, out_specs=P("region", "ctx", None), check_vma=False
    )
```

```python
import functools
import math

import jax
import jax.numpy as jnp
from jax import lax
from jax.experimental import pallas as pl
from jax.experimental.pallas import tpu as pltpu
from jax.sharding import PartitionSpec as P

HEADS = 16


def layer_modulate(device_tokens, mods, width):
    values = device_tokens.astype(jnp.float32)
    center = jnp.mean(values, axis=1, keepdims=True)
    spread = jnp.mean((values - center) ** 2, axis=1, keepdims=True)
    normed = (values - center) * lax.rsqrt(spread + 1e-06)
    shift = mods[:, :width]
    scale = mods[:, width : 2 * width]
    return (normed * (1.0 + scale) + shift).astype(jnp.bfloat16)


def enter(shards):
    me = lax.axis_index("ctx")
    region = lax.axis_index("region")
    barrier = pltpu.get_barrier_semaphore()
    for d in range(1, shards):
        peer = lax.rem(me + d, shards)
        pl.semaphore_signal(
            barrier, 1, device_id=(region, peer), device_id_type=pl.DeviceIdType.MESH
        )
    pl.semaphore_wait(barrier, shards - 1)


def start_array(a, send, got, send_sem, recv_sem, local_sem, shards):
    me = lax.axis_index("ctx")
    region = lax.axis_index("region")
    local = pltpu.make_async_copy(send.at[me], got.at[me], local_sem.at[a])
    local.start()
    copies = [local]
    for d in range(1, shards):
        peer = lax.rem(me + d, shards)
        remote = pltpu.make_async_remote_copy(
            src_ref=send.at[peer],
            dst_ref=got.at[me],
            send_sem=send_sem.at[a, d - 1],
            recv_sem=recv_sem.at[a, d - 1],
            device_id=(region, peer),
            device_id_type=pl.DeviceIdType.MESH,
        )
        remote.start()
        copies.append(remote)
    return copies


def start_sends(sends, gots, send_sem, recv_sem, local_sem, shards):
    enter(shards)
    copies = []
    for a in range(len(sends)):
        copies += start_array(a, sends[a], gots[a], send_sem, recv_sem, local_sem, shards)
    return copies


def exchange_kernel(*refs, count, shards):
    sends = refs[:count]
    gots = refs[count : 2 * count]
    copies = start_sends(sends, gots, *refs[2 * count :], shards)
    for copy in copies:
        copy.wait()


def send_scratch(count, shards):
    return [
        pltpu.SemaphoreType.DMA((count, shards - 1)),
        pltpu.SemaphoreType.DMA((count, shards - 1)),
        pltpu.SemaphoreType.DMA((count,)),
    ]


def exchange(arrays, shards, collective_id):
    count = len(arrays)
    kernel = functools.partial(exchange_kernel, count=count, shards=shards)
    any_spec = pl.BlockSpec(memory_space=pl.ANY)
    return pl.pallas_call(
        kernel,
        out_shape=[jax.ShapeDtypeStruct(x.shape, x.dtype) for x in arrays],
        in_specs=[any_spec] * count,
        out_specs=[any_spec] * count,
        scratch_shapes=send_scratch(count, shards),
        compiler_params=pltpu.CompilerParams(
            collective_id=collective_id, has_side_effects=True
        ),
    )(*arrays)


def attend_body(
    qt_ref, kt_ref, vt_ref, o_ref, s_scr, k_ref, inv_root, after_block=None, before_block=None,
    first=1,
):
    blocks, head_dim, q_rows = qt_ref.shape
    for c in range(blocks):
        k_ref[c] = kt_ref[c].astype(jnp.float32).T.astype(k_ref.dtype)

    me = lax.axis_index("ctx")

    def one_block(j, carry):
        if first == 0:
            b = lax.rem(me - j + blocks, blocks)
        else:
            b = lax.rem(j + me + first, blocks)
        if before_block is not None:
            before_block(j, b)
        qt = qt_ref[b]

        def score(c, m):
            s = jnp.dot(k_ref[c], qt, preferred_element_type=jnp.float32) * inv_root
            s_scr[c] = s
            return jnp.maximum(m, jnp.max(s, axis=0, keepdims=True))

        m = lax.fori_loop(
            0, blocks, score, jnp.full((1, q_rows), -jnp.inf, jnp.float32), unroll=2
        )

        def accumulate(c, inner):
            total, acc = inner
            expo = jnp.exp(s_scr[c] - m)
            total = total + jnp.sum(expo, axis=0, keepdims=True)
            acc = acc + jnp.dot(
                vt_ref[c], expo.astype(jnp.bfloat16), preferred_element_type=jnp.float32
            )
            return total, acc

        total, acc = lax.fori_loop(
            0,
            blocks,
            accumulate,
            (
                jnp.zeros((1, q_rows), jnp.float32),
                jnp.zeros((head_dim, q_rows), jnp.float32),
            ),
            unroll=2,
        )
        o_ref[b] = (acc / total).astype(o_ref.dtype)
        if after_block is not None:
            after_block(b)
        return carry

    lax.fori_loop(0, blocks, one_block, 0)


def attend_send_kernel(*refs, count, shards, inv_root, stream, pull):
    qt_ref, k_ref, vt_ref = refs[:3]
    sends = refs[3 : 3 + count]
    o_ref = refs[3 + count]
    gots = refs[4 + count : 4 + 2 * count]
    rest = refs[4 + 2 * count :]
    if stream:
        back_ref = rest[0]
        rest = rest[1:]
    s_scr, k_scr = rest[0], rest[1]
    rest = rest[1:]
    enter(shards)
    before_block = None
    first = 1
    if pull:
        q_vmem, q_send, q_recv, q_local = rest[7:11] if stream else rest[4:8]
        me_q = lax.axis_index("ctx")
        region_q = lax.axis_index("region")
        q_local_copy = pltpu.make_async_copy(qt_ref.at[me_q], q_vmem.at[me_q], q_local.at[0])
        q_local_copy.start()

        def q_remote(d):
            peer = lax.rem(me_q + d, shards)
            return pltpu.make_async_remote_copy(
                src_ref=qt_ref.at[peer],
                dst_ref=q_vmem.at[me_q],
                send_sem=q_send.at[d - 1],
                recv_sem=q_recv.at[d - 1],
                device_id=(region_q, peer),
                device_id_type=pl.DeviceIdType.MESH,
            )

        for d in range(1, shards):
            q_remote(d).start()

        def before_block(j, b):
            @pl.when(j == 0)
            def _():
                q_local_copy.wait()

            @pl.when(j > 0)
            def _():
                pltpu.make_async_remote_copy(
                    src_ref=qt_ref.at[b],
                    dst_ref=q_vmem.at[b],
                    send_sem=q_send.at[j - 1],
                    recv_sem=q_recv.at[j - 1],
                    device_id=(region_q, b),
                    device_id_type=pl.DeviceIdType.MESH,
                ).wait_recv()

        first = 0
        qt_ref = q_vmem
    copies = []
    for a in range(count):
        copies += start_array(a, sends[a], gots[a], *rest[1:4], shards)
    after_block = None
    if stream:
        block_send, block_recv, block_local = rest[4:7]
        me = lax.axis_index("ctx")
        region = lax.axis_index("region")

        def remote_block(b):
            return pltpu.make_async_remote_copy(
                src_ref=o_ref.at[b],
                dst_ref=back_ref.at[me],
                send_sem=block_send.at[b],
                recv_sem=block_recv.at[me],
                device_id=(region, b),
                device_id_type=pl.DeviceIdType.MESH,
            )

        def local_block(b):
            return pltpu.make_async_copy(o_ref.at[b], back_ref.at[b], block_local.at[0])

        def after_block(b):
            @pl.when(b == me)
            def _():
                local_block(b).start()

            @pl.when(b != me)
            def _():
                remote_block(b).start()

    attend_body(
        qt_ref, k_ref, vt_ref, o_ref, s_scr, k_scr, inv_root, after_block, before_block, first
    )
    for copy in copies:
        copy.wait()
    if pull:
        for d in range(1, shards):
            q_remote(d).wait_send()
    if stream:
        for b in range(shards):
            @pl.when(b == me)
            def _():
                local_block(b).wait()

            @pl.when(b != me)
            def _():
                remote_block(b).wait_send()
                pltpu.make_async_remote_copy(
                    src_ref=o_ref.at[b],
                    dst_ref=back_ref.at[b],
                    send_sem=block_send.at[b],
                    recv_sem=block_recv.at[b],
                    device_id=(region, b),
                    device_id_type=pl.DeviceIdType.MESH,
                ).wait_recv()


def attend_send(
    q_t, k_tok, v_t, sends, shards, inv_root, collective_id, stream=False, pull=False
):
    blocks, head_dim, rows = q_t.shape
    count = len(sends)
    kernel = functools.partial(
        attend_send_kernel,
        count=count,
        shards=shards,
        inv_root=inv_root,
        stream=stream,
        pull=pull,
    )
    any_spec = pl.BlockSpec(memory_space=pl.ANY)
    vmem_spec = pl.BlockSpec(memory_space=pltpu.VMEM)
    out_shape = [jax.ShapeDtypeStruct(q_t.shape, jnp.bfloat16)]
    out_shape += [jax.ShapeDtypeStruct(x.shape, x.dtype) for x in sends]
    out_specs = [vmem_spec] + [any_spec] * count
    scratch = [
        pltpu.VMEM((blocks, rows, rows), jnp.float32),
        pltpu.VMEM((blocks, rows, head_dim), jnp.bfloat16),
    ] + send_scratch(count, shards)
    if stream:
        out_shape.append(jax.ShapeDtypeStruct(q_t.shape, jnp.bfloat16))
        out_specs.append(any_spec)
        scratch += [
            pltpu.SemaphoreType.DMA((shards,)),
            pltpu.SemaphoreType.DMA((shards,)),
            pltpu.SemaphoreType.DMA((1,)),
        ]
    if pull:
        scratch += [
            pltpu.VMEM(q_t.shape, q_t.dtype),
            pltpu.SemaphoreType.DMA((shards - 1,)),
            pltpu.SemaphoreType.DMA((shards - 1,)),
            pltpu.SemaphoreType.DMA((1,)),
        ]
    outs = pl.pallas_call(
        kernel,
        out_shape=out_shape,
        in_specs=[any_spec if pull else vmem_spec] + [vmem_spec] * 2 + [any_spec] * count,
        out_specs=out_specs,
        scratch_shapes=scratch,
        compiler_params=pltpu.CompilerParams(
            collective_id=collective_id,
            has_side_effects=True,
            vmem_limit_bytes=48 * 1024 * 1024,
        ),
    )(q_t, k_tok, v_t, *sends)
    return outs[0], outs[1:]


def project_kernel(mod_ref, w_ref, act_ref, wg_ref, bg_ref, *refs, shards, pair, head_dim):
    got0 = refs[:2]
    q0_ref = refs[2]
    later = refs[3 : 3 * pair]
    gate_ref = refs[3 * pair]
    send0 = (q0_ref,) + tuple(refs[3 * pair + 1 : 3 * pair + 3])
    sems = refs[3 * pair + 3 :]
    modulated = mod_ref[...]

    def fill(h, dests, i):
        out_t = lax.dot_general(
            w_ref[i, h],
            modulated,
            (((1,), (1,)), ((), ())),
            preferred_element_type=jnp.float32,
        )
        for p in range(shards):
            piece = out_t[p * head_dim : (p + 1) * head_dim]
            dests[i][p] = piece.astype(jnp.bfloat16)

    enter(shards)
    copies = []
    for i in range(1, 3):
        fill(0, send0, i)
        copies += start_array(i - 1, send0[i], got0[i - 1], *sems, shards)
    fill(0, send0, 0)
    for h in range(1, pair):
        for i in range(3):
            fill(h, later[3 * (h - 1) : 3 * h], i)
    gate = jnp.dot(act_ref[...], wg_ref[...], preferred_element_type=jnp.float32)
    gate_ref[...] = (gate + bg_ref[...]).astype(gate_ref.dtype)
    for copy in copies:
        copy.wait()


def project_send(modulated, w_t, activated, w_gate, b_gate, shards, pair, head_dim):
    rows, width = modulated.shape
    q_shape = jax.ShapeDtypeStruct((shards, head_dim, rows), jnp.bfloat16)
    shapes = [q_shape, q_shape, q_shape]
    kernel = functools.partial(
        project_kernel, shards=shards, pair=pair, head_dim=head_dim
    )
    any_spec = pl.BlockSpec(memory_space=pl.ANY)
    vmem_spec = pl.BlockSpec(memory_space=pltpu.VMEM)
    outs = pl.pallas_call(
        kernel,
        out_shape=shapes * pair
        + [jax.ShapeDtypeStruct((rows, w_gate.shape[1]), jnp.bfloat16)],
        in_specs=[vmem_spec] * 5,
        out_specs=[any_spec] * 2 + [vmem_spec] * (3 * (pair - 1) + 2),
        scratch_shapes=[pltpu.VMEM(x.shape, x.dtype) for x in shapes[1:]]
        + send_scratch(2, shards),
        compiler_params=pltpu.CompilerParams(
            collective_id=pair + 1,
            has_side_effects=True,
            vmem_limit_bytes=48 * 1024 * 1024,
        ),
    )(modulated, w_t, activated, w_gate, b_gate)
    got = (outs[2], outs[0], outs[1])
    return got, [outs[3 * h : 3 * h + 3] for h in range(1, pair)], outs[3 * pair]


def head_pipeline(modulated, w_t, gate_parts, shards, pair, head_dim, inverse_root):
    got, later, gate = project_send(modulated, w_t, *gate_parts, shards, pair, head_dim)
    backs = []
    for h in range(pair):
        last = h + 1 == pair
        sends = [] if last else list(later[h])
        if h > 0:
            sends = sends + [out_prev]
        out_prev, sent = attend_send(
            *got, sends, shards, inverse_root, 1 + h, stream=last, pull=h == 0
        )
        if not last:
            got = sent[:3]
            sent = sent[3:]
        backs.extend(sent)
    return jnp.stack(backs, axis=1), gate


def request_kernel(req_ref, asked_ref, send_sem, recv_sem, local_sem, *, groups, shards):
    total = groups * shards
    me = lax.axis_index("region") * shards + lax.axis_index("ctx")
    mesh_id = pl.DeviceIdType.MESH
    barrier = pltpu.get_barrier_semaphore()

    def greet(d, carry):
        peer = lax.rem(me + d, total)
        pl.semaphore_signal(
            barrier, 1, device_id=(peer // shards, peer % shards), device_id_type=mesh_id
        )
        return carry

    lax.fori_loop(1, total, greet, 0)
    pl.semaphore_wait(barrier, total - 1)
    local = pltpu.make_async_copy(req_ref.at[me], asked_ref.at[me], local_sem.at[0])
    local.start()

    def remote(d):
        peer = lax.rem(me + d, total)
        return pltpu.make_async_remote_copy(
            src_ref=req_ref.at[peer],
            dst_ref=asked_ref.at[me],
            send_sem=send_sem.at[d - 1],
            recv_sem=recv_sem.at[d - 1],
            device_id=(peer // shards, peer % shards),
            device_id_type=mesh_id,
        )

    def launch(d, carry):
        remote(d).start()
        return carry

    def finish(d, carry):
        remote(d).wait()
        return carry

    lax.fori_loop(1, total, launch, 0)
    local.wait()
    lax.fori_loop(1, total, finish, 0)


def exchange_requests(requests, groups, shards):
    total = groups * shards
    any_spec = pl.BlockSpec(memory_space=pl.ANY)
    return pl.pallas_call(
        functools.partial(request_kernel, groups=groups, shards=shards),
        out_shape=jax.ShapeDtypeStruct(requests.shape, requests.dtype),
        in_specs=[any_spec],
        out_specs=any_spec,
        scratch_shapes=[
            pltpu.SemaphoreType.DMA((total - 1,)),
            pltpu.SemaphoreType.DMA((total - 1,)),
            pltpu.SemaphoreType.DMA((1,)),
        ],
        compiler_params=pltpu.CompilerParams(collective_id=7, has_side_effects=True),
    )(requests)


def per_device(
    tokens, element_ids, element_slot, live_count, cond_table, w_ada, b_ada, w_qkv, w_out
):
    device_tokens = tokens[0]
    tok_rows, width = device_tokens.shape
    owners = lax.axis_size(("region", "ctx"))
    shards = lax.axis_size("ctx")
    elem_rows = cond_table.shape[0]
    capacity = -(-max(2, 3 * tok_rows // (2 * owners)) // 8) * 8
    slots = element_slot[element_ids[0]]
    owner_index = slots // elem_rows
    local_row = slots % elem_rows
    position = jnp.arange(tok_rows, dtype=jnp.int32)
    solid = position < live_count[0, 0]
    earlier = (
        (owner_index[:, None] == owner_index[None, :])
        & (position[None, :] < position[:, None])
        & solid[None, :]
    )
    place_rank = jnp.sum(earlier.astype(jnp.int32), axis=1)
    target = jnp.where(solid, owner_index * capacity + place_rank, owners * capacity)
    requests = jnp.zeros((owners * capacity,), jnp.int32).at[target].set(local_row, mode="drop")
    asked = exchange_requests(
        requests.reshape(owners, capacity), owners // shards, shards
    ).reshape(-1)
    pick_at = jnp.minimum(target, owners * capacity - 1)
    served_hot = (asked[:, None] == jnp.arange(elem_rows, dtype=jnp.int32)[None, :]).astype(
        jnp.bfloat16
    )
    served = (
        jnp.dot(served_hot, cond_table, preferred_element_type=jnp.float32)
        .astype(jnp.bfloat16)
        .reshape(owners, capacity, width)
    )
    replies = lax.all_to_all(served, ("region", "ctx"), split_axis=0, concat_axis=0, tiled=True)
    pick_hot = (
        pick_at[:, None] == jnp.arange(owners * capacity, dtype=jnp.int32)[None, :]
    ).astype(jnp.bfloat16)
    picked = jnp.dot(
        pick_hot, replies.reshape(owners * capacity, width), preferred_element_type=jnp.float32
    )
    activated = jnp.where(solid[:, None], jax.nn.silu(picked.astype(jnp.float32)), 0.0).astype(
        jnp.bfloat16
    )
    mods = (
        jnp.dot(activated, w_ada[:, : 2 * width], preferred_element_type=jnp.float32)
        + b_ada[: 2 * width]
    ).astype(jnp.bfloat16)
    mods = mods.astype(jnp.float32)
    gate_parts = (activated, w_ada[:, 2 * width :], b_ada[None, 2 * width :])
    modulated = layer_modulate(device_tokens, mods, width)

    head_dim = width // HEADS
    pair = HEADS // shards
    inverse_root = 1.0 / math.sqrt(head_dim)
    w_t = (
        w_qkv.reshape(width, 3, shards, pair, head_dim)
        .transpose(1, 3, 2, 4, 0)
        .reshape(3, pair, shards * head_dim, width)
    )
    backs, gate = head_pipeline(
        modulated, w_t, gate_parts, shards, pair, head_dim, inverse_root
    )
    w_out_parts = w_out.reshape(shards, pair, head_dim, width)
    projected = jnp.einsum(
        "phet,pheD->tD",
        backs,
        w_out_parts,
        preferred_element_type=jnp.float32,
    )
    gate = gate.astype(jnp.float32)
    output = (device_tokens.astype(jnp.float32) + gate * projected).astype(jnp.bfloat16)
    return output[None]


def solution(mesh):
    placed = (
        P("region", "ctx", None),
        P("region", "ctx"),
        P(),
        P("region", "ctx"),
        P(("region", "ctx"), None),
        P(),
        P(),
        P(),
        P(),
    )
    return jax.shard_map(
        per_device, mesh=mesh, in_specs=placed, out_specs=P("region", "ctx", None), check_vma=False
    )
```

```python
import functools
import math

import jax
import jax.numpy as jnp
from jax import lax
from jax.experimental import pallas as pl
from jax.experimental.pallas import tpu as pltpu
from jax.sharding import PartitionSpec as P

HEADS = 16


def layer_modulate(device_tokens, mods, width):
    values = device_tokens.astype(jnp.float32)
    center = jnp.mean(values, axis=1, keepdims=True)
    spread = jnp.mean((values - center) ** 2, axis=1, keepdims=True)
    normed = (values - center) * lax.rsqrt(spread + 1e-06)
    shift = mods[:, :width]
    scale = mods[:, width : 2 * width]
    return (normed * (1.0 + scale) + shift).astype(jnp.bfloat16)


def enter(shards):
    me = lax.axis_index("ctx")
    region = lax.axis_index("region")
    barrier = pltpu.get_barrier_semaphore()
    for d in range(1, shards):
        peer = lax.rem(me + d, shards)
        pl.semaphore_signal(
            barrier, 1, device_id=(region, peer), device_id_type=pl.DeviceIdType.MESH
        )
    pl.semaphore_wait(barrier, shards - 1)


def start_array(a, send, got, send_sem, recv_sem, local_sem, shards):
    me = lax.axis_index("ctx")
    region = lax.axis_index("region")
    local = pltpu.make_async_copy(send.at[me], got.at[me], local_sem.at[a])
    local.start()
    copies = [local]
    for d in range(1, shards):
        peer = lax.rem(me + d, shards)
        remote = pltpu.make_async_remote_copy(
            src_ref=send.at[peer],
            dst_ref=got.at[me],
            send_sem=send_sem.at[a, d - 1],
            recv_sem=recv_sem.at[a, d - 1],
            device_id=(region, peer),
            device_id_type=pl.DeviceIdType.MESH,
        )
        remote.start()
        copies.append(remote)
    return copies


def start_sends(sends, gots, send_sem, recv_sem, local_sem, shards):
    enter(shards)
    copies = []
    for a in range(len(sends)):
        copies += start_array(a, sends[a], gots[a], send_sem, recv_sem, local_sem, shards)
    return copies


def exchange_kernel(*refs, count, shards):
    sends = refs[:count]
    gots = refs[count : 2 * count]
    copies = start_sends(sends, gots, *refs[2 * count :], shards)
    for copy in copies:
        copy.wait()


def send_scratch(count, shards):
    return [
        pltpu.SemaphoreType.DMA((count, shards - 1)),
        pltpu.SemaphoreType.DMA((count, shards - 1)),
        pltpu.SemaphoreType.DMA((count,)),
    ]


def exchange(arrays, shards, collective_id):
    count = len(arrays)
    kernel = functools.partial(exchange_kernel, count=count, shards=shards)
    any_spec = pl.BlockSpec(memory_space=pl.ANY)
    return pl.pallas_call(
        kernel,
        out_shape=[jax.ShapeDtypeStruct(x.shape, x.dtype) for x in arrays],
        in_specs=[any_spec] * count,
        out_specs=[any_spec] * count,
        scratch_shapes=send_scratch(count, shards),
        compiler_params=pltpu.CompilerParams(
            collective_id=collective_id, has_side_effects=True
        ),
    )(*arrays)


def attend_body(
    qt_ref, kt_ref, vt_ref, o_ref, s_scr, k_ref, inv_root, after_block=None, before_block=None,
    first=1, span=None, between=None,
):
    blocks, head_dim, q_rows = qt_ref.shape
    for c in range(blocks):
        k_ref[c] = kt_ref[c].astype(jnp.float32).T.astype(k_ref.dtype)

    me = lax.axis_index("ctx")

    def one_block(j, carry):
        if first == 0:
            b = lax.rem(me - j + blocks, blocks)
        else:
            b = lax.rem(j + me + first, blocks)
        if before_block is not None:
            before_block(j, b)
        qt = qt_ref[b]

        def score(c, m):
            s = jnp.dot(k_ref[c], qt, preferred_element_type=jnp.float32) * inv_root
            s_scr[c] = s
            return jnp.maximum(m, jnp.max(s, axis=0, keepdims=True))

        m = lax.fori_loop(
            0, blocks, score, jnp.full((1, q_rows), -jnp.inf, jnp.float32), unroll=2
        )

        def accumulate(c, inner):
            total, acc = inner
            expo = jnp.exp(s_scr[c] - m)
            total = total + jnp.sum(expo, axis=0, keepdims=True)
            acc = acc + jnp.dot(
                vt_ref[c], expo.astype(jnp.bfloat16), preferred_element_type=jnp.float32
            )
            return total, acc

        total, acc = lax.fori_loop(
            0,
            blocks,
            accumulate,
            (
                jnp.zeros((1, q_rows), jnp.float32),
                jnp.zeros((head_dim, q_rows), jnp.float32),
            ),
            unroll=2,
        )
        o_ref[b] = (acc / total).astype(o_ref.dtype)
        if after_block is not None:
            after_block(b)
        return carry

    if between is None:
        lax.fori_loop(0, blocks, one_block, 0)
    else:
        lax.fori_loop(0, span, one_block, 0)
        between()
        lax.fori_loop(span, blocks, one_block, 0)


def attend_send_kernel(*refs, count, shards, inv_root, stream, pull):
    qt_ref, k_ref, vt_ref = refs[:3]
    sends = refs[3 : 3 + count]
    o_ref = refs[3 + count]
    gots = refs[4 + count : 4 + 2 * count]
    rest = refs[4 + 2 * count :]
    if stream:
        back_ref = rest[0]
        rest = rest[1:]
    s_scr, k_scr = rest[0], rest[1]
    rest = rest[1:]
    enter(shards)
    before_block = None
    first = 1
    if pull:
        q_vmem, q_send, q_recv, q_local = rest[7:11] if stream else rest[4:8]
        me_q = lax.axis_index("ctx")
        region_q = lax.axis_index("region")
        q_local_copy = pltpu.make_async_copy(qt_ref.at[me_q], q_vmem.at[me_q], q_local.at[0])
        q_local_copy.start()

        def q_remote(d):
            peer = lax.rem(me_q + d, shards)
            return pltpu.make_async_remote_copy(
                src_ref=qt_ref.at[peer],
                dst_ref=q_vmem.at[me_q],
                send_sem=q_send.at[d - 1],
                recv_sem=q_recv.at[d - 1],
                device_id=(region_q, peer),
                device_id_type=pl.DeviceIdType.MESH,
            )

        for d in range(1, shards):
            q_remote(d).start()

        def before_block(j, b):
            @pl.when(j == 0)
            def _():
                q_local_copy.wait()

            @pl.when(j > 0)
            def _():
                pltpu.make_async_remote_copy(
                    src_ref=qt_ref.at[b],
                    dst_ref=q_vmem.at[b],
                    send_sem=q_send.at[j - 1],
                    recv_sem=q_recv.at[j - 1],
                    device_id=(region_q, b),
                    device_id_type=pl.DeviceIdType.MESH,
                ).wait_recv()

        first = 0
        qt_ref = q_vmem
    copies = []

    def launch():
        for a in range(count):
            copies.extend(start_array(a, sends[a], gots[a], *rest[1:4], shards))

    between = None
    if pull:
        between = launch
    else:
        launch()
    after_block = None
    if stream:
        block_send, block_recv, block_local = rest[4:7]
        me = lax.axis_index("ctx")
        region = lax.axis_index("region")

        def remote_block(b):
            return pltpu.make_async_remote_copy(
                src_ref=o_ref.at[b],
                dst_ref=back_ref.at[me],
                send_sem=block_send.at[b],
                recv_sem=block_recv.at[me],
                device_id=(region, b),
                device_id_type=pl.DeviceIdType.MESH,
            )

        def local_block(b):
            return pltpu.make_async_copy(o_ref.at[b], back_ref.at[b], block_local.at[0])

        def after_block(b):
            @pl.when(b == me)
            def _():
                local_block(b).start()

            @pl.when(b != me)
            def _():
                remote_block(b).start()

    attend_body(
        qt_ref, k_ref, vt_ref, o_ref, s_scr, k_scr, inv_root, after_block, before_block, first,
        span=1, between=between,
    )
    for copy in copies:
        copy.wait()
    if pull:
        for d in range(1, shards):
            q_remote(d).wait_send()
    if stream:
        for b in range(shards):
            @pl.when(b == me)
            def _():
                local_block(b).wait()

            @pl.when(b != me)
            def _():
                remote_block(b).wait_send()
                pltpu.make_async_remote_copy(
                    src_ref=o_ref.at[b],
                    dst_ref=back_ref.at[b],
                    send_sem=block_send.at[b],
                    recv_sem=block_recv.at[b],
                    device_id=(region, b),
                    device_id_type=pl.DeviceIdType.MESH,
                ).wait_recv()


def attend_send(
    q_t, k_tok, v_t, sends, shards, inv_root, collective_id, stream=False, pull=False
):
    blocks, head_dim, rows = q_t.shape
    count = len(sends)
    kernel = functools.partial(
        attend_send_kernel,
        count=count,
        shards=shards,
        inv_root=inv_root,
        stream=stream,
        pull=pull,
    )
    any_spec = pl.BlockSpec(memory_space=pl.ANY)
    vmem_spec = pl.BlockSpec(memory_space=pltpu.VMEM)
    out_shape = [jax.ShapeDtypeStruct(q_t.shape, jnp.bfloat16)]
    out_shape += [jax.ShapeDtypeStruct(x.shape, x.dtype) for x in sends]
    out_specs = [vmem_spec] + [any_spec] * count
    scratch = [
        pltpu.VMEM((blocks, rows, rows), jnp.float32),
        pltpu.VMEM((blocks, rows, head_dim), jnp.bfloat16),
    ] + send_scratch(count, shards)
    if stream:
        out_shape.append(jax.ShapeDtypeStruct(q_t.shape, jnp.bfloat16))
        out_specs.append(any_spec)
        scratch += [
            pltpu.SemaphoreType.DMA((shards,)),
            pltpu.SemaphoreType.DMA((shards,)),
            pltpu.SemaphoreType.DMA((1,)),
        ]
    if pull:
        scratch += [
            pltpu.VMEM(q_t.shape, q_t.dtype),
            pltpu.SemaphoreType.DMA((shards - 1,)),
            pltpu.SemaphoreType.DMA((shards - 1,)),
            pltpu.SemaphoreType.DMA((1,)),
        ]
    outs = pl.pallas_call(
        kernel,
        out_shape=out_shape,
        in_specs=[any_spec if pull else vmem_spec] + [vmem_spec] * 2 + [any_spec] * count,
        out_specs=out_specs,
        scratch_shapes=scratch,
        compiler_params=pltpu.CompilerParams(
            collective_id=collective_id,
            has_side_effects=True,
            vmem_limit_bytes=48 * 1024 * 1024,
        ),
    )(q_t, k_tok, v_t, *sends)
    return outs[0], outs[1:]


def project_kernel(mod_ref, w_ref, act_ref, wg_ref, bg_ref, *refs, shards, pair, head_dim):
    got0 = refs[:2]
    q0_ref = refs[2]
    later = refs[3 : 3 * pair]
    gate_ref = refs[3 * pair]
    send0 = (q0_ref,) + tuple(refs[3 * pair + 1 : 3 * pair + 3])
    sems = refs[3 * pair + 3 :]
    modulated = mod_ref[...]

    def fill(h, dests, i):
        out_t = lax.dot_general(
            w_ref[i, h],
            modulated,
            (((1,), (1,)), ((), ())),
            preferred_element_type=jnp.float32,
        )
        for p in range(shards):
            piece = out_t[p * head_dim : (p + 1) * head_dim]
            dests[i][p] = piece.astype(jnp.bfloat16)

    enter(shards)
    copies = []
    fill(0, send0, 0)
    for i in range(1, 3):
        fill(0, send0, i)
        copies += start_array(i - 1, send0[i], got0[i - 1], *sems, shards)
    for h in range(1, pair):
        for i in range(3):
            fill(h, later[3 * (h - 1) : 3 * h], i)
    gate = jnp.dot(act_ref[...], wg_ref[...], preferred_element_type=jnp.float32)
    gate_ref[...] = (gate + bg_ref[...]).astype(gate_ref.dtype)
    for copy in copies:
        copy.wait()


def project_send(modulated, w_t, activated, w_gate, b_gate, shards, pair, head_dim):
    rows, width = modulated.shape
    q_shape = jax.ShapeDtypeStruct((shards, head_dim, rows), jnp.bfloat16)
    shapes = [q_shape, q_shape, q_shape]
    kernel = functools.partial(
        project_kernel, shards=shards, pair=pair, head_dim=head_dim
    )
    any_spec = pl.BlockSpec(memory_space=pl.ANY)
    vmem_spec = pl.BlockSpec(memory_space=pltpu.VMEM)
    outs = pl.pallas_call(
        kernel,
        out_shape=shapes * pair
        + [jax.ShapeDtypeStruct((rows, w_gate.shape[1]), jnp.bfloat16)],
        in_specs=[vmem_spec] * 5,
        out_specs=[any_spec] * 2 + [vmem_spec] * (3 * (pair - 1) + 2),
        scratch_shapes=[pltpu.VMEM(x.shape, x.dtype) for x in shapes[1:]]
        + send_scratch(2, shards),
        compiler_params=pltpu.CompilerParams(
            collective_id=pair + 1,
            has_side_effects=True,
            vmem_limit_bytes=48 * 1024 * 1024,
        ),
    )(modulated, w_t, activated, w_gate, b_gate)
    got = (outs[2], outs[0], outs[1])
    return got, [outs[3 * h : 3 * h + 3] for h in range(1, pair)], outs[3 * pair]


def head_pipeline(modulated, w_t, gate_parts, shards, pair, head_dim, inverse_root):
    got, later, gate = project_send(modulated, w_t, *gate_parts, shards, pair, head_dim)
    backs = []
    for h in range(pair):
        last = h + 1 == pair
        sends = [] if last else list(later[h])
        if h > 0:
            sends = sends + [out_prev]
        out_prev, sent = attend_send(
            *got, sends, shards, inverse_root, 1 + h, stream=last, pull=h == 0
        )
        if not last:
            got = sent[:3]
            sent = sent[3:]
        backs.extend(sent)
    return jnp.stack(backs, axis=1), gate


def request_kernel(req_ref, asked_ref, send_sem, recv_sem, local_sem, *, groups, shards):
    total = groups * shards
    me = lax.axis_index("region") * shards + lax.axis_index("ctx")
    mesh_id = pl.DeviceIdType.MESH
    barrier = pltpu.get_barrier_semaphore()

    def greet(d, carry):
        peer = lax.rem(me + d, total)
        pl.semaphore_signal(
            barrier, 1, device_id=(peer // shards, peer % shards), device_id_type=mesh_id
        )
        return carry

    lax.fori_loop(1, total, greet, 0)
    pl.semaphore_wait(barrier, total - 1)
    local = pltpu.make_async_copy(req_ref.at[me], asked_ref.at[me], local_sem.at[0])
    local.start()

    def remote(d):
        peer = lax.rem(me + d, total)
        return pltpu.make_async_remote_copy(
            src_ref=req_ref.at[peer],
            dst_ref=asked_ref.at[me],
            send_sem=send_sem.at[d - 1],
            recv_sem=recv_sem.at[d - 1],
            device_id=(peer // shards, peer % shards),
            device_id_type=mesh_id,
        )

    def launch(d, carry):
        remote(d).start()
        return carry

    def finish(d, carry):
        remote(d).wait()
        return carry

    lax.fori_loop(1, total, launch, 0)
    local.wait()
    lax.fori_loop(1, total, finish, 0)


def exchange_requests(requests, groups, shards):
    total = groups * shards
    any_spec = pl.BlockSpec(memory_space=pl.ANY)
    return pl.pallas_call(
        functools.partial(request_kernel, groups=groups, shards=shards),
        out_shape=jax.ShapeDtypeStruct(requests.shape, requests.dtype),
        in_specs=[any_spec],
        out_specs=any_spec,
        scratch_shapes=[
            pltpu.SemaphoreType.DMA((total - 1,)),
            pltpu.SemaphoreType.DMA((total - 1,)),
            pltpu.SemaphoreType.DMA((1,)),
        ],
        compiler_params=pltpu.CompilerParams(collective_id=7, has_side_effects=True),
    )(requests)


def per_device(
    tokens, element_ids, element_slot, live_count, cond_table, w_ada, b_ada, w_qkv, w_out
):
    device_tokens = tokens[0]
    tok_rows, width = device_tokens.shape
    owners = lax.axis_size(("region", "ctx"))
    shards = lax.axis_size("ctx")
    elem_rows = cond_table.shape[0]
    capacity = -(-max(2, 3 * tok_rows // (2 * owners)) // 8) * 8
    slots = element_slot[element_ids[0]]
    owner_index = slots // elem_rows
    local_row = slots % elem_rows
    position = jnp.arange(tok_rows, dtype=jnp.int32)
    solid = position < live_count[0, 0]
    earlier = (
        (owner_index[:, None] == owner_index[None, :])
        & (position[None, :] < position[:, None])
        & solid[None, :]
    )
    place_rank = jnp.sum(earlier.astype(jnp.int32), axis=1)
    target = jnp.where(solid, owner_index * capacity + place_rank, owners * capacity)
    requests = jnp.zeros((owners * capacity,), jnp.int32).at[target].set(local_row, mode="drop")
    asked = exchange_requests(
        requests.reshape(owners, capacity), owners // shards, shards
    ).reshape(-1)
    pick_at = jnp.minimum(target, owners * capacity - 1)
    served_hot = (asked[:, None] == jnp.arange(elem_rows, dtype=jnp.int32)[None, :]).astype(
        jnp.bfloat16
    )
    served = (
        jnp.dot(served_hot, cond_table, preferred_element_type=jnp.float32)
        .astype(jnp.bfloat16)
        .reshape(owners, capacity, width)
    )
    replies = lax.all_to_all(served, ("region", "ctx"), split_axis=0, concat_axis=0, tiled=True)
    pick_hot = (
        pick_at[:, None] == jnp.arange(owners * capacity, dtype=jnp.int32)[None, :]
    ).astype(jnp.bfloat16)
    picked = jnp.dot(
        pick_hot, replies.reshape(owners * capacity, width), preferred_element_type=jnp.float32
    )
    activated = jnp.where(solid[:, None], jax.nn.silu(picked.astype(jnp.float32)), 0.0).astype(
        jnp.bfloat16
    )
    mods = (
        jnp.dot(activated, w_ada[:, : 2 * width], preferred_element_type=jnp.float32)
        + b_ada[: 2 * width]
    ).astype(jnp.bfloat16)
    mods = mods.astype(jnp.float32)
    gate_parts = (activated, w_ada[:, 2 * width :], b_ada[None, 2 * width :])
    modulated = layer_modulate(device_tokens, mods, width)

    head_dim = width // HEADS
    pair = HEADS // shards
    inverse_root = 1.0 / math.sqrt(head_dim)
    w_t = (
        w_qkv.reshape(width, 3, shards, pair, head_dim)
        .transpose(1, 3, 2, 4, 0)
        .reshape(3, pair, shards * head_dim, width)
    )
    backs, gate = head_pipeline(
        modulated, w_t, gate_parts, shards, pair, head_dim, inverse_root
    )
    w_out_parts = w_out.reshape(shards, pair, head_dim, width)
    projected = jnp.einsum(
        "phet,pheD->tD",
        backs,
        w_out_parts,
        preferred_element_type=jnp.float32,
    )
    gate = gate.astype(jnp.float32)
    output = (device_tokens.astype(jnp.float32) + gate * projected).astype(jnp.bfloat16)
    return output[None]


def solution(mesh):
    placed = (
        P("region", "ctx", None),
        P("region", "ctx"),
        P(),
        P("region", "ctx"),
        P(("region", "ctx"), None),
        P(),
        P(),
        P(),
        P(),
    )
    return jax.shard_map(
        per_device, mesh=mesh, in_specs=placed, out_specs=P("region", "ctx", None), check_vma=False
    )
```

```python
import functools
import math

import jax
import jax.numpy as jnp
from jax import lax
from jax.experimental import pallas as pl
from jax.experimental.pallas import tpu as pltpu
from jax.sharding import PartitionSpec as P

HEADS = 16


def layer_modulate(device_tokens, mods, width):
    values = device_tokens.astype(jnp.float32)
    center = jnp.mean(values, axis=1, keepdims=True)
    spread = jnp.mean((values - center) ** 2, axis=1, keepdims=True)
    normed = (values - center) * lax.rsqrt(spread + 1e-06)
    shift = mods[:, :width]
    scale = mods[:, width : 2 * width]
    return (normed * (1.0 + scale) + shift).astype(jnp.bfloat16)


def enter(shards):
    me = lax.axis_index("ctx")
    region = lax.axis_index("region")
    barrier = pltpu.get_barrier_semaphore()
    for d in range(1, shards):
        peer = lax.rem(me + d, shards)
        pl.semaphore_signal(
            barrier, 1, device_id=(region, peer), device_id_type=pl.DeviceIdType.MESH
        )
    pl.semaphore_wait(barrier, shards - 1)


def start_array(a, send, got, send_sem, recv_sem, local_sem, shards):
    me = lax.axis_index("ctx")
    region = lax.axis_index("region")
    local = pltpu.make_async_copy(send.at[me], got.at[me], local_sem.at[a])
    local.start()
    copies = [local]
    for d in range(1, shards):
        peer = lax.rem(me + d, shards)
        remote = pltpu.make_async_remote_copy(
            src_ref=send.at[peer],
            dst_ref=got.at[me],
            send_sem=send_sem.at[a, d - 1],
            recv_sem=recv_sem.at[a, d - 1],
            device_id=(region, peer),
            device_id_type=pl.DeviceIdType.MESH,
        )
        remote.start()
        copies.append(remote)
    return copies


def start_sends(sends, gots, send_sem, recv_sem, local_sem, shards):
    enter(shards)
    copies = []
    for a in range(len(sends)):
        copies += start_array(a, sends[a], gots[a], send_sem, recv_sem, local_sem, shards)
    return copies


def exchange_kernel(*refs, count, shards):
    sends = refs[:count]
    gots = refs[count : 2 * count]
    copies = start_sends(sends, gots, *refs[2 * count :], shards)
    for copy in copies:
        copy.wait()


def send_scratch(count, shards):
    return [
        pltpu.SemaphoreType.DMA((count, shards - 1)),
        pltpu.SemaphoreType.DMA((count, shards - 1)),
        pltpu.SemaphoreType.DMA((count,)),
    ]


def exchange(arrays, shards, collective_id):
    count = len(arrays)
    kernel = functools.partial(exchange_kernel, count=count, shards=shards)
    any_spec = pl.BlockSpec(memory_space=pl.ANY)
    return pl.pallas_call(
        kernel,
        out_shape=[jax.ShapeDtypeStruct(x.shape, x.dtype) for x in arrays],
        in_specs=[any_spec] * count,
        out_specs=[any_spec] * count,
        scratch_shapes=send_scratch(count, shards),
        compiler_params=pltpu.CompilerParams(
            collective_id=collective_id, has_side_effects=True
        ),
    )(*arrays)


def attend_body(
    qt_ref, kt_ref, vt_ref, o_ref, s_scr, k_ref, inv_root, after_block=None, before_block=None,
    first=1, span=None, between=None,
):
    blocks, head_dim, q_rows = qt_ref.shape
    for c in range(blocks):
        k_ref[c] = kt_ref[c].astype(jnp.float32).T.astype(k_ref.dtype)

    me = lax.axis_index("ctx")

    def one_block(j, carry):
        if first == 0:
            b = lax.rem(me - j + blocks, blocks)
        else:
            b = lax.rem(j + me + first, blocks)
        if before_block is not None:
            before_block(j, b)
        qt = qt_ref[b]

        def score(c, m):
            s = jnp.dot(k_ref[c], qt, preferred_element_type=jnp.float32) * inv_root
            s_scr[c] = s
            return jnp.maximum(m, jnp.max(s, axis=0, keepdims=True))

        m = lax.fori_loop(
            0, blocks, score, jnp.full((1, q_rows), -jnp.inf, jnp.float32), unroll=2
        )

        def accumulate(c, inner):
            total, acc = inner
            expo = jnp.exp(s_scr[c] - m)
            total = total + jnp.sum(expo, axis=0, keepdims=True)
            acc = acc + jnp.dot(
                vt_ref[c], expo.astype(jnp.bfloat16), preferred_element_type=jnp.float32
            )
            return total, acc

        total, acc = lax.fori_loop(
            0,
            blocks,
            accumulate,
            (
                jnp.zeros((1, q_rows), jnp.float32),
                jnp.zeros((head_dim, q_rows), jnp.float32),
            ),
            unroll=2,
        )
        o_ref[b] = (acc / total).astype(o_ref.dtype)
        if after_block is not None:
            after_block(b)
        return carry

    if between is None:
        lax.fori_loop(0, blocks, one_block, 0, unroll=2)
    else:
        lax.fori_loop(0, span, one_block, 0)
        between()
        lax.fori_loop(span, blocks, one_block, 0, unroll=2)


def attend_send_kernel(*refs, count, shards, inv_root, stream, pull):
    qt_ref, k_ref, vt_ref = refs[:3]
    sends = refs[3 : 3 + count]
    o_ref = refs[3 + count]
    gots = refs[4 + count : 4 + 2 * count]
    rest = refs[4 + 2 * count :]
    if stream:
        back_ref = rest[0]
        rest = rest[1:]
    s_scr, k_scr = rest[0], rest[1]
    rest = rest[1:]
    enter(shards)
    before_block = None
    first = 1
    if pull:
        q_vmem, q_send, q_recv, q_local = rest[7:11] if stream else rest[4:8]
        me_q = lax.axis_index("ctx")
        region_q = lax.axis_index("region")
        q_local_copy = pltpu.make_async_copy(qt_ref.at[me_q], q_vmem.at[me_q], q_local.at[0])
        q_local_copy.start()

        def q_remote(d):
            peer = lax.rem(me_q + d, shards)
            return pltpu.make_async_remote_copy(
                src_ref=qt_ref.at[peer],
                dst_ref=q_vmem.at[me_q],
                send_sem=q_send.at[d - 1],
                recv_sem=q_recv.at[d - 1],
                device_id=(region_q, peer),
                device_id_type=pl.DeviceIdType.MESH,
            )

        for d in range(1, shards):
            q_remote(d).start()

        def before_block(j, b):
            @pl.when(j == 0)
            def _():
                q_local_copy.wait()

            @pl.when(j > 0)
            def _():
                pltpu.make_async_remote_copy(
                    src_ref=qt_ref.at[b],
                    dst_ref=q_vmem.at[b],
                    send_sem=q_send.at[j - 1],
                    recv_sem=q_recv.at[j - 1],
                    device_id=(region_q, b),
                    device_id_type=pl.DeviceIdType.MESH,
                ).wait_recv()

        first = 0
        qt_ref = q_vmem
    copies = []

    def launch():
        for a in range(count):
            copies.extend(start_array(a, sends[a], gots[a], *rest[1:4], shards))

    between = None
    if pull:
        between = launch
    else:
        launch()
    after_block = None
    if stream:
        block_send, block_recv, block_local = rest[4:7]
        me = lax.axis_index("ctx")
        region = lax.axis_index("region")

        def remote_block(b):
            return pltpu.make_async_remote_copy(
                src_ref=o_ref.at[b],
                dst_ref=back_ref.at[me],
                send_sem=block_send.at[b],
                recv_sem=block_recv.at[me],
                device_id=(region, b),
                device_id_type=pl.DeviceIdType.MESH,
            )

        def local_block(b):
            return pltpu.make_async_copy(o_ref.at[b], back_ref.at[b], block_local.at[0])

        def after_block(b):
            @pl.when(b == me)
            def _():
                local_block(b).start()

            @pl.when(b != me)
            def _():
                remote_block(b).start()

    attend_body(
        qt_ref, k_ref, vt_ref, o_ref, s_scr, k_scr, inv_root, after_block, before_block, first,
        span=1, between=between,
    )
    for copy in copies:
        copy.wait()
    if pull:
        for d in range(1, shards):
            q_remote(d).wait_send()
    if stream:
        for b in range(shards):
            @pl.when(b == me)
            def _():
                local_block(b).wait()

            @pl.when(b != me)
            def _():
                remote_block(b).wait_send()
                pltpu.make_async_remote_copy(
                    src_ref=o_ref.at[b],
                    dst_ref=back_ref.at[b],
                    send_sem=block_send.at[b],
                    recv_sem=block_recv.at[b],
                    device_id=(region, b),
                    device_id_type=pl.DeviceIdType.MESH,
                ).wait_recv()


def attend_send(
    q_t, k_tok, v_t, sends, shards, inv_root, collective_id, stream=False, pull=False
):
    blocks, head_dim, rows = q_t.shape
    count = len(sends)
    kernel = functools.partial(
        attend_send_kernel,
        count=count,
        shards=shards,
        inv_root=inv_root,
        stream=stream,
        pull=pull,
    )
    any_spec = pl.BlockSpec(memory_space=pl.ANY)
    vmem_spec = pl.BlockSpec(memory_space=pltpu.VMEM)
    out_shape = [jax.ShapeDtypeStruct(q_t.shape, jnp.bfloat16)]
    out_shape += [jax.ShapeDtypeStruct(x.shape, x.dtype) for x in sends]
    out_specs = [vmem_spec] + [any_spec] * count
    scratch = [
        pltpu.VMEM((blocks, rows, rows), jnp.float32),
        pltpu.VMEM((blocks, rows, head_dim), jnp.bfloat16),
    ] + send_scratch(count, shards)
    if stream:
        out_shape.append(jax.ShapeDtypeStruct(q_t.shape, jnp.bfloat16))
        out_specs.append(any_spec)
        scratch += [
            pltpu.SemaphoreType.DMA((shards,)),
            pltpu.SemaphoreType.DMA((shards,)),
            pltpu.SemaphoreType.DMA((1,)),
        ]
    if pull:
        scratch += [
            pltpu.VMEM(q_t.shape, q_t.dtype),
            pltpu.SemaphoreType.DMA((shards - 1,)),
            pltpu.SemaphoreType.DMA((shards - 1,)),
            pltpu.SemaphoreType.DMA((1,)),
        ]
    outs = pl.pallas_call(
        kernel,
        out_shape=out_shape,
        in_specs=[any_spec if pull else vmem_spec] + [vmem_spec] * 2 + [any_spec] * count,
        out_specs=out_specs,
        scratch_shapes=scratch,
        compiler_params=pltpu.CompilerParams(
            collective_id=collective_id,
            has_side_effects=True,
            vmem_limit_bytes=48 * 1024 * 1024,
        ),
    )(q_t, k_tok, v_t, *sends)
    return outs[0], outs[1:]


def project_kernel(mod_ref, w_ref, act_ref, wg_ref, bg_ref, *refs, shards, pair, head_dim):
    got0 = refs[:2]
    q0_ref = refs[2]
    later = refs[3 : 3 * pair]
    gate_ref = refs[3 * pair]
    send0 = (q0_ref,) + tuple(refs[3 * pair + 1 : 3 * pair + 3])
    sems = refs[3 * pair + 3 :]
    modulated = mod_ref[...]

    def fill(h, dests, i):
        out_t = lax.dot_general(
            w_ref[i, h],
            modulated,
            (((1,), (1,)), ((), ())),
            preferred_element_type=jnp.float32,
        )
        for p in range(shards):
            piece = out_t[p * head_dim : (p + 1) * head_dim]
            dests[i][p] = piece.astype(jnp.bfloat16)

    enter(shards)
    copies = []
    fill(0, send0, 0)
    for i in range(1, 3):
        fill(0, send0, i)
        copies += start_array(i - 1, send0[i], got0[i - 1], *sems, shards)
    for h in range(1, pair):
        for i in range(3):
            fill(h, later[3 * (h - 1) : 3 * h], i)
    gate = jnp.dot(act_ref[...], wg_ref[...], preferred_element_type=jnp.float32)
    gate_ref[...] = (gate + bg_ref[...]).astype(gate_ref.dtype)
    for copy in copies:
        copy.wait()


def project_send(modulated, w_t, activated, w_gate, b_gate, shards, pair, head_dim):
    rows, width = modulated.shape
    q_shape = jax.ShapeDtypeStruct((shards, head_dim, rows), jnp.bfloat16)
    shapes = [q_shape, q_shape, q_shape]
    kernel = functools.partial(
        project_kernel, shards=shards, pair=pair, head_dim=head_dim
    )
    any_spec = pl.BlockSpec(memory_space=pl.ANY)
    vmem_spec = pl.BlockSpec(memory_space=pltpu.VMEM)
    outs = pl.pallas_call(
        kernel,
        out_shape=shapes * pair
        + [jax.ShapeDtypeStruct((rows, w_gate.shape[1]), jnp.bfloat16)],
        in_specs=[vmem_spec] * 5,
        out_specs=[any_spec] * 2 + [vmem_spec] * (3 * (pair - 1) + 2),
        scratch_shapes=[pltpu.VMEM(x.shape, x.dtype) for x in shapes[1:]]
        + send_scratch(2, shards),
        compiler_params=pltpu.CompilerParams(
            collective_id=pair + 1,
            has_side_effects=True,
            vmem_limit_bytes=48 * 1024 * 1024,
        ),
    )(modulated, w_t, activated, w_gate, b_gate)
    got = (outs[2], outs[0], outs[1])
    return got, [outs[3 * h : 3 * h + 3] for h in range(1, pair)], outs[3 * pair]


def head_pipeline(modulated, w_t, gate_parts, shards, pair, head_dim, inverse_root):
    got, later, gate = project_send(modulated, w_t, *gate_parts, shards, pair, head_dim)
    backs = []
    for h in range(pair):
        last = h + 1 == pair
        sends = [] if last else list(later[h])
        if h > 0:
            sends = sends + [out_prev]
        out_prev, sent = attend_send(
            *got, sends, shards, inverse_root, 1 + h, stream=last, pull=h == 0
        )
        if not last:
            got = sent[:3]
            sent = sent[3:]
        backs.extend(sent)
    return jnp.stack(backs, axis=1), gate


def request_kernel(req_ref, asked_ref, send_sem, recv_sem, local_sem, *, groups, shards):
    total = groups * shards
    me = lax.axis_index("region") * shards + lax.axis_index("ctx")
    mesh_id = pl.DeviceIdType.MESH
    barrier = pltpu.get_barrier_semaphore()

    def greet(d, carry):
        peer = lax.rem(me + d, total)
        pl.semaphore_signal(
            barrier, 1, device_id=(peer // shards, peer % shards), device_id_type=mesh_id
        )
        return carry

    lax.fori_loop(1, total, greet, 0)
    pl.semaphore_wait(barrier, total - 1)
    local = pltpu.make_async_copy(req_ref.at[me], asked_ref.at[me], local_sem.at[0])
    local.start()

    def remote(d):
        peer = lax.rem(me + d, total)
        return pltpu.make_async_remote_copy(
            src_ref=req_ref.at[peer],
            dst_ref=asked_ref.at[me],
            send_sem=send_sem.at[d - 1],
            recv_sem=recv_sem.at[d - 1],
            device_id=(peer // shards, peer % shards),
            device_id_type=mesh_id,
        )

    def launch(d, carry):
        remote(d).start()
        return carry

    def finish(d, carry):
        remote(d).wait()
        return carry

    lax.fori_loop(1, total, launch, 0)
    local.wait()
    lax.fori_loop(1, total, finish, 0)


def exchange_requests(requests, groups, shards):
    total = groups * shards
    any_spec = pl.BlockSpec(memory_space=pl.ANY)
    return pl.pallas_call(
        functools.partial(request_kernel, groups=groups, shards=shards),
        out_shape=jax.ShapeDtypeStruct(requests.shape, requests.dtype),
        in_specs=[any_spec],
        out_specs=any_spec,
        scratch_shapes=[
            pltpu.SemaphoreType.DMA((total - 1,)),
            pltpu.SemaphoreType.DMA((total - 1,)),
            pltpu.SemaphoreType.DMA((1,)),
        ],
        compiler_params=pltpu.CompilerParams(collective_id=7, has_side_effects=True),
    )(requests)


def per_device(
    tokens, element_ids, element_slot, live_count, cond_table, w_ada, b_ada, w_qkv, w_out
):
    device_tokens = tokens[0]
    tok_rows, width = device_tokens.shape
    owners = lax.axis_size(("region", "ctx"))
    shards = lax.axis_size("ctx")
    elem_rows = cond_table.shape[0]
    capacity = -(-max(2, 3 * tok_rows // (2 * owners)) // 8) * 8
    slots = element_slot[element_ids[0]]
    owner_index = slots // elem_rows
    local_row = slots % elem_rows
    position = jnp.arange(tok_rows, dtype=jnp.int32)
    solid = position < live_count[0, 0]
    earlier = (
        (owner_index[:, None] == owner_index[None, :])
        & (position[None, :] < position[:, None])
        & solid[None, :]
    )
    place_rank = jnp.sum(earlier.astype(jnp.int32), axis=1)
    target = jnp.where(solid, owner_index * capacity + place_rank, owners * capacity)
    requests = jnp.zeros((owners * capacity,), jnp.int32).at[target].set(local_row, mode="drop")
    asked = exchange_requests(
        requests.reshape(owners, capacity), owners // shards, shards
    ).reshape(-1)
    pick_at = jnp.minimum(target, owners * capacity - 1)
    served_hot = (asked[:, None] == jnp.arange(elem_rows, dtype=jnp.int32)[None, :]).astype(
        jnp.bfloat16
    )
    served = (
        jnp.dot(served_hot, cond_table, preferred_element_type=jnp.float32)
        .astype(jnp.bfloat16)
        .reshape(owners, capacity, width)
    )
    replies = lax.all_to_all(served, ("region", "ctx"), split_axis=0, concat_axis=0, tiled=True)
    pick_hot = (
        pick_at[:, None] == jnp.arange(owners * capacity, dtype=jnp.int32)[None, :]
    ).astype(jnp.bfloat16)
    picked = jnp.dot(
        pick_hot, replies.reshape(owners * capacity, width), preferred_element_type=jnp.float32
    )
    activated = jnp.where(solid[:, None], jax.nn.silu(picked.astype(jnp.float32)), 0.0).astype(
        jnp.bfloat16
    )
    mods = (
        jnp.dot(activated, w_ada[:, : 2 * width], preferred_element_type=jnp.float32)
        + b_ada[: 2 * width]
    ).astype(jnp.bfloat16)
    mods = mods.astype(jnp.float32)
    gate_parts = (activated, w_ada[:, 2 * width :], b_ada[None, 2 * width :])
    modulated = layer_modulate(device_tokens, mods, width)

    head_dim = width // HEADS
    pair = HEADS // shards
    inverse_root = 1.0 / math.sqrt(head_dim)
    w_t = (
        w_qkv.reshape(width, 3, shards, pair, head_dim)
        .transpose(1, 3, 2, 4, 0)
        .reshape(3, pair, shards * head_dim, width)
    )
    backs, gate = head_pipeline(
        modulated, w_t, gate_parts, shards, pair, head_dim, inverse_root
    )
    w_out_parts = w_out.reshape(shards, pair, head_dim, width)
    projected = jnp.einsum(
        "phet,pheD->tD",
        backs,
        w_out_parts,
        preferred_element_type=jnp.float32,
    )
    gate = gate.astype(jnp.float32)
    output = (device_tokens.astype(jnp.float32) + gate * projected).astype(jnp.bfloat16)
    return output[None]


def solution(mesh):
    placed = (
        P("region", "ctx", None),
        P("region", "ctx"),
        P(),
        P("region", "ctx"),
        P(("region", "ctx"), None),
        P(),
        P(),
        P(),
        P(),
    )
    return jax.shard_map(
        per_device, mesh=mesh, in_specs=placed, out_specs=P("region", "ctx", None), check_vma=False
    )
```
